32 devices in a mesh: parts: 2 (over y), walk: 4 (over z), slab: 2 (over x), row: 2 (over core).
Axes of the slice: x: 2, y: 2, z: 4, core: 2. Of those that a mesh axis runs over, the one named last changes fastest.
Arguments:
- walkers: bfloat16 [64, 1024, 256], P(('parts', 'walk'), ('slab', 'row')), parts along dimension 0
- trial_orbitals: bfloat16 [2048, 256], P(('parts', 'slab', 'row')), parts along dimension 0
- cholesky: bfloat16 [16, 256, 1024], P(('parts', 'slab', 'row')), parts along dimension 0, may hold values from -0.359375 to 0.359375
- branches: int32 [64], P('parts'), parts along dimension 0, may hold values from 0 to 31, as said below
- counts: int32 [8], P(('parts', 'walk')), parts along dimension 0, may hold values from 4 to 8, as said below
- field: float32 [64, 1024], P(('parts', 'walk'), ('slab', 'row')), parts along dimension 0, may hold values from 0.7 to 1.3
Outputs:
- force_bias: float32 [64, 8], P(('parts', 'walk'), ('slab', 'row')), parts along dimension 0
- exchange_energy: float32 [64, 8], P(('parts', 'walk'), ('slab', 'row')), parts along dimension 0
The draws below stay inside these ranges and needn't reach their ends.
There are 2 independent parts, one for each index of `parts`. The reference program is written for one: setup_inputs(seed, part) draws one part's arguments, and reference() takes and returns one part's arrays. A program takes and returns all parts, laid end to end along the dimension named above; each array names one. Nothing has to cross between parts.
Inputs may be any that keep to these rules, and one draw needn't show every extreme that they name: `branches`: the new walkers of one walk index copy at most 2 walkers from any one walk index, and some walk index gives exactly 2 to some walk index. `counts`: at least one walk index has all 8 alive; the alive ones are the first of its walkers.
All inputs are finite; a program needn't handle non-finite values. Where the reference program divides by a largest or mean magnitude, that divisor is 1e-20 or more.
Results may differ from the reference program's by a relative error of at most 0.0068.
Values may be sent and summed in bfloat16 or wider, within the bound.
A program may use at most 64 MiB of HBM per device.

```python
import math
import jax
import jax.numpy as jnp
from jax import lax

ORB = 1024
ELEC = 256
WALK_DEV = 8
ITERS = 10
WALKERS = 32
NCHOL = 8
SLOTS = 2


def joint_draw(key):
    folded = jax.random.fold_in(key, 101)
    key_orbitals = jax.random.fold_in(folded, 0)
    key_mixing = jax.random.fold_in(folded, 1)
    key_residue = jax.random.fold_in(folded, 3)
    orbitals = jax.random.normal(key_orbitals, (ORB, ELEC), jnp.float32) / math.sqrt(ORB)
    mixing = jnp.eye(ELEC, dtype=jnp.float32)[None] + 0.3 / math.sqrt(ELEC) * jax.random.normal(key_mixing, (WALKERS, ELEC, ELEC), jnp.float32)
    residue = 0.5 / math.sqrt(ORB) * jax.random.normal(key_residue, (WALKERS, ORB, ELEC), jnp.float32)
    walkers = jnp.einsum('mn,wnk->wmk', orbitals, mixing) + residue
    return (orbitals, walkers)


def draw_walkers(key, part):
    orbitals, walkers = joint_draw(key)
    return walkers.astype(jnp.bfloat16)


def draw_trial_orbitals(key, part):
    orbitals, walkers = joint_draw(key)
    return orbitals.astype(jnp.bfloat16)


def draw_branches(key, part):
    folded = jax.random.fold_in(key, 202)
    key_scores, key_favour, key_local = jax.random.split(folded, 3)
    walk_count = WALKERS // WALK_DEV
    capacity = SLOTS
    candidates = walk_count * capacity
    favour = jax.random.randint(key_favour, (walk_count,), 0, 4) * 1536
    scores = jax.random.randint(key_scores, (walk_count, candidates), 0, 4096) + jnp.repeat(favour, capacity)[None, :]
    scores = scores * candidates + jnp.arange(candidates, dtype=jnp.int32)[None, :]
    top_values, chosen = lax.top_k(scores, WALK_DEV)
    sender = chosen // capacity
    local_index = jax.random.randint(key_local, (walk_count, WALK_DEV), 0, WALK_DEV)
    return (sender * WALK_DEV + local_index).reshape(WALKERS).astype(jnp.int32)


def draw_counts(key, part):
    folded = jax.random.fold_in(key, 303)
    key_counts, key_fullest = jax.random.split(folded)
    walk_count = WALKERS // WALK_DEV
    living = jax.random.randint(key_counts, (walk_count,), WALK_DEV // 2, WALK_DEV + 1)
    fullest = jax.random.randint(key_fullest, (), 0, walk_count)
    return living.at[fullest].set(WALK_DEV).astype(jnp.int32)


def shard_levels(rng, shape, cuts, low, top_value):
    level, own = 1.0, jax.random.fold_in(rng, 6)
    for dim, shards_of in cuts:
        draws = jnp.exp(jax.random.uniform(jax.random.fold_in(own, dim), (shards_of,), jnp.float32, low / len(cuts), top_value / len(cuts)))
        level = level * jnp.repeat(draws, shape[dim] // shards_of).reshape([-1 if axis == dim else 1 for axis in range(len(shape))])
    return level


def noise(own_key, extent, spread, limit, shards=(), kind=jnp.bfloat16):
    level = shard_levels(own_key, extent, shards, -0.22, 0.18) if shards else 1.0
    result = jax.random.normal(own_key, extent, jnp.float32) * spread * level
    return jnp.minimum(jnp.maximum(result, -limit), limit).astype(kind)


def setup_inputs(seed: int = 0, part: int = 0) -> dict:
    splits = jax.random.split(jax.random.key(seed), 7)
    part_splits = jax.random.split(jax.random.fold_in(splits[6], part), 7)
    return {
        "walkers": draw_walkers(jax.random.fold_in(jax.random.fold_in(splits[6], part), 71), part),
        "trial_orbitals": draw_trial_orbitals(jax.random.fold_in(jax.random.fold_in(splits[6], part), 71), part),
        "cholesky": noise(part_splits[2], (NCHOL, ELEC, ORB), 0.06, 0.359375, ((0, 4),)),
        "branches": draw_branches(jax.random.fold_in(jax.random.fold_in(splits[6], part), 71), part),
        "counts": draw_counts(jax.random.fold_in(jax.random.fold_in(splits[6], part), 71), part),
        "field": jnp.clip(0.7 + 0.59999996 * jax.random.uniform(part_splits[5], (WALKERS, ORB), jnp.float32) ** shard_levels(part_splits[5], (WALKERS, ORB), ((0, 4), (1, 4)), -0.2, 0.2), 0.7, 1.3),
    }


HIGHEST = lax.Precision.HIGHEST


def newton_schulz(intersection):
    column_max = jnp.max(jnp.sum(jnp.abs(intersection), axis=0))
    row_max = jnp.max(jnp.sum(jnp.abs(intersection), axis=1))
    inverse = intersection.T / (column_max * row_max)
    twice_identity = 2.0 * jnp.eye(intersection.shape[0], dtype=intersection.dtype)
    for iteration in range(ITERS):
        inverse = jnp.dot(inverse, twice_identity - jnp.dot(intersection, inverse, precision=HIGHEST), precision=HIGHEST)
    return inverse


def reference(walkers, trial_orbitals, cholesky, branches, counts, field):
    vectors = cholesky.astype(jnp.float32)

    def per_walker(walker_index):
        source = walkers[branches[walker_index]]
        walker = (source.astype(jnp.float32) * field[walker_index][:, None]).astype(jnp.bfloat16)
        intersection = jnp.dot(trial_orbitals.T, walker, preferred_element_type=jnp.float32)
        inverse = newton_schulz(intersection).astype(jnp.bfloat16)
        green_half = jnp.dot(walker, inverse, preferred_element_type=jnp.float32).astype(jnp.bfloat16)
        contracted = jnp.einsum('gnm,mk->gnk', vectors, green_half.astype(jnp.float32), precision=HIGHEST)
        living = (walker_index % WALK_DEV < counts[walker_index // WALK_DEV]).astype(jnp.float32)
        force_bias = jnp.trace(contracted, axis1=1, axis2=2) * living
        exchange_energy = -0.5 * jnp.einsum('gnk,gkn->g', contracted, contracted, precision=HIGHEST) * living
        return force_bias, exchange_energy

    force_bias, exchange_energy = lax.map(per_walker, jnp.arange(WALKERS, dtype=jnp.int32))
    return force_bias, exchange_energy
```

```python
import functools

import jax
import jax.numpy as jnp
from jax import lax
from jax.experimental import pallas as pl
from jax.experimental.pallas import tpu as pltpu
from jax.sharding import PartitionSpec as P

ITERS = 10
EARLY = 4
PASSES = 6
PIECES = 4
MESH = pl.DeviceIdType.MESH


def split(x):
    high = x.astype(jnp.bfloat16)
    low = (x - high.astype(jnp.float32)).astype(jnp.bfloat16)
    return high, low


def dot(a, b):
    return jnp.dot(a, b, preferred_element_type=jnp.float32)


def dot3(a, b):
    ah, al = split(a)
    bh, bl = split(b)
    return dot(ah, bh) + (dot(ah, bl) + dot(al, bh))


def partner(position, step, size):
    if size & (size - 1):
        return (position + step) % size
    result, bit = 0, 1
    while bit < size:
        digit = (position // bit) % 2
        result += bit * (1 - digit if step & bit else digit)
        bit *= 2
    return result


def kernel(
    sizes, branch_in, walker_ref, trial_ref, chol_ref, field_ref, bias_ref, exch_ref,
    branch_ref, trial_t, source, outgoing, field_in, field_out, traces, squares, bias_rows, exch_rows, raw, trial, field, chol, prop, half, inter, stack, inverse,
    z_send, z_recv, x_send, x_recv, c_send, c_recv, i_send, i_recv,
    tx_send, tx_recv, tc_send, tc_recv, fx_send, fx_recv, fc_send, fc_recv, own_sem,
):
    walks, slabs, cores, slots, local = sizes
    walk, slab, core = lax.axis_index("walk"), lax.axis_index("slab"), lax.axis_index("row")
    rows, electrons = trial_ref.shape
    vectors = chol_ref.shape[0] // electrons
    mine = slab * cores + core

    def slab_peer(step):
        return lax.rem(slab + step, slabs)

    def core_peer(step):
        return lax.rem(core + step, cores)

    def slab_source(step):
        return lax.rem(slab + slabs - step, slabs)

    def core_source(step):
        return lax.rem(core + cores - step, cores)

    loads = [(branch_in, branch_ref), (walker_ref, source), (field_ref, field_in), (trial_ref, trial.at[mine]), (chol_ref, chol)]
    own = [pltpu.make_async_copy(src, dst, own_sem.at[k]) for k, (src, dst) in enumerate(loads)]
    for copy in own:
        copy.start()
    barrier = pltpu.get_barrier_semaphore()
    greeted = 0
    if local < slots:
        for step in range(1, walks):
            pl.semaphore_signal(barrier, inc=1, device_id={"walk": partner(walk, step, walks)}, device_id_type=MESH)
            greeted += 1
    for step in range(1, slabs):
        pl.semaphore_signal(barrier, inc=1, device_id={"slab": slab_peer(step)}, device_id_type=MESH)
        greeted += 1
    for step in range(1, cores):
        pl.semaphore_signal(barrier, inc=1, device_id={"row": core_peer(step)}, device_id_type=MESH)
        greeted += 1

    def sender(w, k):
        return lax.div(branch_ref[w * slots + k], slots)

    def kth(w, origin, values):
        picks, count = [jnp.int32(0)] * local, jnp.int32(0)
        for k in range(slots):
            hit = sender(w, k) == origin
            picks = [jnp.where(hit & (count == place), values(k), pick) for place, pick in enumerate(picks)]
            count = count + jnp.where(hit, 1, 0)
        return picks

    for copy in own[:3]:
        copy.wait()
    slot_of = list(range(slots))
    if local < slots:
        origins = []
        for step in range(walks):
            target = partner(walk, step, walks)
            picks = kth(target, walk, lambda k: lax.rem(branch_ref[target * slots + k], slots))
            for place, pick in enumerate(picks):
                if step == 0:
                    raw[place, mine] = source[pick]
                else:
                    outgoing[step * local + place] = source[pick]
            origin = target if walks & (walks - 1) == 0 else (walk + walks - step) % walks
            origins.append(origin)
            for place, pick in enumerate(kth(walk, origin, lambda k: k)):
                i = step * local + place
                field_out[i : i + 1, :] = field_in[pl.ds(pick, 1), :]
        for j in range(slots):
            origin, rank, step_of = sender(walk, j), jnp.int32(0), jnp.int32(0)
            for k in range(j):
                rank = rank + jnp.where(sender(walk, k) == origin, 1, 0)
            for step in range(walks):
                step_of = jnp.where(origins[step] == origin, step, step_of)
            slot_of[j] = jnp.minimum(step_of * local + rank, slots - 1)
    else:
        for i in range(slots):
            raw[i, mine] = source[i]
        field_out[...] = field_in[...]
    field[mine] = field_out[...]
    for copy in own[3:]:
        copy.wait()
    pl.semaphore_wait(barrier, greeted)

    def remote(src, dst, send, recv, target):
        return pltpu.make_async_remote_copy(
            src_ref=src, dst_ref=dst, send_sem=send, recv_sem=recv, device_id=target, device_id_type=MESH
        )

    def z_copy(i, step):
        return remote(outgoing.at[i], raw.at[i, mine], z_send.at[i], z_recv.at[i], {"walk": partner(walk, step, walks)})

    def x_copy(i, step):
        return remote(raw.at[i, mine], raw.at[i, mine], x_send.at[step, i], x_recv.at[step, i], {"slab": slab_peer(step)})

    def c_copy(i, hop, step):
        q = slab_source(hop) * cores + core
        return remote(raw.at[i, q], raw.at[i, q], c_send.at[hop, step, i], c_recv.at[hop, step, i], {"row": core_peer(step)})

    def small(src, buf, xs, xr, cs, cr):
        def x(step):
            return remote(src, buf.at[mine], xs.at[step], xr.at[step], {"slab": slab_peer(step)})

        def c(hop, step):
            q = slab_source(hop) * cores + core
            block = src if hop == 0 else buf.at[q]
            return remote(block, buf.at[q], cs.at[hop, step], cr.at[hop, step], {"row": core_peer(step)})

        return x, c

    for i in range(local, slots):
        z_copy(i, i // local).start()
    pairs = [
        small(trial_ref, trial, tx_send, tx_recv, tc_send, tc_recv),
        small(field_out, field, fx_send, fx_recv, fc_send, fc_recv),
    ]
    for x, c in pairs:
        for step in range(1, slabs):
            x(step).start()
        for step in range(1, cores):
            c(0, step).start()
    def spread(i):
        for step in range(1, slabs):
            x_copy(i, step).start()
        for step in range(1, cores):
            c_copy(i, 0, step).start()

    def relay(i):
        for hop in range(1, slabs):
            x_copy(i, hop).wait_recv()
            for step in range(1, cores):
                c_copy(i, hop, step).start()

    def compute(i):
        for hop in range(slabs):
            for step in range(1, cores):
                c_copy(i, hop, step).wait_recv()
        for q in range(slabs * cores):
            column = jnp.transpose(field[q])
            lane = lax.broadcasted_iota(jnp.int32, column.shape, 1)
            scale = jnp.sum(jnp.where(lane == i, column, 0.0), axis=1, keepdims=True)
            prop[q * rows : (q + 1) * rows, :] = (raw[i, q].astype(jnp.float32) * scale).astype(jnp.bfloat16)
        @pl.when(lax.rem(i, cores) == core)
        def _():
            total = dot(trial_t[0], prop[0:rows, :])
            for q in range(1, slabs * cores):
                total += dot(trial_t[q], prop[q * rows : (q + 1) * rows, :])
            inter[i // cores] = total

        half[i] = dot(chol[...], prop[...]).astype(jnp.bfloat16)

    for i in range(local):
        spread(i)
    for x, c in pairs:
        for hop in range(1, slabs):
            x(hop).wait_recv()
            for step in range(1, cores):
                c(hop, step).start()
    for x, c in pairs:
        for hop in range(slabs):
            for step in range(1, cores):
                c(hop, step).wait_recv()

    for q in range(slabs * cores):
        trial_t[q] = jnp.transpose(trial[q].astype(jnp.float32)).astype(jnp.bfloat16)
    share = slots // cores
    line = lax.broadcasted_iota(jnp.int32, (electrons, electrons), 0)
    diagonal = line == lax.broadcasted_iota(jnp.int32, (electrons, electrons), 1)

    def i_copy(i, step):
        place = inverse.at[i]
        return remote(place, place, i_send.at[i // cores, step], i_recv.at[i // cores, step], {"row": core_peer(step)})

    def first_guess(n):
        matrix = inter[n]
        sizes_of = jnp.abs(matrix)
        column_max = jnp.max(jnp.sum(sizes_of, axis=0, keepdims=True), axis=1, keepdims=True)
        row_max = jnp.max(jnp.sum(sizes_of, axis=1, keepdims=True), axis=0, keepdims=True)
        start = jnp.transpose(matrix) / (column_max * row_max)
        stack[0:electrons, :] = start
        stack[electrons:, :] = dot3(matrix, start)

    def finish(i):
        @pl.when(lax.rem(i, cores) != core)
        def _():
            i_copy(i, lax.rem(core + cores - lax.rem(i, cores), cores)).wait_recv()

        contracted = dot(half[i], inverse[i])
        for g in range(vectors):
            block = contracted[g * electrons : (g + 1) * electrons, :]
            traces[i, g : g + 1, :] = jnp.sum(jnp.where(diagonal, block, 0.0), axis=0, keepdims=True)
            squares[i, g : g + 1, :] = jnp.sum(block * jnp.transpose(block), axis=0, keepdims=True)

    ready = cores + 1

    @pl.loop(0, slots + ready + cores + 1)
    def _(i):
        @pl.when((i >= local) & (i < slots))
        def _():
            z_copy(i, 0).wait_recv()
            spread(i)

        @pl.when((i > 1) & (i < slots + 2))
        def _():
            compute(i - 2)

        @pl.when((i > 0) & (i <= slots))
        def _():
            relay(i - 1)

        for part in range(cores):

            @pl.when((i >= ready) & (i < slots + ready) & (lax.rem(i + cores - 1, cores) == part))
            def _():
                n = (i - ready) // cores
                if part == 0:
                    first_guess(n)

                first, middle, last = ITERS * part // cores, EARLY, ITERS * (part + 1) // cores

                @pl.loop(first, max(first, min(middle, last)))
                def _(iteration):
                    both = stack[...]
                    low = both.astype(jnp.bfloat16)
                    stack[...] = 2.0 * both - dot(low, low[electrons:, :])

                @pl.loop(min(last, max(middle, first)), last)
                def _(iteration):
                    both = stack[...]
                    stack[...] = 2.0 * both - dot3(both, both[electrons:, :])

                if part == cores - 1:
                    inverse[n * cores + core] = stack[0:electrons, :].astype(jnp.bfloat16)
                    for step in range(1, cores):
                        i_copy(n * cores + core, step).start()

        @pl.when(i > ready + cores)
        def _():
            finish(i - ready - cores - 1)


    column = lax.broadcasted_iota(jnp.int32, bias_ref.shape, 1)
    for terms, rows_of, result in ((traces, bias_rows, bias_ref), (squares, exch_rows, exch_ref)):
        for j in range(slots):
            block = terms[slot_of[j]]
            for g in range(vectors):
                rows_of[g, j : j + 1, :] = block[g : g + 1, :]
        total = jnp.zeros(result.shape, jnp.float32)
        for g in range(vectors):
            total = jnp.where(column == g, jnp.sum(rows_of[g], axis=1, keepdims=True), total)
        result[...] = total

    for i in range(local, slots):
        z_copy(i, i // local).wait_send()

    @pl.loop(0, slots)
    def _(i):
        for step in range(1, slabs):
            x_copy(i, step).wait_send()
        for hop in range(slabs):
            for step in range(1, cores):
                c_copy(i, hop, step).wait_send()

    for x, c in pairs:
        for step in range(1, slabs):
            x(step).wait_send()
        for hop in range(slabs):
            for step in range(1, cores):
                c(hop, step).wait_send()
    for n in range(share):
        for step in range(1, cores):
            i_copy(n * cores + core, step).wait_send()


def xor(a, b, size):
    result, bit = 0, 1
    while bit < size:
        left, right = lax.rem(lax.div(a, bit), 2), lax.rem(lax.div(b, bit), 2)
        result += bit * lax.rem(left + right, 2)
        bit *= 2
    return result


def origin_kernel(
    sizes, branch_in, walker_ref, trial_ref, chol_ref, field_ref, bias_ref, exch_ref,
    branch_ref, source, fields, chosen, outgoing, prop, trial, trial_t, chol, stack, green, lanes, sums, arrived,
    own_sem, f_send, f_recv, t_send, t_recv, tx_send, tp_sem, cx_send, c_send, c_recv, cp_sem, w_send, w_recv, o_send, o_recv,
):
    walks, slabs, cores, slots, local, items = sizes
    walk, slab, core = lax.axis_index("walk"), lax.axis_index("slab"), lax.axis_index("row")
    rows, electrons = trial_ref.shape
    shards = slabs * cores
    vectors = chol_ref.shape[0] // electrons
    mine = slab * cores + core
    other_slab, other_core = 1 - slab, 1 - core
    across, beside, diagonal_q = other_slab * cores + core, slab * cores + other_core, other_slab * cores + other_core
    below, above = walk > 0, walk < walks - 1
    steps = ((1, 1), (1, 0), (0, 1))

    loads = [(branch_in, branch_ref), (walker_ref, source), (field_ref, fields.at[walk]), (trial_ref, trial.at[mine]), (chol_ref, chol.at[mine])]
    own = [pltpu.make_async_copy(src, dst, own_sem.at[k]) for k, (src, dst) in enumerate(loads)]
    for copy in own:
        copy.start()
    barrier = pltpu.get_barrier_semaphore()

    def greet(target):
        pl.semaphore_signal(barrier, inc=1, device_id=target, device_id_type=MESH)

    def place_of(dx, dc):
        return {"slab": lax.rem(slab + dx, slabs), "row": lax.rem(core + dc, cores)}

    for dx, dc in steps:
        greet(place_of(dx, dc))

    @pl.when(below)
    def _():
        greet({"walk": walk - 1})

    @pl.when(above)
    def _():
        greet({"walk": walk + 1})

    pl.semaphore_wait(barrier, len(steps) + jnp.where(below, 1, 0) + jnp.where(above, 1, 0))

    def remote(src, dst, send, recv, target):
        return pltpu.make_async_remote_copy(
            src_ref=src, dst_ref=dst, send_sem=send, recv_sem=recv, device_id=target, device_id_type=MESH
        )

    def field_copy(o, way):
        block = fields.at[o]
        src = field_ref if way[1] else block
        return remote(src, block, f_send.at[way[0], o], f_recv.at[o], {"walk": walk + 1 - 2 * way[0]})

    def trial_view(q, o):
        size = rows // walks
        return trial.at[q, pl.ds(pl.multiple_of(o * size, size), size)]

    def chol_rows(o, p):
        size = chol_ref.shape[0] // (walks * PIECES)
        return pl.ds(pl.multiple_of((o * PIECES + p) * size, size), size)

    def trial_copy(o, way):
        view = trial_view(across, o)
        if way == 2:
            return remote(view, view, t_send.at[2, o], t_recv.at[1, o], {"row": other_core})
        return remote(view, view, t_send.at[way, o], t_recv.at[0, o], {"walk": walk + 1 - 2 * way})

    def trial_beside(o):
        view = trial_view(diagonal_q, o)
        return remote(view, view, t_send.at[2, o], t_recv.at[1, o], {"row": other_core})

    def chol_copy(o, p, way):
        view = chol.at[across, chol_rows(o, p)]
        if way == 2:
            return remote(view, view, c_send.at[2, o, p], c_recv.at[1, o, p], {"row": other_core})
        return remote(view, view, c_send.at[way, o, p], c_recv.at[0, o, p], {"walk": walk + 1 - 2 * way})

    def chol_beside(o, p):
        view = chol.at[diagonal_q, chol_rows(o, p)]
        return remote(view, view, c_send.at[2, o, p], c_recv.at[1, o, p], {"row": other_core})

    def trial_across():
        size = rows // walks
        src = trial_ref.at[pl.ds(pl.multiple_of(walk * size, size), size)]
        return remote(src, trial_view(mine, walk), tx_send.at[0], t_recv.at[0, walk], {"slab": other_slab})

    def chol_across(p):
        return remote(chol_ref.at[chol_rows(walk, p)], chol.at[mine, chol_rows(walk, p)], cx_send.at[p], c_recv.at[0, walk, p], {"slab": other_slab})

    trial_whole = remote(trial_ref, trial.at[mine], tp_sem.at[0], tp_sem.at[1], {"row": other_core})
    chol_whole = remote(chol_ref, chol.at[mine], cp_sem.at[0], cp_sem.at[1], {"row": other_core})

    def both_ways(action):
        @pl.when(above)
        def _():
            action(0)

        @pl.when(below)
        def _():
            action(1)

    def hop(k, arrive, forward):
        @pl.when(walk >= k)
        def _():
            arrive(walk - k)
            if k < walks - 1:
                pl.when(above)(lambda: forward(walk - k, 0))

        @pl.when(walk + k < walks)
        def _():
            arrive(walk + k)
            if k < walks - 1:
                pl.when(below)(lambda: forward(walk + k, 1))

    def field_hop(k):
        hop(k, lambda o: field_copy(o, (0, False)).wait_recv(), lambda o, way: field_copy(o, (way, False)).start())

    def trial_arrive(o):
        trial_copy(o, 0).wait_recv()
        trial_copy(o, 2).start()

    def trial_hop(k):
        hop(k, trial_arrive, lambda o, way: trial_copy(o, way).start())

    def chol_hop(k):
        @pl.loop(0, PIECES)
        def _(p):
            def arrive(o):
                chol_copy(o, p, 0).wait_recv()
                chol_copy(o, p, 2).start()

            hop(k, arrive, lambda o, way: chol_copy(o, p, way).start())

    def chol_start(p):
        chol_copy(walk, p, 0).wait_recv()
        both_ways(lambda way: chol_copy(walk, p, way).start())
        chol_copy(walk, p, 2).start()

    both_ways(lambda way: field_copy(walk, (way, True)).start())
    trial_across().start()
    for p in range(PIECES):
        chol_across(p).start()
    trial_whole.start()
    chol_whole.start()

    field_hop(1)
    trial_arrive(walk)
    both_ways(lambda way: trial_copy(walk, way).start())
    if walks > 2:
        field_hop(2)
    chol_start(0)
    for k in range(3, walks):
        field_hop(k)

    def sender(w, k):
        return lax.div(branch_ref[w * slots + k], slots)

    def item_target(number):
        step = walks - 1 - lax.div(number, local)
        return xor(walk, step, walks), lax.rem(number, local)

    def locate(number):
        target, place = item_target(number)
        pick, spot, count = jnp.int32(0), jnp.int32(0), jnp.int32(0)
        for k in range(slots):
            hit = sender(target, k) == walk
            here = hit & (count == place)
            pick = jnp.where(here, lax.rem(branch_ref[target * slots + k], slots), pick)
            spot = jnp.where(here, k, spot)
            count = count + jnp.where(hit, 1, 0)
        return target, pick, spot

    def w_copy(r, dx, dc):
        d = dx * cores + dc
        part = pl.ds(pl.multiple_of(mine * rows, rows), rows)
        return remote(outgoing.at[r, d], prop.at[r, part], w_send.at[r, d], w_recv.at[r, d], place_of(dx, dc))

    for copy in own[:3]:
        copy.wait()
    offsets = steps + ((0, 0),)
    picks = []
    for r in range(items):
        for dx, dc in offsets:
            q = lax.rem(slab + dx, slabs) * cores + lax.rem(core + dc, cores)
            target, pick, spot = locate(r * shards + q)
            i = len(picks)
            picks.append(pick)
            chosen[i : i + 1, :] = fields[target, pl.ds(spot, 1), :]
    scales = jnp.transpose(chosen[...])
    for r in range(items):
        for n, (dx, dc) in enumerate(offsets):
            i = r * shards + n
            block = (source[picks[i]].astype(jnp.float32) * scales[:, i : i + 1]).astype(jnp.bfloat16)
            if dx or dc:
                outgoing[r, dx * cores + dc] = block
                w_copy(r, dx, dc).start()
            else:
                prop[r, pl.ds(pl.multiple_of(mine * rows, rows), rows)] = block
        if r + 1 < PIECES:
            chol_start(r + 1)
    for p in range(items + 1, PIECES):
        chol_start(p)
    for k in range(1, walks):
        trial_hop(k)
    chol_hop(1)

    @pl.loop(0, walks)
    def _(o):
        trial_beside(o).wait_recv()

    own[3].wait()
    trial_whole.wait_recv()
    for q in range(shards):
        trial_t[:, q * rows : (q + 1) * rows] = jnp.transpose(trial[q].astype(jnp.float32)).astype(jnp.bfloat16)
    for k in range(2, walks - 1):
        chol_hop(k)

    line = lax.broadcasted_iota(jnp.int32, (electrons, electrons), 0)
    on_diagonal = line == lax.broadcasted_iota(jnp.int32, (electrons, electrons), 1)

    def invert(r):
        for dx, dc in steps:
            w_copy(r, dx, dc).wait_recv()
        matrix = dot(trial_t[...], prop[r])
        sizes_of = jnp.abs(matrix)
        column_max = jnp.max(jnp.sum(sizes_of, axis=0, keepdims=True), axis=1, keepdims=True)
        row_max = jnp.max(jnp.sum(sizes_of, axis=1, keepdims=True), axis=0, keepdims=True)
        start = jnp.transpose(matrix) / (column_max * row_max)
        stack[0:electrons, :] = start
        stack[electrons:, :] = dot3(matrix, start)

        @pl.loop(0, PASSES)
        def _(iteration):
            both = stack[...]
            low = both.astype(jnp.bfloat16)
            stack[...] = 2.0 * both - dot(low, low[electrons:, :])

        @pl.loop(PASSES, ITERS)
        def _(iteration):
            both = stack[...]
            stack[...] = 2.0 * both - dot3(both, both[electrons:, :])

        green[r] = dot(prop[r], stack[0:electrons, :].astype(jnp.bfloat16)).astype(jnp.bfloat16)

    def contract(r, q):
        for g in range(vectors):
            block = dot(chol[q, g * electrons : (g + 1) * electrons, :], green[r])
            number = q * vectors + g
            lanes[r, 0, pl.ds(number, 1), :] = jnp.sum(jnp.where(on_diagonal, block, 0.0), axis=0, keepdims=True)
            lanes[r, 1, pl.ds(number, 1), :] = jnp.sum(block * jnp.transpose(block), axis=0, keepdims=True)

    def o_copy(r, dx, dc):
        number = r * shards + mine
        target, _ = item_target(number)
        device = {"walk": target, **place_of(dx, dc)}
        return target, remote(sums.at[r], arrived.at[number], o_send.at[r, dx * cores + dc], o_recv.at[number], device)

    def publish(r):
        for kind in range(2):
            total = jnp.sum(lanes[r, kind], axis=1, keepdims=True)
            sums[r, kind] = jnp.broadcast_to(total, sums.shape[2:])
        for dx, dc in steps:
            o_copy(r, dx, dc)[1].start()
        target, copy = o_copy(r, 0, 0)
        pl.when(target != walk)(copy.start)

        @pl.when(target == walk)
        def _():
            arrived[r * shards + mine] = sums[r]

    invert(0)
    own[4].wait()
    contract(0, mine)
    chol_whole.wait_recv()
    contract(0, beside)
    if walks > 1:
        chol_hop(walks - 1)
    for r in range(1, items):
        invert(r)

    @pl.loop(0, walks)
    def _(o):
        @pl.loop(0, PIECES)
        def _(p):
            chol_beside(o, p).wait_recv()

    contract(0, across)
    contract(0, diagonal_q)
    publish(0)
    for r in range(1, items):
        for q in (mine, beside, across, diagonal_q):
            contract(r, q)
        publish(r)

    def number_of(j):
        origin, rank = sender(walk, j), jnp.int32(0)
        for k in range(j):
            rank = rank + jnp.where(sender(walk, k) == origin, 1, 0)
        step = jnp.int32(0)
        for s in range(walks):
            step = jnp.where(xor(walk, s, walks) == origin, s, step)
        return jnp.clip((walks - 1 - step) * local + rank, 0, slots - 1)

    numbers = [number_of(j) for j in range(slots)]

    for number in range(slots):
        target, _ = item_target(number)
        from_me = (target == walk) & (mine == number % shards)

        @pl.when(jnp.logical_not(from_me))
        def _():
            remote(sums.at[0], arrived.at[number], o_send.at[0, 0], o_recv.at[number], {"row": other_core}).wait_recv()

    column = lax.broadcasted_iota(jnp.int32, (1, vectors), 1)
    for j in range(slots):
        for kind, result in enumerate((bias_ref, exch_ref)):
            total = jnp.zeros((1, vectors), jnp.float32)
            for g in range(vectors):
                value = arrived[numbers[j], kind, pl.ds(mine * vectors + g, 1), 0:vectors]
                total = jnp.where(column == g, value, total)
            result[j : j + 1, :] = total

    trial_across().wait_send()
    trial_whole.wait_send()
    chol_whole.wait_send()
    for p in range(PIECES):
        chol_across(p).wait_send()

    @pl.loop(0, walks)
    def _(o):
        trial_copy(o, 2).wait_send()

        def sent(way):
            field_copy(o, (way, False)).wait_send()
            trial_copy(o, way).wait_send()

        pl.when(above & (o <= walk))(lambda: sent(0))
        pl.when(below & (o >= walk))(lambda: sent(1))

        @pl.loop(0, PIECES)
        def _(p):
            chol_copy(o, p, 2).wait_send()
            pl.when(above & (o <= walk))(lambda: chol_copy(o, p, 0).wait_send())
            pl.when(below & (o >= walk))(lambda: chol_copy(o, p, 1).wait_send())

    for r in range(items):
        for dx, dc in steps:
            w_copy(r, dx, dc).wait_send()
            o_copy(r, dx, dc)[1].wait_send()
        target, copy = o_copy(r, 0, 0)
        pl.when(target != walk)(copy.wait_send)


def gathered(walkers, trial_orbitals, cholesky, branches, field):
    walks, slabs, cores = lax.axis_size("walk"), lax.axis_size("slab"), lax.axis_size("row")
    walk = lax.axis_index("walk")
    per_device, rows, electrons = walkers.shape
    vectors = cholesky.shape[0]
    capacity = (per_device + walks - 1) // walks
    local = capacity if walks * capacity == per_device else per_device
    if local == per_device:
        sender = branches.reshape(walks, per_device) // per_device
        local_index = branches.reshape(walks, per_device) % per_device
        places = jnp.arange(per_device, dtype=jnp.int32)
        same_sender = sender[:, :, None] == sender[:, None, :]
        rank = jnp.sum(same_sender & (places[None, :] < places[:, None])[None], axis=2)
        ranks = jnp.arange(capacity, dtype=jnp.int32)[None, :, None]
        wanted = (sender[:, None, :] == walk) & (rank[:, None, :] == ranks)
        chosen = jnp.sum(jnp.where(wanted, local_index[:, None, :], 0), axis=2)
        outgoing = jnp.take(walkers, chosen.reshape(-1), axis=0, mode="clip")
        outgoing = outgoing.reshape(walks, capacity, rows, electrons)
        arrived = lax.all_to_all(outgoing, "walk", split_axis=0, concat_axis=0, tiled=True)
        arrived = arrived.reshape(walks * capacity, rows, electrons)
        my_sender = lax.dynamic_index_in_dim(sender, walk, 0, keepdims=False)
        my_rank = lax.dynamic_index_in_dim(rank, walk, 0, keepdims=False)
        walkers = jnp.take(arrived, my_sender * capacity + my_rank, axis=0, mode="clip")
    shards = slabs * cores
    share = per_device // cores
    dma = pltpu.SemaphoreType.DMA
    vmem = pl.BlockSpec(memory_space=pltpu.VMEM)
    bias, exchange = pl.pallas_call(
        functools.partial(kernel, (walks, slabs, cores, per_device, local)),
        out_shape=[jax.ShapeDtypeStruct((per_device, vectors), jnp.float32)] * 2,
        in_specs=[pl.BlockSpec(memory_space=pl.ANY)] * 5,
        out_specs=[vmem] * 2,
        scratch_shapes=[
            pltpu.SMEM(branches.shape, jnp.int32),
            pltpu.VMEM((shards, electrons, rows), jnp.bfloat16),
            pltpu.VMEM((per_device, rows, electrons), jnp.bfloat16),
            pltpu.VMEM((per_device, rows, electrons), jnp.bfloat16),
            pltpu.VMEM((per_device, rows), jnp.float32),
            pltpu.VMEM((per_device, rows), jnp.float32),
            pltpu.VMEM((per_device, vectors, electrons), jnp.float32),
            pltpu.VMEM((per_device, vectors, electrons), jnp.float32),
            pltpu.VMEM((vectors, per_device, electrons), jnp.float32),
            pltpu.VMEM((vectors, per_device, electrons), jnp.float32),
            pltpu.VMEM((per_device, shards, rows, electrons), jnp.bfloat16),
            pltpu.VMEM((shards, rows, electrons), jnp.bfloat16),
            pltpu.VMEM((shards, per_device, rows), jnp.float32),
            pltpu.VMEM((vectors * electrons, shards * rows), jnp.bfloat16),
            pltpu.VMEM((shards * rows, electrons), jnp.bfloat16),
            pltpu.VMEM((per_device, vectors * electrons, electrons), jnp.bfloat16),
            pltpu.VMEM((share, electrons, electrons), jnp.float32),
            pltpu.VMEM((2 * electrons, electrons), jnp.float32),
            pltpu.VMEM((per_device, electrons, electrons), jnp.bfloat16),
            dma((per_device,)), dma((per_device,)),
            dma((slabs, per_device)), dma((slabs, per_device)),
            dma((slabs, cores, per_device)), dma((slabs, cores, per_device)),
            dma((share, cores)), dma((share, cores)),
            dma((slabs,)), dma((slabs,)), dma((slabs, cores)), dma((slabs, cores)),
            dma((slabs,)), dma((slabs,)), dma((slabs, cores)), dma((slabs, cores)),
            dma((5,)),
        ],
        compiler_params=pltpu.CompilerParams(
            collective_id=0, has_side_effects=True, vmem_limit_bytes=63 * 1024 * 1024
        ),
    )(branches, walkers, trial_orbitals, cholesky.reshape(vectors * electrons, shards * rows), field)
    return bias, exchange


def at_origin(walkers, trial_orbitals, cholesky, branches, field):
    walks, slabs, cores = lax.axis_size("walk"), lax.axis_size("slab"), lax.axis_size("row")
    slots, rows, electrons = walkers.shape
    vectors = cholesky.shape[0]
    shards, local = slabs * cores, slots // walks
    items, lines, columns = slots // shards, vectors * electrons, shards * rows
    dma = pltpu.SemaphoreType.DMA
    vmem = pl.BlockSpec(memory_space=pltpu.VMEM)
    return pl.pallas_call(
        functools.partial(origin_kernel, (walks, slabs, cores, slots, local, items)),
        out_shape=[jax.ShapeDtypeStruct((slots, vectors), jnp.float32)] * 2,
        in_specs=[pl.BlockSpec(memory_space=pl.ANY)] * 5,
        out_specs=[vmem] * 2,
        scratch_shapes=[
            pltpu.SMEM(branches.shape, jnp.int32),
            pltpu.VMEM((slots, rows, electrons), jnp.bfloat16),
            pltpu.VMEM((walks, slots, rows), jnp.float32),
            pltpu.VMEM((slots, rows), jnp.float32),
            pltpu.VMEM((items, shards, rows, electrons), jnp.bfloat16),
            pltpu.VMEM((items, columns, electrons), jnp.bfloat16),
            pltpu.VMEM((shards, rows, electrons), jnp.bfloat16),
            pltpu.VMEM((electrons, columns), jnp.bfloat16),
            pltpu.VMEM((shards, lines, columns), jnp.bfloat16),
            pltpu.VMEM((2 * electrons, electrons), jnp.float32),
            pltpu.VMEM((items, columns, electrons), jnp.bfloat16),
            pltpu.VMEM((items, 2, shards * vectors, electrons), jnp.float32),
            pltpu.VMEM((items, 2, shards * vectors, 128), jnp.float32),
            pltpu.VMEM((slots, 2, shards * vectors, 128), jnp.float32),
            dma((5,)),
            dma((2, walks)), dma((walks,)),
            dma((3, walks)), dma((2, walks)), dma((2,)), dma((2,)),
            dma((PIECES,)), dma((3, walks, PIECES)), dma((2, walks, PIECES)), dma((2,)),
            dma((items, shards)), dma((items, shards)),
            dma((items, shards)), dma((slots,)),
        ],
        compiler_params=pltpu.CompilerParams(
            collective_id=0, has_side_effects=True, vmem_limit_bytes=60 * 1024 * 1024
        ),
    )(branches, walkers, trial_orbitals, cholesky.reshape(lines, columns), field)


def on_device(walkers, trial_orbitals, cholesky, branches, counts, field):
    walks, slabs, cores = lax.axis_size("walk"), lax.axis_size("slab"), lax.axis_size("row")
    slots, rows, electrons = walkers.shape
    lines = cholesky.shape[0] * electrons
    even = walks & (walks - 1) == 0 and slots % walks == 0 and slots % (slabs * cores) == 0
    whole = lines % (walks * PIECES * 16) == 0 and rows % (walks * 16) == 0
    if slabs == cores == 2 and even and whole:
        bias, exchange = at_origin(walkers, trial_orbitals, cholesky, branches, field)
    else:
        bias, exchange = gathered(walkers, trial_orbitals, cholesky, branches, field)
    living = (jnp.arange(slots, dtype=jnp.int32) < counts[0]).astype(jnp.float32)[:, None]
    return bias * living, -0.5 * exchange * living


def solution(mesh):
    return jax.shard_map(
        on_device,
        mesh=mesh,
        in_specs=(
            P(("parts", "walk"), ("slab", "row"), None),
            P(("parts", "slab", "row"), None),
            P(("parts", "slab", "row"), None, None),
            P("parts"),
            P(("parts", "walk")),
            P(("parts", "walk"), ("slab", "row")),
        ),
        out_specs=(P(("parts", "walk"), ("slab", "row")), P(("parts", "walk"), ("slab", "row"))),
        check_vma=False,
    )
```

```python
import functools

import jax
import jax.numpy as jnp
from jax import lax
from jax.experimental import pallas as pl
from jax.experimental.pallas import tpu as pltpu
from jax.sharding import PartitionSpec as P

ITERS = 10
EARLY = 4
PASSES = 6
PIECES = 4
MESH = pl.DeviceIdType.MESH


def split(x):
    high = x.astype(jnp.bfloat16)
    low = (x - high.astype(jnp.float32)).astype(jnp.bfloat16)
    return high, low


def dot(a, b):
    return jnp.dot(a, b, preferred_element_type=jnp.float32)


def dot3(a, b):
    ah, al = split(a)
    bh, bl = split(b)
    return dot(ah, bh) + (dot(ah, bl) + dot(al, bh))


def partner(position, step, size):
    if size & (size - 1):
        return (position + step) % size
    result, bit = 0, 1
    while bit < size:
        digit = (position // bit) % 2
        result += bit * (1 - digit if step & bit else digit)
        bit *= 2
    return result


def kernel(
    sizes, branch_in, walker_ref, trial_ref, chol_ref, field_ref, bias_ref, exch_ref,
    branch_ref, trial_t, source, outgoing, field_in, field_out, traces, squares, bias_rows, exch_rows, raw, trial, field, chol, prop, half, inter, stack, inverse,
    z_send, z_recv, x_send, x_recv, c_send, c_recv, i_send, i_recv,
    tx_send, tx_recv, tc_send, tc_recv, fx_send, fx_recv, fc_send, fc_recv, own_sem,
):
    walks, slabs, cores, slots, local = sizes
    walk, slab, core = lax.axis_index("walk"), lax.axis_index("slab"), lax.axis_index("row")
    rows, electrons = trial_ref.shape
    vectors = chol_ref.shape[0] // electrons
    mine = slab * cores + core

    def slab_peer(step):
        return lax.rem(slab + step, slabs)

    def core_peer(step):
        return lax.rem(core + step, cores)

    def slab_source(step):
        return lax.rem(slab + slabs - step, slabs)

    def core_source(step):
        return lax.rem(core + cores - step, cores)

    loads = [(branch_in, branch_ref), (walker_ref, source), (field_ref, field_in), (trial_ref, trial.at[mine]), (chol_ref, chol)]
    own = [pltpu.make_async_copy(src, dst, own_sem.at[k]) for k, (src, dst) in enumerate(loads)]
    for copy in own:
        copy.start()
    barrier = pltpu.get_barrier_semaphore()
    greeted = 0
    if local < slots:
        for step in range(1, walks):
            pl.semaphore_signal(barrier, inc=1, device_id={"walk": partner(walk, step, walks)}, device_id_type=MESH)
            greeted += 1
    for step in range(1, slabs):
        pl.semaphore_signal(barrier, inc=1, device_id={"slab": slab_peer(step)}, device_id_type=MESH)
        greeted += 1
    for step in range(1, cores):
        pl.semaphore_signal(barrier, inc=1, device_id={"row": core_peer(step)}, device_id_type=MESH)
        greeted += 1

    def sender(w, k):
        return lax.div(branch_ref[w * slots + k], slots)

    def kth(w, origin, values):
        picks, count = [jnp.int32(0)] * local, jnp.int32(0)
        for k in range(slots):
            hit = sender(w, k) == origin
            picks = [jnp.where(hit & (count == place), values(k), pick) for place, pick in enumerate(picks)]
            count = count + jnp.where(hit, 1, 0)
        return picks

    for copy in own[:3]:
        copy.wait()
    slot_of = list(range(slots))
    if local < slots:
        origins = []
        for step in range(walks):
            target = partner(walk, step, walks)
            picks = kth(target, walk, lambda k: lax.rem(branch_ref[target * slots + k], slots))
            for place, pick in enumerate(picks):
                if step == 0:
                    raw[place, mine] = source[pick]
                else:
                    outgoing[step * local + place] = source[pick]
            origin = target if walks & (walks - 1) == 0 else (walk + walks - step) % walks
            origins.append(origin)
            for place, pick in enumerate(kth(walk, origin, lambda k: k)):
                i = step * local + place
                field_out[i : i + 1, :] = field_in[pl.ds(pick, 1), :]
        for j in range(slots):
            origin, rank, step_of = sender(walk, j), jnp.int32(0), jnp.int32(0)
            for k in range(j):
                rank = rank + jnp.where(sender(walk, k) == origin, 1, 0)
            for step in range(walks):
                step_of = jnp.where(origins[step] == origin, step, step_of)
            slot_of[j] = jnp.minimum(step_of * local + rank, slots - 1)
    else:
        for i in range(slots):
            raw[i, mine] = source[i]
        field_out[...] = field_in[...]
    field[mine] = field_out[...]
    for copy in own[3:]:
        copy.wait()
    pl.semaphore_wait(barrier, greeted)

    def remote(src, dst, send, recv, target):
        return pltpu.make_async_remote_copy(
            src_ref=src, dst_ref=dst, send_sem=send, recv_sem=recv, device_id=target, device_id_type=MESH
        )

    def z_copy(i, step):
        return remote(outgoing.at[i], raw.at[i, mine], z_send.at[i], z_recv.at[i], {"walk": partner(walk, step, walks)})

    def x_copy(i, step):
        return remote(raw.at[i, mine], raw.at[i, mine], x_send.at[step, i], x_recv.at[step, i], {"slab": slab_peer(step)})

    def c_copy(i, hop, step):
        q = slab_source(hop) * cores + core
        return remote(raw.at[i, q], raw.at[i, q], c_send.at[hop, step, i], c_recv.at[hop, step, i], {"row": core_peer(step)})

    def small(src, buf, xs, xr, cs, cr):
        def x(step):
            return remote(src, buf.at[mine], xs.at[step], xr.at[step], {"slab": slab_peer(step)})

        def c(hop, step):
            q = slab_source(hop) * cores + core
            block = src if hop == 0 else buf.at[q]
            return remote(block, buf.at[q], cs.at[hop, step], cr.at[hop, step], {"row": core_peer(step)})

        return x, c

    for i in range(local, slots):
        z_copy(i, i // local).start()
    pairs = [
        small(trial_ref, trial, tx_send, tx_recv, tc_send, tc_recv),
        small(field_out, field, fx_send, fx_recv, fc_send, fc_recv),
    ]
    for x, c in pairs:
        for step in range(1, slabs):
            x(step).start()
        for step in range(1, cores):
            c(0, step).start()
    def spread(i):
        for step in range(1, slabs):
            x_copy(i, step).start()
        for step in range(1, cores):
            c_copy(i, 0, step).start()

    def relay(i):
        for hop in range(1, slabs):
            x_copy(i, hop).wait_recv()
            for step in range(1, cores):
                c_copy(i, hop, step).start()

    def compute(i):
        for hop in range(slabs):
            for step in range(1, cores):
                c_copy(i, hop, step).wait_recv()
        for q in range(slabs * cores):
            column = jnp.transpose(field[q])
            lane = lax.broadcasted_iota(jnp.int32, column.shape, 1)
            scale = jnp.sum(jnp.where(lane == i, column, 0.0), axis=1, keepdims=True)
            prop[q * rows : (q + 1) * rows, :] = (raw[i, q].astype(jnp.float32) * scale).astype(jnp.bfloat16)
        @pl.when(lax.rem(i, cores) == core)
        def _():
            total = dot(trial_t[0], prop[0:rows, :])
            for q in range(1, slabs * cores):
                total += dot(trial_t[q], prop[q * rows : (q + 1) * rows, :])
            inter[i // cores] = total

        half[i] = dot(chol[...], prop[...]).astype(jnp.bfloat16)

    for i in range(local):
        spread(i)
    for x, c in pairs:
        for hop in range(1, slabs):
            x(hop).wait_recv()
            for step in range(1, cores):
                c(hop, step).start()
    for x, c in pairs:
        for hop in range(slabs):
            for step in range(1, cores):
                c(hop, step).wait_recv()

    for q in range(slabs * cores):
        trial_t[q] = jnp.transpose(trial[q].astype(jnp.float32)).astype(jnp.bfloat16)
    share = slots // cores
    line = lax.broadcasted_iota(jnp.int32, (electrons, electrons), 0)
    diagonal = line == lax.broadcasted_iota(jnp.int32, (electrons, electrons), 1)

    def i_copy(i, step):
        place = inverse.at[i]
        return remote(place, place, i_send.at[i // cores, step], i_recv.at[i // cores, step], {"row": core_peer(step)})

    def first_guess(n):
        matrix = inter[n]
        sizes_of = jnp.abs(matrix)
        column_max = jnp.max(jnp.sum(sizes_of, axis=0, keepdims=True), axis=1, keepdims=True)
        row_max = jnp.max(jnp.sum(sizes_of, axis=1, keepdims=True), axis=0, keepdims=True)
        start = jnp.transpose(matrix) / (column_max * row_max)
        stack[0:electrons, :] = start
        stack[electrons:, :] = dot3(matrix, start)

    def finish(i):
        @pl.when(lax.rem(i, cores) != core)
        def _():
            i_copy(i, lax.rem(core + cores - lax.rem(i, cores), cores)).wait_recv()

        contracted = dot(half[i], inverse[i])
        for g in range(vectors):
            block = contracted[g * electrons : (g + 1) * electrons, :]
            traces[i, g : g + 1, :] = jnp.sum(jnp.where(diagonal, block, 0.0), axis=0, keepdims=True)
            squares[i, g : g + 1, :] = jnp.sum(block * jnp.transpose(block), axis=0, keepdims=True)

    ready = cores + 1

    @pl.loop(0, slots + ready + cores + 1)
    def _(i):
        @pl.when((i >= local) & (i < slots))
        def _():
            z_copy(i, 0).wait_recv()
            spread(i)

        @pl.when((i > 1) & (i < slots + 2))
        def _():
            compute(i - 2)

        @pl.when((i > 0) & (i <= slots))
        def _():
            relay(i - 1)

        for part in range(cores):

            @pl.when((i >= ready) & (i < slots + ready) & (lax.rem(i + cores - 1, cores) == part))
            def _():
                n = (i - ready) // cores
                if part == 0:
                    first_guess(n)

                first, middle, last = ITERS * part // cores, EARLY, ITERS * (part + 1) // cores

                @pl.loop(first, max(first, min(middle, last)))
                def _(iteration):
                    both = stack[...]
                    low = both.astype(jnp.bfloat16)
                    stack[...] = 2.0 * both - dot(low, low[electrons:, :])

                @pl.loop(min(last, max(middle, first)), last)
                def _(iteration):
                    both = stack[...]
                    stack[...] = 2.0 * both - dot3(both, both[electrons:, :])

                if part == cores - 1:
                    inverse[n * cores + core] = stack[0:electrons, :].astype(jnp.bfloat16)
                    for step in range(1, cores):
                        i_copy(n * cores + core, step).start()

        @pl.when(i > ready + cores)
        def _():
            finish(i - ready - cores - 1)


    column = lax.broadcasted_iota(jnp.int32, bias_ref.shape, 1)
    for terms, rows_of, result in ((traces, bias_rows, bias_ref), (squares, exch_rows, exch_ref)):
        for j in range(slots):
            block = terms[slot_of[j]]
            for g in range(vectors):
                rows_of[g, j : j + 1, :] = block[g : g + 1, :]
        total = jnp.zeros(result.shape, jnp.float32)
        for g in range(vectors):
            total = jnp.where(column == g, jnp.sum(rows_of[g], axis=1, keepdims=True), total)
        result[...] = total

    for i in range(local, slots):
        z_copy(i, i // local).wait_send()

    @pl.loop(0, slots)
    def _(i):
        for step in range(1, slabs):
            x_copy(i, step).wait_send()
        for hop in range(slabs):
            for step in range(1, cores):
                c_copy(i, hop, step).wait_send()

    for x, c in pairs:
        for step in range(1, slabs):
            x(step).wait_send()
        for hop in range(slabs):
            for step in range(1, cores):
                c(hop, step).wait_send()
    for n in range(share):
        for step in range(1, cores):
            i_copy(n * cores + core, step).wait_send()


def xor(a, b, size):
    result, bit = 0, 1
    while bit < size:
        left, right = lax.rem(lax.div(a, bit), 2), lax.rem(lax.div(b, bit), 2)
        result += bit * lax.rem(left + right, 2)
        bit *= 2
    return result


def origin_kernel(
    sizes, branch_in, count_in, walker_ref, trial_ref, chol_ref, field_ref, bias_ref, exch_ref,
    branch_ref, count_ref, source, fields, chosen, outgoing, prop, trial, trial_t, chol, stack, green, lanes, sums, arrived,
    own_sem, f_send, f_recv, t_send, t_recv, tx_send, tp_sem, cx_send, c_send, c_recv, cp_sem, w_send, w_recv, o_send, o_recv,
):
    walks, slabs, cores, slots, local, items = sizes
    walk, slab, core = lax.axis_index("walk"), lax.axis_index("slab"), lax.axis_index("row")
    rows, electrons = trial_ref.shape
    shards = slabs * cores
    vectors = chol_ref.shape[0] // electrons
    mine = slab * cores + core
    other_slab, other_core = 1 - slab, 1 - core
    across, beside, diagonal_q = other_slab * cores + core, slab * cores + other_core, other_slab * cores + other_core
    below, above = walk > 0, walk < walks - 1
    steps = ((1, 1), (1, 0), (0, 1))

    loads = [(branch_in, branch_ref), (count_in, count_ref), (walker_ref, source), (field_ref, fields.at[walk]), (trial_ref, trial.at[mine]), (chol_ref, chol.at[mine])]
    own = [pltpu.make_async_copy(src, dst, own_sem.at[k]) for k, (src, dst) in enumerate(loads)]
    for copy in own:
        copy.start()
    barrier = pltpu.get_barrier_semaphore()

    def greet(target):
        pl.semaphore_signal(barrier, inc=1, device_id=target, device_id_type=MESH)

    def place_of(dx, dc):
        return {"slab": lax.rem(slab + dx, slabs), "row": lax.rem(core + dc, cores)}

    for dx, dc in steps:
        greet(place_of(dx, dc))

    @pl.when(below)
    def _():
        greet({"walk": walk - 1})

    @pl.when(above)
    def _():
        greet({"walk": walk + 1})

    for copy in own:
        copy.wait()
    pl.semaphore_wait(barrier, len(steps) + jnp.where(below, 1, 0) + jnp.where(above, 1, 0))

    def remote(src, dst, send, recv, target):
        return pltpu.make_async_remote_copy(
            src_ref=src, dst_ref=dst, send_sem=send, recv_sem=recv, device_id=target, device_id_type=MESH
        )

    def field_copy(o, way):
        return remote(fields.at[o], fields.at[o], f_send.at[way, o], f_recv.at[o], {"walk": walk + 1 - 2 * way})

    def trial_view(q, o):
        size = rows // walks
        return trial.at[q, pl.ds(pl.multiple_of(o * size, size), size)]

    def chol_rows(o, p):
        size = chol_ref.shape[0] // (walks * PIECES)
        return pl.ds(pl.multiple_of((o * PIECES + p) * size, size), size)

    def trial_copy(o, way):
        view = trial_view(across, o)
        if way == 2:
            return remote(view, view, t_send.at[2, o], t_recv.at[1, o], {"row": other_core})
        return remote(view, view, t_send.at[way, o], t_recv.at[0, o], {"walk": walk + 1 - 2 * way})

    def trial_beside(o):
        view = trial_view(diagonal_q, o)
        return remote(view, view, t_send.at[2, o], t_recv.at[1, o], {"row": other_core})

    def chol_copy(o, p, way):
        view = chol.at[across, chol_rows(o, p)]
        if way == 2:
            return remote(view, view, c_send.at[2, o, p], c_recv.at[1, o, p], {"row": other_core})
        return remote(view, view, c_send.at[way, o, p], c_recv.at[0, o, p], {"walk": walk + 1 - 2 * way})

    def chol_beside(o, p):
        view = chol.at[diagonal_q, chol_rows(o, p)]
        return remote(view, view, c_send.at[2, o, p], c_recv.at[1, o, p], {"row": other_core})

    def trial_across():
        return remote(trial_view(mine, walk), trial_view(mine, walk), tx_send.at[0], t_recv.at[0, walk], {"slab": other_slab})

    def chol_across(p):
        return remote(chol.at[mine, chol_rows(walk, p)], chol.at[mine, chol_rows(walk, p)], cx_send.at[p], c_recv.at[0, walk, p], {"slab": other_slab})

    trial_whole = remote(trial.at[mine], trial.at[mine], tp_sem.at[0], tp_sem.at[1], {"row": other_core})
    chol_whole = remote(chol.at[mine], chol.at[mine], cp_sem.at[0], cp_sem.at[1], {"row": other_core})

    def both_ways(action):
        @pl.when(above)
        def _():
            action(0)

        @pl.when(below)
        def _():
            action(1)

    def hop(k, arrive, forward):
        @pl.when(walk >= k)
        def _():
            arrive(walk - k)
            if k < walks - 1:
                pl.when(above)(lambda: forward(walk - k, 0))

        @pl.when(walk + k < walks)
        def _():
            arrive(walk + k)
            if k < walks - 1:
                pl.when(below)(lambda: forward(walk + k, 1))

    def field_hop(k):
        hop(k, lambda o: field_copy(o, 0).wait_recv(), lambda o, way: field_copy(o, way).start())

    def trial_arrive(o):
        trial_copy(o, 0).wait_recv()
        trial_copy(o, 2).start()

    def trial_hop(k):
        hop(k, trial_arrive, lambda o, way: trial_copy(o, way).start())

    def chol_hop(k, p):
        def arrive(o):
            chol_copy(o, p, 0).wait_recv()
            chol_copy(o, p, 2).start()

        hop(k, arrive, lambda o, way: chol_copy(o, p, way).start())

    def chol_start(p):
        chol_copy(walk, p, 0).wait_recv()
        both_ways(lambda way: chol_copy(walk, p, way).start())
        chol_copy(walk, p, 2).start()

    def sender(w, k):
        return lax.div(branch_ref[w * slots + k], slots)

    def step_of(number):
        order = lax.div(number, shards) * cores + lax.rem(number, cores)
        return walks - 1 - order, lax.div(lax.rem(number, shards), cores)

    def item_target(number):
        return xor(walk, step_of(number)[0], walks)

    def locate(number):
        target, place = item_target(number), step_of(number)[1]
        pick, spot, count = jnp.int32(0), jnp.int32(0), jnp.int32(0)
        for k in range(slots):
            hit = sender(target, k) == walk
            here = hit & (count == place)
            pick = jnp.where(here, lax.rem(branch_ref[target * slots + k], slots), pick)
            spot = jnp.where(here, k, spot)
            count = count + jnp.where(hit, 1, 0)
        return target, pick, spot

    slot_line = lax.broadcasted_iota(jnp.int32, (slots, rows), 0)
    my_rows = pl.ds(pl.multiple_of(mine * rows, rows), rows)

    def w_copy(r, dx, row):
        place = {"slab": lax.rem(slab + dx, slabs), "row": row}
        return remote(outgoing.at[r, dx * cores + row], prop.at[r, my_rows], w_send.at[r, dx * cores + row], w_recv.at[r, mine], place)

    def send_group(r, row):
        found = []
        for dx in range(slabs):
            target, pick, spot = locate(r * shards + lax.rem(slab + dx, slabs) * cores + row)
            found.append(pick)
            chosen[dx : dx + 1, :] = jnp.sum(jnp.where(slot_line == spot, fields[target], 0.0), axis=0, keepdims=True)
        scales = jnp.transpose(chosen[...])
        for dx in reversed(range(slabs)):
            block = (source[found[dx]].astype(jnp.float32) * scales[:, dx : dx + 1]).astype(jnp.bfloat16)
            outgoing[r, dx * cores + row] = block
            if dx:
                w_copy(r, dx, row).start()
            else:
                pl.when(core != row)(w_copy(r, dx, row).start)

                @pl.when(core == row)
                def _():
                    prop[r, my_rows] = outgoing[r, row]

    both_ways(lambda way: field_copy(walk, way).start())
    trial_across().start()
    for p in range(PIECES):
        chol_across(p).start()
    trial_whole.start()
    chol_whole.start()

    last = walks - 1
    field_hop(1)
    trial_arrive(walk)
    both_ways(lambda way: trial_copy(walk, way).start())
    chol_start(0)
    for k in range(2, last):
        field_hop(k)
    send_group(0, 1)
    trial_hop(1)
    chol_start(1)
    chol_start(2)
    if last > 1:
        field_hop(last)
    send_group(0, 0)
    if last > 1:
        trial_hop(2)
    send_group(1, 0)
    send_group(1, 1)
    chol_start(3)
    for k in range(1, last - 1):
        for p in range(PIECES):
            chol_hop(k, p)
    for k in range(3, walks):
        trial_hop(k)

    @pl.loop(0, walks)
    def _(o):
        trial_beside(o).wait_recv()

    trial_whole.wait_recv()
    for q in range(shards):
        trial_t[:, q * rows : (q + 1) * rows] = jnp.transpose(trial[q].astype(jnp.float32)).astype(jnp.bfloat16)

    line = lax.broadcasted_iota(jnp.int32, (electrons, electrons), 0)
    on_diagonal = line == lax.broadcasted_iota(jnp.int32, (electrons, electrons), 1)

    def invert(r, hooks):
        for q in (beside, across, diagonal_q):
            part = pl.ds(pl.multiple_of(q * rows, rows), rows)
            remote(prop.at[r, part], prop.at[r, part], w_send.at[r, 0], w_recv.at[r, q], {"row": other_core}).wait_recv()
        hooks[0]()
        matrix = dot(trial_t[...], prop[r])
        sizes_of = jnp.abs(matrix)
        column_max = jnp.max(jnp.sum(sizes_of, axis=0, keepdims=True), axis=1, keepdims=True)
        row_max = jnp.max(jnp.sum(sizes_of, axis=1, keepdims=True), axis=0, keepdims=True)
        start = jnp.transpose(matrix) / (column_max * row_max)
        stack[0:electrons, :] = start
        stack[electrons:, :] = dot3(matrix, start)

        hooks[1]()

        @pl.loop(0, PASSES)
        def _(iteration):
            both = stack[...]
            low = both.astype(jnp.bfloat16)
            stack[...] = 2.0 * both - dot(low, low[electrons:, :])

        hooks[2]()

        @pl.loop(PASSES, ITERS)
        def _(iteration):
            both = stack[...]
            stack[...] = 2.0 * both - dot3(both, both[electrons:, :])

        hooks[3]()
        green[r] = dot(prop[r], stack[0:electrons, :].astype(jnp.bfloat16)).astype(jnp.bfloat16)

    blocks = (mine, beside, across, diagonal_q)

    def contract(r, n):
        for g in range(vectors):
            block = dot(chol[blocks[n], g * electrons : (g + 1) * electrons, :], green[r])
            number = n * vectors + g
            lanes[r, 0, number : number + 1, :] = jnp.sum(jnp.where(on_diagonal, block, 0.0), axis=0, keepdims=True)
            lanes[r, 1, number : number + 1, :] = jnp.sum(block * jnp.transpose(block), axis=0, keepdims=True)

    def o_copy(r, dx, dc):
        number = r * shards + mine
        target = item_target(number)
        device = {"walk": target, **place_of(dx, dc)}
        return target, remote(sums.at[r], arrived.at[number], o_send.at[r, dx * cores + dc], o_recv.at[number], device)

    def publish(r):
        for kind in range(2):
            total = jnp.sum(lanes[r, kind], axis=1, keepdims=True)
            sums[r, kind] = jnp.broadcast_to(total, sums.shape[2:])
        for dx, dc in steps:
            o_copy(r, dx, dc)[1].start()
        target, copy = o_copy(r, 0, 0)
        pl.when(target != walk)(copy.start)

        @pl.when(target == walk)
        def _():
            arrived[r * shards + mine] = sums[r]

    def hooks_of(k):
        return [functools.partial(chol_hop, k, p) for p in range(PIECES)] if k > 0 else [lambda: None] * PIECES

    invert(0, hooks_of(last - 1))
    contract(0, 0)
    chol_whole.wait_recv()
    contract(0, 1)
    for r in range(1, items):
        invert(r, hooks_of(last) if r == 1 else hooks_of(0))
    contract(0, 2)

    @pl.loop(0, walks)
    def _(o):
        @pl.loop(0, PIECES)
        def _(p):
            chol_beside(o, p).wait_recv()

    contract(0, 3)
    publish(0)
    for r in range(1, items):
        for n in range(shards):
            contract(r, n)
        publish(r)

    def number_of(j):
        origin, rank = sender(walk, j), jnp.int32(0)
        for k in range(j):
            rank = rank + jnp.where(sender(walk, k) == origin, 1, 0)
        step = jnp.int32(0)
        for s in range(walks):
            step = jnp.where(xor(walk, s, walks) == origin, s, step)
        order = walks - 1 - step
        number = lax.div(order, cores) * shards + lax.min(rank, local - 1) * cores + lax.rem(order, cores)
        return jnp.clip(number, 0, slots - 1)

    numbers = [number_of(j) for j in range(slots)]

    for number in range(slots):
        target = item_target(number)
        from_me = (target == walk) & (mine == number % shards)

        @pl.when(jnp.logical_not(from_me))
        def _():
            remote(sums.at[0], arrived.at[number], o_send.at[0, 0], o_recv.at[number], {"row": other_core}).wait_recv()

    column = lax.broadcasted_iota(jnp.int32, bias_ref.shape, 1)
    for kind, result in enumerate((bias_ref, exch_ref)):
        total = jnp.zeros(result.shape, jnp.float32)
        for j in range(slots):
            q = lax.rem(numbers[j], shards)
            dx, dc = lax.rem(lax.div(q, cores) + slab, slabs), lax.rem(lax.rem(q, cores) + core, cores)
            first = (dx * cores + dc) * vectors
            total = jnp.where(column == j, arrived[numbers[j], kind, pl.ds(first, vectors), 0:slots], total)
        result[...] = jnp.where(column < count_ref[0], total * (1.0, -0.5)[kind], 0.0)

    trial_across().wait_send()
    trial_whole.wait_send()
    chol_whole.wait_send()
    for p in range(PIECES):
        chol_across(p).wait_send()

    @pl.loop(0, walks)
    def _(o):
        trial_copy(o, 2).wait_send()

        def sent(way):
            field_copy(o, way).wait_send()
            trial_copy(o, way).wait_send()

        pl.when(above & (o <= walk))(lambda: sent(0))
        pl.when(below & (o >= walk))(lambda: sent(1))

        @pl.loop(0, PIECES)
        def _(p):
            chol_copy(o, p, 2).wait_send()
            pl.when(above & (o <= walk))(lambda: chol_copy(o, p, 0).wait_send())
            pl.when(below & (o >= walk))(lambda: chol_copy(o, p, 1).wait_send())

    for r in range(items):
        for dx, dc in steps:
            o_copy(r, dx, dc)[1].wait_send()
        target, copy = o_copy(r, 0, 0)
        pl.when(target != walk)(copy.wait_send)
        for row in range(cores):
            for dx in range(1, slabs):
                w_copy(r, dx, row).wait_send()
            pl.when(core != row)(w_copy(r, 0, row).wait_send)


def gathered(walkers, trial_orbitals, cholesky, branches, field):
    walks, slabs, cores = lax.axis_size("walk"), lax.axis_size("slab"), lax.axis_size("row")
    walk = lax.axis_index("walk")
    per_device, rows, electrons = walkers.shape
    vectors = cholesky.shape[0]
    capacity = (per_device + walks - 1) // walks
    local = capacity if walks * capacity == per_device else per_device
    if local == per_device:
        sender = branches.reshape(walks, per_device) // per_device
        local_index = branches.reshape(walks, per_device) % per_device
        places = jnp.arange(per_device, dtype=jnp.int32)
        same_sender = sender[:, :, None] == sender[:, None, :]
        rank = jnp.sum(same_sender & (places[None, :] < places[:, None])[None], axis=2)
        ranks = jnp.arange(capacity, dtype=jnp.int32)[None, :, None]
        wanted = (sender[:, None, :] == walk) & (rank[:, None, :] == ranks)
        chosen = jnp.sum(jnp.where(wanted, local_index[:, None, :], 0), axis=2)
        outgoing = jnp.take(walkers, chosen.reshape(-1), axis=0, mode="clip")
        outgoing = outgoing.reshape(walks, capacity, rows, electrons)
        arrived = lax.all_to_all(outgoing, "walk", split_axis=0, concat_axis=0, tiled=True)
        arrived = arrived.reshape(walks * capacity, rows, electrons)
        my_sender = lax.dynamic_index_in_dim(sender, walk, 0, keepdims=False)
        my_rank = lax.dynamic_index_in_dim(rank, walk, 0, keepdims=False)
        walkers = jnp.take(arrived, my_sender * capacity + my_rank, axis=0, mode="clip")
    shards = slabs * cores
    share = per_device // cores
    dma = pltpu.SemaphoreType.DMA
    vmem = pl.BlockSpec(memory_space=pltpu.VMEM)
    bias, exchange = pl.pallas_call(
        functools.partial(kernel, (walks, slabs, cores, per_device, local)),
        out_shape=[jax.ShapeDtypeStruct((per_device, vectors), jnp.float32)] * 2,
        in_specs=[pl.BlockSpec(memory_space=pl.ANY)] * 5,
        out_specs=[vmem] * 2,
        scratch_shapes=[
            pltpu.SMEM(branches.shape, jnp.int32),
            pltpu.VMEM((shards, electrons, rows), jnp.bfloat16),
            pltpu.VMEM((per_device, rows, electrons), jnp.bfloat16),
            pltpu.VMEM((per_device, rows, electrons), jnp.bfloat16),
            pltpu.VMEM((per_device, rows), jnp.float32),
            pltpu.VMEM((per_device, rows), jnp.float32),
            pltpu.VMEM((per_device, vectors, electrons), jnp.float32),
            pltpu.VMEM((per_device, vectors, electrons), jnp.float32),
            pltpu.VMEM((vectors, per_device, electrons), jnp.float32),
            pltpu.VMEM((vectors, per_device, electrons), jnp.float32),
            pltpu.VMEM((per_device, shards, rows, electrons), jnp.bfloat16),
            pltpu.VMEM((shards, rows, electrons), jnp.bfloat16),
            pltpu.VMEM((shards, per_device, rows), jnp.float32),
            pltpu.VMEM((vectors * electrons, shards * rows), jnp.bfloat16),
            pltpu.VMEM((shards * rows, electrons), jnp.bfloat16),
            pltpu.VMEM((per_device, vectors * electrons, electrons), jnp.bfloat16),
            pltpu.VMEM((share, electrons, electrons), jnp.float32),
            pltpu.VMEM((2 * electrons, electrons), jnp.float32),
            pltpu.VMEM((per_device, electrons, electrons), jnp.bfloat16),
            dma((per_device,)), dma((per_device,)),
            dma((slabs, per_device)), dma((slabs, per_device)),
            dma((slabs, cores, per_device)), dma((slabs, cores, per_device)),
            dma((share, cores)), dma((share, cores)),
            dma((slabs,)), dma((slabs,)), dma((slabs, cores)), dma((slabs, cores)),
            dma((slabs,)), dma((slabs,)), dma((slabs, cores)), dma((slabs, cores)),
            dma((5,)),
        ],
        compiler_params=pltpu.CompilerParams(
            collective_id=0, has_side_effects=True, vmem_limit_bytes=63 * 1024 * 1024
        ),
    )(branches, walkers, trial_orbitals, cholesky.reshape(vectors * electrons, shards * rows), field)
    return bias, exchange


def at_origin(walkers, trial_orbitals, cholesky, branches, counts, field):
    walks, slabs, cores = lax.axis_size("walk"), lax.axis_size("slab"), lax.axis_size("row")
    slots, rows, electrons = walkers.shape
    vectors = cholesky.shape[0]
    shards, local = slabs * cores, slots // walks
    items, lines, columns = slots // shards, vectors * electrons, shards * rows
    dma = pltpu.SemaphoreType.DMA
    vmem = pl.BlockSpec(memory_space=pltpu.VMEM)
    bias, exchange = pl.pallas_call(
        functools.partial(origin_kernel, (walks, slabs, cores, slots, local, items)),
        out_shape=[jax.ShapeDtypeStruct((vectors, slots), jnp.float32)] * 2,
        in_specs=[pl.BlockSpec(memory_space=pl.ANY)] * 6,
        out_specs=[vmem] * 2,
        scratch_shapes=[
            pltpu.SMEM(branches.shape, jnp.int32),
            pltpu.SMEM(counts.shape, jnp.int32),
            pltpu.VMEM((slots, rows, electrons), jnp.bfloat16),
            pltpu.VMEM((walks, slots, rows), jnp.float32),
            pltpu.VMEM((slots, rows), jnp.float32),
            pltpu.VMEM((items, shards, rows, electrons), jnp.bfloat16),
            pltpu.VMEM((items, columns, electrons), jnp.bfloat16),
            pltpu.VMEM((shards, rows, electrons), jnp.bfloat16),
            pltpu.VMEM((electrons, columns), jnp.bfloat16),
            pltpu.VMEM((shards, lines, columns), jnp.bfloat16),
            pltpu.VMEM((2 * electrons, electrons), jnp.float32),
            pltpu.VMEM((items, columns, electrons), jnp.bfloat16),
            pltpu.VMEM((items, 2, shards * vectors, electrons), jnp.float32),
            pltpu.VMEM((items, 2, shards * vectors, 128), jnp.float32),
            pltpu.VMEM((slots, 2, shards * vectors, 128), jnp.float32),
            dma((6,)),
            dma((2, walks)), dma((walks,)),
            dma((3, walks)), dma((2, walks)), dma((2,)), dma((2,)),
            dma((PIECES,)), dma((3, walks, PIECES)), dma((2, walks, PIECES)), dma((2,)),
            dma((items, shards)), dma((items, shards)),
            dma((items, shards)), dma((slots,)),
        ],
        compiler_params=pltpu.CompilerParams(
            collective_id=0, has_side_effects=True, vmem_limit_bytes=60 * 1024 * 1024
        ),
    )(branches, counts, walkers, trial_orbitals, cholesky.reshape(lines, columns), field)
    return bias.T, exchange.T


def on_device(walkers, trial_orbitals, cholesky, branches, counts, field):
    walks, slabs, cores = lax.axis_size("walk"), lax.axis_size("slab"), lax.axis_size("row")
    slots, rows, electrons = walkers.shape
    lines = cholesky.shape[0] * electrons
    even = walks & (walks - 1) == 0 and slots % walks == 0 and slots % (slabs * cores) == 0
    whole = lines % (walks * PIECES * 16) == 0 and rows % (walks * 16) == 0
    if slabs == cores == 2 and slots == 2 * walks and PIECES == 4 and even and whole:
        return at_origin(walkers, trial_orbitals, cholesky, branches, counts, field)
    bias, exchange = gathered(walkers, trial_orbitals, cholesky, branches, field)
    living = (jnp.arange(slots, dtype=jnp.int32) < counts[0]).astype(jnp.float32)[:, None]
    return bias * living, -0.5 * exchange * living


def solution(mesh):
    return jax.shard_map(
        on_device,
        mesh=mesh,
        in_specs=(
            P(("parts", "walk"), ("slab", "row"), None),
            P(("parts", "slab", "row"), None),
            P(("parts", "slab", "row"), None, None),
            P("parts"),
            P(("parts", "walk")),
            P(("parts", "walk"), ("slab", "row")),
        ),
        out_specs=(P(("parts", "walk"), ("slab", "row")), P(("parts", "walk"), ("slab", "row"))),
        check_vma=False,
    )
```

```python
import functools

import jax
import jax.numpy as jnp
from jax import lax
from jax.experimental import pallas as pl
from jax.experimental.pallas import tpu as pltpu
from jax.sharding import PartitionSpec as P

ITERS = 10
EARLY = 4
PASSES = 7
PIECES = 4
DIRECT = 3
LATER = 8
HOOKS = (((), (), (0,), (1,), (2, 3)), ((), (), (), (), (0, 1, 2, 3)))
MESH = pl.DeviceIdType.MESH


def split(x):
    high = x.astype(jnp.bfloat16)
    low = (x - high.astype(jnp.float32)).astype(jnp.bfloat16)
    return high, low


def dot(a, b):
    return jnp.dot(a, b, preferred_element_type=jnp.float32)


def dot3(a, b):
    ah, al = split(a)
    bh, bl = split(b)
    return dot(ah, bh) + (dot(ah, bl) + dot(al, bh))


def partner(position, step, size):
    if size & (size - 1):
        return (position + step) % size
    result, bit = 0, 1
    while bit < size:
        digit = (position // bit) % 2
        result += bit * (1 - digit if step & bit else digit)
        bit *= 2
    return result


def kernel(
    sizes, branch_in, walker_ref, trial_ref, chol_ref, field_ref, bias_ref, exch_ref,
    branch_ref, trial_t, source, outgoing, field_in, field_out, traces, squares, bias_rows, exch_rows, raw, trial, field, chol, prop, half, inter, stack, inverse,
    z_send, z_recv, x_send, x_recv, c_send, c_recv, i_send, i_recv,
    tx_send, tx_recv, tc_send, tc_recv, fx_send, fx_recv, fc_send, fc_recv, own_sem,
):
    walks, slabs, cores, slots, local = sizes
    walk, slab, core = lax.axis_index("walk"), lax.axis_index("slab"), lax.axis_index("row")
    rows, electrons = trial_ref.shape
    vectors = chol_ref.shape[0] // electrons
    mine = slab * cores + core

    def slab_peer(step):
        return lax.rem(slab + step, slabs)

    def core_peer(step):
        return lax.rem(core + step, cores)

    def slab_source(step):
        return lax.rem(slab + slabs - step, slabs)

    def core_source(step):
        return lax.rem(core + cores - step, cores)

    loads = [(branch_in, branch_ref), (walker_ref, source), (field_ref, field_in), (trial_ref, trial.at[mine]), (chol_ref, chol)]
    own = [pltpu.make_async_copy(src, dst, own_sem.at[k]) for k, (src, dst) in enumerate(loads)]
    for copy in own:
        copy.start()
    barrier = pltpu.get_barrier_semaphore()
    greeted = 0
    if local < slots:
        for step in range(1, walks):
            pl.semaphore_signal(barrier, inc=1, device_id={"walk": partner(walk, step, walks)}, device_id_type=MESH)
            greeted += 1
    for step in range(1, slabs):
        pl.semaphore_signal(barrier, inc=1, device_id={"slab": slab_peer(step)}, device_id_type=MESH)
        greeted += 1
    for step in range(1, cores):
        pl.semaphore_signal(barrier, inc=1, device_id={"row": core_peer(step)}, device_id_type=MESH)
        greeted += 1

    def sender(w, k):
        return lax.div(branch_ref[w * slots + k], slots)

    def kth(w, origin, values):
        picks, count = [jnp.int32(0)] * local, jnp.int32(0)
        for k in range(slots):
            hit = sender(w, k) == origin
            picks = [jnp.where(hit & (count == place), values(k), pick) for place, pick in enumerate(picks)]
            count = count + jnp.where(hit, 1, 0)
        return picks

    for copy in own[:3]:
        copy.wait()
    slot_of = list(range(slots))
    if local < slots:
        origins = []
        for step in range(walks):
            target = partner(walk, step, walks)
            picks = kth(target, walk, lambda k: lax.rem(branch_ref[target * slots + k], slots))
            for place, pick in enumerate(picks):
                if step == 0:
                    raw[place, mine] = source[pick]
                else:
                    outgoing[step * local + place] = source[pick]
            origin = target if walks & (walks - 1) == 0 else (walk + walks - step) % walks
            origins.append(origin)
            for place, pick in enumerate(kth(walk, origin, lambda k: k)):
                i = step * local + place
                field_out[i : i + 1, :] = field_in[pl.ds(pick, 1), :]
        for j in range(slots):
            origin, rank, step_of = sender(walk, j), jnp.int32(0), jnp.int32(0)
            for k in range(j):
                rank = rank + jnp.where(sender(walk, k) == origin, 1, 0)
            for step in range(walks):
                step_of = jnp.where(origins[step] == origin, step, step_of)
            slot_of[j] = jnp.minimum(step_of * local + rank, slots - 1)
    else:
        for i in range(slots):
            raw[i, mine] = source[i]
        field_out[...] = field_in[...]
    field[mine] = field_out[...]
    for copy in own[3:]:
        copy.wait()
    pl.semaphore_wait(barrier, greeted)

    def remote(src, dst, send, recv, target):
        return pltpu.make_async_remote_copy(
            src_ref=src, dst_ref=dst, send_sem=send, recv_sem=recv, device_id=target, device_id_type=MESH
        )

    def z_copy(i, step):
        return remote(outgoing.at[i], raw.at[i, mine], z_send.at[i], z_recv.at[i], {"walk": partner(walk, step, walks)})

    def x_copy(i, step):
        return remote(raw.at[i, mine], raw.at[i, mine], x_send.at[step, i], x_recv.at[step, i], {"slab": slab_peer(step)})

    def c_copy(i, hop, step):
        q = slab_source(hop) * cores + core
        return remote(raw.at[i, q], raw.at[i, q], c_send.at[hop, step, i], c_recv.at[hop, step, i], {"row": core_peer(step)})

    def small(src, buf, xs, xr, cs, cr):
        def x(step):
            return remote(src, buf.at[mine], xs.at[step], xr.at[step], {"slab": slab_peer(step)})

        def c(hop, step):
            q = slab_source(hop) * cores + core
            block = src if hop == 0 else buf.at[q]
            return remote(block, buf.at[q], cs.at[hop, step], cr.at[hop, step], {"row": core_peer(step)})

        return x, c

    for i in range(local, slots):
        z_copy(i, i // local).start()
    pairs = [
        small(trial_ref, trial, tx_send, tx_recv, tc_send, tc_recv),
        small(field_out, field, fx_send, fx_recv, fc_send, fc_recv),
    ]
    for x, c in pairs:
        for step in range(1, slabs):
            x(step).start()
        for step in range(1, cores):
            c(0, step).start()
    def spread(i):
        for step in range(1, slabs):
            x_copy(i, step).start()
        for step in range(1, cores):
            c_copy(i, 0, step).start()

    def relay(i):
        for hop in range(1, slabs):
            x_copy(i, hop).wait_recv()
            for step in range(1, cores):
                c_copy(i, hop, step).start()

    def compute(i):
        for hop in range(slabs):
            for step in range(1, cores):
                c_copy(i, hop, step).wait_recv()
        for q in range(slabs * cores):
            column = jnp.transpose(field[q])
            lane = lax.broadcasted_iota(jnp.int32, column.shape, 1)
            scale = jnp.sum(jnp.where(lane == i, column, 0.0), axis=1, keepdims=True)
            prop[q * rows : (q + 1) * rows, :] = (raw[i, q].astype(jnp.float32) * scale).astype(jnp.bfloat16)
        @pl.when(lax.rem(i, cores) == core)
        def _():
            total = dot(trial_t[0], prop[0:rows, :])
            for q in range(1, slabs * cores):
                total += dot(trial_t[q], prop[q * rows : (q + 1) * rows, :])
            inter[i // cores] = total

        half[i] = dot(chol[...], prop[...]).astype(jnp.bfloat16)

    for i in range(local):
        spread(i)
    for x, c in pairs:
        for hop in range(1, slabs):
            x(hop).wait_recv()
            for step in range(1, cores):
                c(hop, step).start()
    for x, c in pairs:
        for hop in range(slabs):
            for step in range(1, cores):
                c(hop, step).wait_recv()

    for q in range(slabs * cores):
        trial_t[q] = jnp.transpose(trial[q].astype(jnp.float32)).astype(jnp.bfloat16)
    share = slots // cores
    line = lax.broadcasted_iota(jnp.int32, (electrons, electrons), 0)
    diagonal = line == lax.broadcasted_iota(jnp.int32, (electrons, electrons), 1)

    def i_copy(i, step):
        place = inverse.at[i]
        return remote(place, place, i_send.at[i // cores, step], i_recv.at[i // cores, step], {"row": core_peer(step)})

    def first_guess(n):
        matrix = inter[n]
        sizes_of = jnp.abs(matrix)
        column_max = jnp.max(jnp.sum(sizes_of, axis=0, keepdims=True), axis=1, keepdims=True)
        row_max = jnp.max(jnp.sum(sizes_of, axis=1, keepdims=True), axis=0, keepdims=True)
        start = jnp.transpose(matrix) / (column_max * row_max)
        stack[0:electrons, :] = start
        stack[electrons:, :] = dot3(matrix, start)

    def finish(i):
        @pl.when(lax.rem(i, cores) != core)
        def _():
            i_copy(i, lax.rem(core + cores - lax.rem(i, cores), cores)).wait_recv()

        contracted = dot(half[i], inverse[i])
        for g in range(vectors):
            block = contracted[g * electrons : (g + 1) * electrons, :]
            traces[i, g : g + 1, :] = jnp.sum(jnp.where(diagonal, block, 0.0), axis=0, keepdims=True)
            squares[i, g : g + 1, :] = jnp.sum(block * jnp.transpose(block), axis=0, keepdims=True)

    ready = cores + 1

    @pl.loop(0, slots + ready + cores + 1)
    def _(i):
        @pl.when((i >= local) & (i < slots))
        def _():
            z_copy(i, 0).wait_recv()
            spread(i)

        @pl.when((i > 1) & (i < slots + 2))
        def _():
            compute(i - 2)

        @pl.when((i > 0) & (i <= slots))
        def _():
            relay(i - 1)

        for part in range(cores):

            @pl.when((i >= ready) & (i < slots + ready) & (lax.rem(i + cores - 1, cores) == part))
            def _():
                n = (i - ready) // cores
                if part == 0:
                    first_guess(n)

                first, middle, last = ITERS * part // cores, EARLY, ITERS * (part + 1) // cores

                @pl.loop(first, max(first, min(middle, last)))
                def _(iteration):
                    both = stack[...]
                    low = both.astype(jnp.bfloat16)
                    stack[...] = 2.0 * both - dot(low, low[electrons:, :])

                @pl.loop(min(last, max(middle, first)), last)
                def _(iteration):
                    both = stack[...]
                    stack[...] = 2.0 * both - dot3(both, both[electrons:, :])

                if part == cores - 1:
                    inverse[n * cores + core] = stack[0:electrons, :].astype(jnp.bfloat16)
                    for step in range(1, cores):
                        i_copy(n * cores + core, step).start()

        @pl.when(i > ready + cores)
        def _():
            finish(i - ready - cores - 1)


    column = lax.broadcasted_iota(jnp.int32, bias_ref.shape, 1)
    for terms, rows_of, result in ((traces, bias_rows, bias_ref), (squares, exch_rows, exch_ref)):
        for j in range(slots):
            block = terms[slot_of[j]]
            for g in range(vectors):
                rows_of[g, j : j + 1, :] = block[g : g + 1, :]
        total = jnp.zeros(result.shape, jnp.float32)
        for g in range(vectors):
            total = jnp.where(column == g, jnp.sum(rows_of[g], axis=1, keepdims=True), total)
        result[...] = total

    for i in range(local, slots):
        z_copy(i, i // local).wait_send()

    @pl.loop(0, slots)
    def _(i):
        for step in range(1, slabs):
            x_copy(i, step).wait_send()
        for hop in range(slabs):
            for step in range(1, cores):
                c_copy(i, hop, step).wait_send()

    for x, c in pairs:
        for step in range(1, slabs):
            x(step).wait_send()
        for hop in range(slabs):
            for step in range(1, cores):
                c(hop, step).wait_send()
    for n in range(share):
        for step in range(1, cores):
            i_copy(n * cores + core, step).wait_send()


def xor(a, b, size):
    result, bit = 0, 1
    while bit < size:
        left, right = lax.rem(lax.div(a, bit), 2), lax.rem(lax.div(b, bit), 2)
        result += bit * lax.rem(left + right, 2)
        bit *= 2
    return result


def origin_kernel(
    sizes, branch_in, walker_ref, trial_ref, chol_ref, field_ref, bias_ref, exch_ref,
    branch_ref, source, fields, chosen, outgoing, prop, trial, trial_t, chol, stack, green, lanes, sums, arrived,
    own_sem, f_send, f_recv, t_send, t_recv, tx_send, tp_sem, cx_send, cd_send, c_send, c_recv, cp_sem, w_send, w_recv, o_send, o_recv,
):
    walks, slabs, cores, slots, local, items = sizes
    walk, slab, core = lax.axis_index("walk"), lax.axis_index("slab"), lax.axis_index("row")
    rows, electrons = trial_ref.shape
    shards = slabs * cores
    vectors = chol_ref.shape[0] // electrons
    mine = slab * cores + core
    other_slab, other_core = 1 - slab, 1 - core
    across, beside, diagonal_q = other_slab * cores + core, slab * cores + other_core, other_slab * cores + other_core
    below, above = walk > 0, walk < walks - 1
    steps = ((1, 1), (1, 0), (0, 1))

    loads = [(branch_in, branch_ref), (walker_ref, source), (field_ref, fields.at[walk]), (trial_ref, trial.at[mine]), (chol_ref, chol.at[mine])]
    own = [pltpu.make_async_copy(src, dst, own_sem.at[k]) for k, (src, dst) in enumerate(loads)]
    for copy in own:
        copy.start()
    barrier = pltpu.get_barrier_semaphore()

    def greet(target):
        pl.semaphore_signal(barrier, inc=1, device_id=target, device_id_type=MESH)

    def place_of(dx, dc):
        return {"slab": lax.rem(slab + dx, slabs), "row": lax.rem(core + dc, cores)}

    for dx, dc in steps:
        greet(place_of(dx, dc))

    @pl.when(below)
    def _():
        greet({"walk": walk - 1})

    @pl.when(above)
    def _():
        greet({"walk": walk + 1})

    for copy in own:
        copy.wait()
    pl.semaphore_wait(barrier, len(steps) + jnp.where(below, 1, 0) + jnp.where(above, 1, 0))

    def remote(src, dst, send, recv, target):
        return pltpu.make_async_remote_copy(
            src_ref=src, dst_ref=dst, send_sem=send, recv_sem=recv, device_id=target, device_id_type=MESH
        )

    def field_copy(o, way):
        return remote(fields.at[o], fields.at[o], f_send.at[way, o], f_recv.at[o], {"walk": walk + 1 - 2 * way})

    half = lax.rem(walk, 2)

    def trial_view(q, part):
        size = rows // 2
        return trial.at[q, pl.ds(pl.multiple_of(part * size, size), size)]

    def chol_rows(o, p):
        size = chol_ref.shape[0] // (walks * PIECES)
        return pl.ds(pl.multiple_of((o * PIECES + p) * size, size), size)

    def trial_next(part):
        view = trial_view(across, part)
        return remote(view, view, t_send.at[0], t_recv.at[0, part], {"walk": walk + 1 - 2 * half})

    def trial_relay(part):
        view = trial_view(across, part)
        return remote(view, view, t_send.at[1 + part], t_recv.at[1, part], {"row": other_core})

    def trial_beside(part):
        view = trial_view(diagonal_q, part)
        return remote(view, view, t_send.at[1 + part], t_recv.at[1, part], {"row": other_core})

    def chol_copy(o, p, way):
        view = chol.at[across, chol_rows(o, p)]
        if way == 2:
            return remote(view, view, c_send.at[2, o, p], c_recv.at[1, o, p], {"row": other_core})
        return remote(view, view, c_send.at[way, o, p], c_recv.at[0, o, p], {"walk": walk + 1 - 2 * way})

    def chol_beside(o, p):
        view = chol.at[diagonal_q, chol_rows(o, p)]
        return remote(view, view, c_send.at[2, o, p], c_recv.at[1, o, p], {"row": other_core})

    def trial_across():
        view = trial_view(mine, half)
        return remote(view, view, tx_send.at[0], t_recv.at[0, half], {"slab": other_slab})

    def chol_across(p):
        return remote(chol.at[mine, chol_rows(walk, p)], chol.at[mine, chol_rows(walk, p)], cx_send.at[p], c_recv.at[0, walk, p], {"slab": other_slab})

    trial_whole = remote(trial.at[mine], trial.at[mine], tp_sem.at[0], tp_sem.at[1], {"row": other_core})
    chol_whole = remote(chol.at[mine], chol.at[mine], cp_sem.at[0], cp_sem.at[1], {"row": other_core})

    def both_ways(action):
        @pl.when(above)
        def _():
            action(0)

        @pl.when(below)
        def _():
            action(1)

    def hop(k, arrive, forward):
        @pl.when(walk >= k)
        def _():
            arrive(walk - k)
            if k < walks - 1:
                pl.when(above)(lambda: forward(walk - k, 0))

        @pl.when(walk + k < walks)
        def _():
            arrive(walk + k)
            if k < walks - 1:
                pl.when(below)(lambda: forward(walk + k, 1))

    def field_hop(k):
        hop(k, lambda o: field_copy(o, 0).wait_recv(), lambda o, way: field_copy(o, way).start())

    def chol_hop(k, p):
        def arrive(o):
            chol_copy(o, p, 0).wait_recv()
            chol_copy(o, p, 2).start()

        def forward(o, way):
            if k < walks - 2 or p < PIECES - DIRECT:
                chol_copy(o, p, way).start()

        hop(k, arrive, forward)

    def chol_direct(p, action):
        if walks > 2:
            far = walks - 1 - walk
            view = chol.at[mine, chol_rows(far, p)]
            copy = remote(view, view, cd_send.at[p], c_recv.at[0, far, p], {"slab": other_slab})
            pl.when(jnp.logical_not(above & below))(lambda: action(copy))

    def chol_start(p):
        chol_copy(walk, p, 0).wait_recv()
        both_ways(lambda way: chol_copy(walk, p, way).start())
        chol_copy(walk, p, 2).start()

    def sender(w, k):
        return lax.div(branch_ref[w * slots + k], slots)

    def step_of(number):
        order = lax.div(number, shards) * cores + lax.rem(number, cores)
        return walks - 1 - order, lax.div(lax.rem(number, shards), cores)

    def item_target(number):
        return xor(walk, step_of(number)[0], walks)

    def locate(number):
        target, place = item_target(number), step_of(number)[1]
        pick, spot, count = jnp.int32(0), jnp.int32(0), jnp.int32(0)
        for k in range(slots):
            hit = sender(target, k) == walk
            here = hit & (count == place)
            pick = jnp.where(here, lax.rem(branch_ref[target * slots + k], slots), pick)
            spot = jnp.where(here, k, spot)
            count = count + jnp.where(hit, 1, 0)
        return target, pick, spot

    slot_line = lax.broadcasted_iota(jnp.int32, (slots, rows), 0)
    my_rows = pl.ds(pl.multiple_of(mine * rows, rows), rows)

    def w_copy(r, dx, row):
        place = {"slab": lax.rem(slab + dx, slabs), "row": row}
        return remote(outgoing.at[r, dx * cores + row], prop.at[r, my_rows], w_send.at[r, dx * cores + row], w_recv.at[r, mine], place)

    def send_group(r, row):
        found = []
        for dx in range(slabs):
            target, pick, spot = locate(r * shards + lax.rem(slab + dx, slabs) * cores + row)
            found.append(pick)
            chosen[dx : dx + 1, :] = jnp.sum(jnp.where(slot_line == spot, fields[target], 0.0), axis=0, keepdims=True)
        scales = jnp.transpose(chosen[...])
        for dx in reversed(range(slabs)):
            block = (source[found[dx]].astype(jnp.float32) * scales[:, dx : dx + 1]).astype(jnp.bfloat16)
            outgoing[r, dx * cores + row] = block
            if dx:
                w_copy(r, dx, row).start()
            else:
                pl.when(core != row)(w_copy(r, dx, row).start)

                @pl.when(core == row)
                def _():
                    prop[r, my_rows] = outgoing[r, row]

    both_ways(lambda way: field_copy(walk, way).start())
    chol_across(0).start()
    trial_across().start()
    for p in range(1, PIECES):
        chol_across(p).start()
    trial_whole.start()
    chol_whole.start()

    last = walks - 1
    field_hop(1)
    chol_start(0)
    for k in range(2, last):
        field_hop(k)
    trial_next(half).wait_recv()
    trial_next(half).start()
    trial_relay(half).start()
    send_group(0, 1)
    chol_start(1)
    if last > 1:
        field_hop(last)
    send_group(0, 0)
    send_group(1, 0)
    send_group(1, 1)
    for p in range(PIECES - DIRECT, PIECES):
        chol_direct(p, lambda copy: copy.start())
    if last > 2:
        chol_hop(1, 0)
    chol_start(2)
    trial_next(1 - half).wait_recv()
    trial_relay(1 - half).start()
    chol_start(3)
    for k in range(1, last - 1):
        for p in range(1 if k == 1 else 0, PIECES):
            chol_hop(k, p)
    for part in range(2):
        trial_beside(part).wait_recv()
    trial_whole.wait_recv()
    for q in range(shards):
        trial_t[:, q * rows : (q + 1) * rows] = jnp.transpose(trial[q].astype(jnp.float32)).astype(jnp.bfloat16)

    line = lax.broadcasted_iota(jnp.int32, (electrons, electrons), 0)
    on_diagonal = line == lax.broadcasted_iota(jnp.int32, (electrons, electrons), 1)

    def invert(r, hooks):
        for q in (beside, across, diagonal_q):
            part = pl.ds(pl.multiple_of(q * rows, rows), rows)
            remote(prop.at[r, part], prop.at[r, part], w_send.at[r, 0], w_recv.at[r, q], {"row": other_core}).wait_recv()
        hooks[0]()
        matrix = dot(trial_t[...], prop[r])
        sizes_of = jnp.abs(matrix)
        column_max = jnp.max(jnp.sum(sizes_of, axis=0, keepdims=True), axis=1, keepdims=True)
        row_max = jnp.max(jnp.sum(sizes_of, axis=1, keepdims=True), axis=0, keepdims=True)
        start = jnp.transpose(matrix) / (column_max * row_max)
        stack[0:electrons, :] = start
        stack[electrons:, :] = dot3(matrix, start)

        hooks[1]()

        @pl.loop(0, PASSES)
        def _(iteration):
            both = stack[...]
            low = both.astype(jnp.bfloat16)
            stack[...] = 2.0 * both - dot(low, low[electrons:, :])

        hooks[2]()

        for first, end, hook in ((PASSES, LATER, 3), (LATER, ITERS, 4)):

            @pl.loop(first, end)
            def _(iteration):
                both = stack[...]
                stack[...] = 2.0 * both - dot3(both, both[electrons:, :])

            hooks[hook]()

        green[r] = dot(prop[r], stack[0:electrons, :].astype(jnp.bfloat16)).astype(jnp.bfloat16)

    blocks = (mine, beside, across, diagonal_q)

    def contract(r, n):
        for g in range(vectors):
            block = dot(chol[blocks[n], g * electrons : (g + 1) * electrons, :], green[r])
            number = n * vectors + g
            lanes[r, 0, number : number + 1, :] = jnp.sum(jnp.where(on_diagonal, block, 0.0), axis=0, keepdims=True)
            lanes[r, 1, number : number + 1, :] = jnp.sum(block * jnp.transpose(block), axis=0, keepdims=True)

    def o_copy(r, dx, dc):
        number = r * shards + mine
        target = item_target(number)
        device = {"walk": target, **place_of(dx, dc)}
        return target, remote(sums.at[r], arrived.at[number], o_send.at[r, dx * cores + dc], o_recv.at[number], device)

    def publish(r):
        for kind in range(2):
            total = jnp.sum(lanes[r, kind], axis=1, keepdims=True)
            sums[r, kind] = jnp.broadcast_to(total, sums.shape[2:])
        for dx, dc in steps:
            o_copy(r, dx, dc)[1].start()
        target, copy = o_copy(r, 0, 0)
        pl.when(target != walk)(copy.start)

        @pl.when(target == walk)
        def _():
            arrived[r * shards + mine] = sums[r]

    def hooks_of(k, pieces):
        def relay(group):
            def run():
                if k > 0:
                    for p in group:
                        chol_hop(k, p)

            return run

        return [relay(group) for group in pieces]

    invert(0, hooks_of(last - 1 if last > 2 else 0, HOOKS[0]))
    contract(0, 0)
    chol_whole.wait_recv()
    contract(0, 1)
    for r in range(1, items):
        invert(r, hooks_of(last, HOOKS[1]) if r == 1 else hooks_of(0, HOOKS[1]))
        contract(r, 0)
        contract(r, 1)
    contract(0, 2)

    @pl.loop(0, walks)
    def _(o):
        @pl.loop(0, PIECES)
        def _(p):
            chol_beside(o, p).wait_recv()

    contract(0, 3)
    publish(0)
    for r in range(1, items):
        for n in range(2, shards):
            contract(r, n)
        publish(r)

    def number_of(j):
        origin, rank = sender(walk, j), jnp.int32(0)
        for k in range(j):
            rank = rank + jnp.where(sender(walk, k) == origin, 1, 0)
        step = jnp.int32(0)
        for s in range(walks):
            step = jnp.where(xor(walk, s, walks) == origin, s, step)
        order = walks - 1 - step
        number = lax.div(order, cores) * shards + lax.min(rank, local - 1) * cores + lax.rem(order, cores)
        return jnp.clip(number, 0, slots - 1)

    numbers = [number_of(j) for j in range(slots)]

    for number in range(slots):
        target = item_target(number)
        from_me = (target == walk) & (mine == number % shards)

        @pl.when(jnp.logical_not(from_me))
        def _():
            remote(sums.at[0], arrived.at[number], o_send.at[0, 0], o_recv.at[number], {"row": other_core}).wait_recv()

    column = lax.broadcasted_iota(jnp.int32, bias_ref.shape, 1)
    for kind, result in enumerate((bias_ref, exch_ref)):
        total = jnp.zeros(result.shape, jnp.float32)
        for j in range(slots):
            q = lax.rem(numbers[j], shards)
            dx, dc = lax.rem(lax.div(q, cores) + slab, slabs), lax.rem(lax.rem(q, cores) + core, cores)
            first = (dx * cores + dc) * vectors
            total = jnp.where(column == j, arrived[numbers[j], kind, pl.ds(first, vectors), 0:slots], total)
        result[...] = total

    trial_across().wait_send()
    trial_next(half).wait_send()
    for part in range(2):
        trial_relay(part).wait_send()
    trial_whole.wait_send()
    for p in range(PIECES - DIRECT, PIECES):
        chol_direct(p, lambda copy: copy.wait_send())
    chol_whole.wait_send()
    for p in range(PIECES):
        chol_across(p).wait_send()

    @pl.loop(0, walks)
    def _(o):
        def sent(way):
            field_copy(o, way).wait_send()

        pl.when(above & (o <= walk))(lambda: sent(0))
        pl.when(below & (o >= walk))(lambda: sent(1))

        @pl.loop(0, PIECES)
        def _(p):
            chol_copy(o, p, 2).wait_send()
            chained = (p < PIECES - DIRECT) | (walks < 3)
            upward, downward = (o > 0) | (walk < walks - 2), (o < walks - 1) | (walk > 1)
            pl.when(above & (o <= walk) & (chained | upward))(lambda: chol_copy(o, p, 0).wait_send())
            pl.when(below & (o >= walk) & (chained | downward))(lambda: chol_copy(o, p, 1).wait_send())

    for r in range(items):
        for dx, dc in steps:
            o_copy(r, dx, dc)[1].wait_send()
        target, copy = o_copy(r, 0, 0)
        pl.when(target != walk)(copy.wait_send)
        for row in range(cores):
            for dx in range(1, slabs):
                w_copy(r, dx, row).wait_send()
            pl.when(core != row)(w_copy(r, 0, row).wait_send)


def gathered(walkers, trial_orbitals, cholesky, branches, field):
    walks, slabs, cores = lax.axis_size("walk"), lax.axis_size("slab"), lax.axis_size("row")
    walk = lax.axis_index("walk")
    per_device, rows, electrons = walkers.shape
    vectors = cholesky.shape[0]
    capacity = (per_device + walks - 1) // walks
    local = capacity if walks * capacity == per_device else per_device
    if local == per_device:
        sender = branches.reshape(walks, per_device) // per_device
        local_index = branches.reshape(walks, per_device) % per_device
        places = jnp.arange(per_device, dtype=jnp.int32)
        same_sender = sender[:, :, None] == sender[:, None, :]
        rank = jnp.sum(same_sender & (places[None, :] < places[:, None])[None], axis=2)
        ranks = jnp.arange(capacity, dtype=jnp.int32)[None, :, None]
        wanted = (sender[:, None, :] == walk) & (rank[:, None, :] == ranks)
        chosen = jnp.sum(jnp.where(wanted, local_index[:, None, :], 0), axis=2)
        outgoing = jnp.take(walkers, chosen.reshape(-1), axis=0, mode="clip")
        outgoing = outgoing.reshape(walks, capacity, rows, electrons)
        arrived = lax.all_to_all(outgoing, "walk", split_axis=0, concat_axis=0, tiled=True)
        arrived = arrived.reshape(walks * capacity, rows, electrons)
        my_sender = lax.dynamic_index_in_dim(sender, walk, 0, keepdims=False)
        my_rank = lax.dynamic_index_in_dim(rank, walk, 0, keepdims=False)
        walkers = jnp.take(arrived, my_sender * capacity + my_rank, axis=0, mode="clip")
    shards = slabs * cores
    share = per_device // cores
    dma = pltpu.SemaphoreType.DMA
    vmem = pl.BlockSpec(memory_space=pltpu.VMEM)
    bias, exchange = pl.pallas_call(
        functools.partial(kernel, (walks, slabs, cores, per_device, local)),
        out_shape=[jax.ShapeDtypeStruct((per_device, vectors), jnp.float32)] * 2,
        in_specs=[pl.BlockSpec(memory_space=pl.ANY)] * 5,
        out_specs=[vmem] * 2,
        scratch_shapes=[
            pltpu.SMEM(branches.shape, jnp.int32),
            pltpu.VMEM((shards, electrons, rows), jnp.bfloat16),
            pltpu.VMEM((per_device, rows, electrons), jnp.bfloat16),
            pltpu.VMEM((per_device, rows, electrons), jnp.bfloat16),
            pltpu.VMEM((per_device, rows), jnp.float32),
            pltpu.VMEM((per_device, rows), jnp.float32),
            pltpu.VMEM((per_device, vectors, electrons), jnp.float32),
            pltpu.VMEM((per_device, vectors, electrons), jnp.float32),
            pltpu.VMEM((vectors, per_device, electrons), jnp.float32),
            pltpu.VMEM((vectors, per_device, electrons), jnp.float32),
            pltpu.VMEM((per_device, shards, rows, electrons), jnp.bfloat16),
            pltpu.VMEM((shards, rows, electrons), jnp.bfloat16),
            pltpu.VMEM((shards, per_device, rows), jnp.float32),
            pltpu.VMEM((vectors * electrons, shards * rows), jnp.bfloat16),
            pltpu.VMEM((shards * rows, electrons), jnp.bfloat16),
            pltpu.VMEM((per_device, vectors * electrons, electrons), jnp.bfloat16),
            pltpu.VMEM((share, electrons, electrons), jnp.float32),
            pltpu.VMEM((2 * electrons, electrons), jnp.float32),
            pltpu.VMEM((per_device, electrons, electrons), jnp.bfloat16),
            dma((per_device,)), dma((per_device,)),
            dma((slabs, per_device)), dma((slabs, per_device)),
            dma((slabs, cores, per_device)), dma((slabs, cores, per_device)),
            dma((share, cores)), dma((share, cores)),
            dma((slabs,)), dma((slabs,)), dma((slabs, cores)), dma((slabs, cores)),
            dma((slabs,)), dma((slabs,)), dma((slabs, cores)), dma((slabs, cores)),
            dma((5,)),
        ],
        compiler_params=pltpu.CompilerParams(
            collective_id=0, has_side_effects=True, vmem_limit_bytes=63 * 1024 * 1024
        ),
    )(branches, walkers, trial_orbitals, cholesky.reshape(vectors * electrons, shards * rows), field)
    return bias, exchange


def at_origin(walkers, trial_orbitals, cholesky, branches, field):
    walks, slabs, cores = lax.axis_size("walk"), lax.axis_size("slab"), lax.axis_size("row")
    slots, rows, electrons = walkers.shape
    vectors = cholesky.shape[0]
    shards, local = slabs * cores, slots // walks
    items, lines, columns = slots // shards, vectors * electrons, shards * rows
    dma = pltpu.SemaphoreType.DMA
    vmem = pl.BlockSpec(memory_space=pltpu.VMEM)
    bias, exchange = pl.pallas_call(
        functools.partial(origin_kernel, (walks, slabs, cores, slots, local, items)),
        out_shape=[jax.ShapeDtypeStruct((vectors, slots), jnp.float32)] * 2,
        in_specs=[pl.BlockSpec(memory_space=pltpu.HBM)] * 5,
        out_specs=[vmem] * 2,
        scratch_shapes=[
            pltpu.SMEM(branches.shape, jnp.int32),
            pltpu.VMEM((slots, rows, electrons), jnp.bfloat16),
            pltpu.VMEM((walks, slots, rows), jnp.float32),
            pltpu.VMEM((slots, rows), jnp.float32),
            pltpu.VMEM((items, shards, rows, electrons), jnp.bfloat16),
            pltpu.VMEM((items, columns, electrons), jnp.bfloat16),
            pltpu.VMEM((shards, rows, electrons), jnp.bfloat16),
            pltpu.VMEM((electrons, columns), jnp.bfloat16),
            pltpu.VMEM((shards, lines, columns), jnp.bfloat16),
            pltpu.VMEM((2 * electrons, electrons), jnp.float32),
            pltpu.VMEM((items, columns, electrons), jnp.bfloat16),
            pltpu.VMEM((items, 2, shards * vectors, electrons), jnp.float32),
            pltpu.VMEM((items, 2, shards * vectors, 128), jnp.float32),
            pltpu.VMEM((slots, 2, shards * vectors, 128), jnp.float32),
            dma((5,)),
            dma((2, walks)), dma((walks,)),
            dma((3,)), dma((2, 2)), dma((2,)), dma((2,)),
            dma((PIECES,)), dma((PIECES,)), dma((3, walks, PIECES)), dma((2, walks, PIECES)), dma((2,)),
            dma((items, shards)), dma((items, shards)),
            dma((items, shards)), dma((slots,)),
        ],
        compiler_params=pltpu.CompilerParams(
            collective_id=0, has_side_effects=True, vmem_limit_bytes=55200 * 1024
        ),
    )(branches, walkers, trial_orbitals, cholesky.reshape(lines, columns), field)
    return bias.T, exchange.T


def on_device(walkers, trial_orbitals, cholesky, branches, counts, field):
    walks, slabs, cores = lax.axis_size("walk"), lax.axis_size("slab"), lax.axis_size("row")
    slots, rows, electrons = walkers.shape
    lines = cholesky.shape[0] * electrons
    even = walks & (walks - 1) == 0 and slots % walks == 0 and slots % (slabs * cores) == 0
    whole = lines % (walks * PIECES * 16) == 0 and rows % 32 == 0 and walks > 2
    if slabs == cores == 2 and slots == 2 * walks and PIECES == 4 and even and whole:
        bias, exchange = at_origin(walkers, trial_orbitals, cholesky, branches, field)
    else:
        bias, exchange = gathered(walkers, trial_orbitals, cholesky, branches, field)
    living = (jnp.arange(slots, dtype=jnp.int32) < counts[0]).astype(jnp.float32)[:, None]
    return bias * living, -0.5 * exchange * living


def solution(mesh):
    return jax.shard_map(
        on_device,
        mesh=mesh,
        in_specs=(
            P(("parts", "walk"), ("slab", "row"), None),
            P(("parts", "slab", "row"), None),
            P(("parts", "slab", "row"), None, None),
            P("parts"),
            P(("parts", "walk")),
            P(("parts", "walk"), ("slab", "row")),
        ),
        out_specs=(P(("parts", "walk"), ("slab", "row")), P(("parts", "walk"), ("slab", "row"))),
        check_vma=False,
    )
```

```python
import functools

import jax
import jax.numpy as jnp
from jax import lax
from jax.experimental import pallas as pl
from jax.experimental.pallas import tpu as pltpu
from jax.sharding import PartitionSpec as P

ITERS = 10
EARLY = 4
PASSES = 7
PIECES = 4
DIRECT = 3
LATER = 8
HOOKS = (((), (), (0,), (1,), (2, 3)), ((), (), (), (), (0, 1, 2, 3)))
MESH = pl.DeviceIdType.MESH


def split(x):
    high = x.astype(jnp.bfloat16)
    low = (x - high.astype(jnp.float32)).astype(jnp.bfloat16)
    return high, low


def dot(a, b):
    return jnp.dot(a, b, preferred_element_type=jnp.float32)


def dot3(a, b):
    ah, al = split(a)
    bh, bl = split(b)
    return dot(ah, bh) + (dot(ah, bl) + dot(al, bh))


def partner(position, step, size):
    if size & (size - 1):
        return (position + step) % size
    result, bit = 0, 1
    while bit < size:
        digit = (position // bit) % 2
        result += bit * (1 - digit if step & bit else digit)
        bit *= 2
    return result


def kernel(
    sizes, branch_in, walker_ref, trial_ref, chol_ref, field_ref, bias_ref, exch_ref,
    branch_ref, trial_t, source, outgoing, field_in, field_out, traces, squares, bias_rows, exch_rows, raw, trial, field, chol, prop, half, inter, stack, inverse,
    z_send, z_recv, x_send, x_recv, c_send, c_recv, i_send, i_recv,
    tx_send, tx_recv, tc_send, tc_recv, fx_send, fx_recv, fc_send, fc_recv, own_sem,
):
    walks, slabs, cores, slots, local = sizes
    walk, slab, core = lax.axis_index("walk"), lax.axis_index("slab"), lax.axis_index("row")
    rows, electrons = trial_ref.shape
    vectors = chol_ref.shape[0] // electrons
    mine = slab * cores + core

    def slab_peer(step):
        return lax.rem(slab + step, slabs)

    def core_peer(step):
        return lax.rem(core + step, cores)

    def slab_source(step):
        return lax.rem(slab + slabs - step, slabs)

    def core_source(step):
        return lax.rem(core + cores - step, cores)

    loads = [(branch_in, branch_ref), (walker_ref, source), (field_ref, field_in), (trial_ref, trial.at[mine]), (chol_ref, chol)]
    own = [pltpu.make_async_copy(src, dst, own_sem.at[k]) for k, (src, dst) in enumerate(loads)]
    for copy in own:
        copy.start()
    barrier = pltpu.get_barrier_semaphore()
    greeted = 0
    if local < slots:
        for step in range(1, walks):
            pl.semaphore_signal(barrier, inc=1, device_id={"walk": partner(walk, step, walks)}, device_id_type=MESH)
            greeted += 1
    for step in range(1, slabs):
        pl.semaphore_signal(barrier, inc=1, device_id={"slab": slab_peer(step)}, device_id_type=MESH)
        greeted += 1
    for step in range(1, cores):
        pl.semaphore_signal(barrier, inc=1, device_id={"row": core_peer(step)}, device_id_type=MESH)
        greeted += 1

    def sender(w, k):
        return lax.div(branch_ref[w * slots + k], slots)

    def kth(w, origin, values):
        picks, count = [jnp.int32(0)] * local, jnp.int32(0)
        for k in range(slots):
            hit = sender(w, k) == origin
            picks = [jnp.where(hit & (count == place), values(k), pick) for place, pick in enumerate(picks)]
            count = count + jnp.where(hit, 1, 0)
        return picks

    for copy in own[:3]:
        copy.wait()
    slot_of = list(range(slots))
    if local < slots:
        origins = []
        for step in range(walks):
            target = partner(walk, step, walks)
            picks = kth(target, walk, lambda k: lax.rem(branch_ref[target * slots + k], slots))
            for place, pick in enumerate(picks):
                if step == 0:
                    raw[place, mine] = source[pick]
                else:
                    outgoing[step * local + place] = source[pick]
            origin = target if walks & (walks - 1) == 0 else (walk + walks - step) % walks
            origins.append(origin)
            for place, pick in enumerate(kth(walk, origin, lambda k: k)):
                i = step * local + place
                field_out[i : i + 1, :] = field_in[pl.ds(pick, 1), :]
        for j in range(slots):
            origin, rank, step_of = sender(walk, j), jnp.int32(0), jnp.int32(0)
            for k in range(j):
                rank = rank + jnp.where(sender(walk, k) == origin, 1, 0)
            for step in range(walks):
                step_of = jnp.where(origins[step] == origin, step, step_of)
            slot_of[j] = jnp.minimum(step_of * local + rank, slots - 1)
    else:
        for i in range(slots):
            raw[i, mine] = source[i]
        field_out[...] = field_in[...]
    field[mine] = field_out[...]
    for copy in own[3:]:
        copy.wait()
    pl.semaphore_wait(barrier, greeted)

    def remote(src, dst, send, recv, target):
        return pltpu.make_async_remote_copy(
            src_ref=src, dst_ref=dst, send_sem=send, recv_sem=recv, device_id=target, device_id_type=MESH
        )

    def z_copy(i, step):
        return remote(outgoing.at[i], raw.at[i, mine], z_send.at[i], z_recv.at[i], {"walk": partner(walk, step, walks)})

    def x_copy(i, step):
        return remote(raw.at[i, mine], raw.at[i, mine], x_send.at[step, i], x_recv.at[step, i], {"slab": slab_peer(step)})

    def c_copy(i, hop, step):
        q = slab_source(hop) * cores + core
        return remote(raw.at[i, q], raw.at[i, q], c_send.at[hop, step, i], c_recv.at[hop, step, i], {"row": core_peer(step)})

    def small(src, buf, xs, xr, cs, cr):
        def x(step):
            return remote(src, buf.at[mine], xs.at[step], xr.at[step], {"slab": slab_peer(step)})

        def c(hop, step):
            q = slab_source(hop) * cores + core
            block = src if hop == 0 else buf.at[q]
            return remote(block, buf.at[q], cs.at[hop, step], cr.at[hop, step], {"row": core_peer(step)})

        return x, c

    for i in range(local, slots):
        z_copy(i, i // local).start()
    pairs = [
        small(trial_ref, trial, tx_send, tx_recv, tc_send, tc_recv),
        small(field_out, field, fx_send, fx_recv, fc_send, fc_recv),
    ]
    for x, c in pairs:
        for step in range(1, slabs):
            x(step).start()
        for step in range(1, cores):
            c(0, step).start()
    def spread(i):
        for step in range(1, slabs):
            x_copy(i, step).start()
        for step in range(1, cores):
            c_copy(i, 0, step).start()

    def relay(i):
        for hop in range(1, slabs):
            x_copy(i, hop).wait_recv()
            for step in range(1, cores):
                c_copy(i, hop, step).start()

    def compute(i):
        for hop in range(slabs):
            for step in range(1, cores):
                c_copy(i, hop, step).wait_recv()
        for q in range(slabs * cores):
            column = jnp.transpose(field[q])
            lane = lax.broadcasted_iota(jnp.int32, column.shape, 1)
            scale = jnp.sum(jnp.where(lane == i, column, 0.0), axis=1, keepdims=True)
            prop[q * rows : (q + 1) * rows, :] = (raw[i, q].astype(jnp.float32) * scale).astype(jnp.bfloat16)
        @pl.when(lax.rem(i, cores) == core)
        def _():
            total = dot(trial_t[0], prop[0:rows, :])
            for q in range(1, slabs * cores):
                total += dot(trial_t[q], prop[q * rows : (q + 1) * rows, :])
            inter[i // cores] = total

        half[i] = dot(chol[...], prop[...]).astype(jnp.bfloat16)

    for i in range(local):
        spread(i)
    for x, c in pairs:
        for hop in range(1, slabs):
            x(hop).wait_recv()
            for step in range(1, cores):
                c(hop, step).start()
    for x, c in pairs:
        for hop in range(slabs):
            for step in range(1, cores):
                c(hop, step).wait_recv()

    for q in range(slabs * cores):
        trial_t[q] = jnp.transpose(trial[q].astype(jnp.float32)).astype(jnp.bfloat16)
    share = slots // cores
    line = lax.broadcasted_iota(jnp.int32, (electrons, electrons), 0)
    diagonal = line == lax.broadcasted_iota(jnp.int32, (electrons, electrons), 1)

    def i_copy(i, step):
        place = inverse.at[i]
        return remote(place, place, i_send.at[i // cores, step], i_recv.at[i // cores, step], {"row": core_peer(step)})

    def first_guess(n):
        matrix = inter[n]
        sizes_of = jnp.abs(matrix)
        column_max = jnp.max(jnp.sum(sizes_of, axis=0, keepdims=True), axis=1, keepdims=True)
        row_max = jnp.max(jnp.sum(sizes_of, axis=1, keepdims=True), axis=0, keepdims=True)
        start = jnp.transpose(matrix) / (column_max * row_max)
        stack[0:electrons, :] = start
        stack[electrons:, :] = dot3(matrix, start)

    def finish(i):
        @pl.when(lax.rem(i, cores) != core)
        def _():
            i_copy(i, lax.rem(core + cores - lax.rem(i, cores), cores)).wait_recv()

        contracted = dot(half[i], inverse[i])
        for g in range(vectors):
            block = contracted[g * electrons : (g + 1) * electrons, :]
            traces[i, g : g + 1, :] = jnp.sum(jnp.where(diagonal, block, 0.0), axis=0, keepdims=True)
            squares[i, g : g + 1, :] = jnp.sum(block * jnp.transpose(block), axis=0, keepdims=True)

    ready = cores + 1

    @pl.loop(0, slots + ready + cores + 1)
    def _(i):
        @pl.when((i >= local) & (i < slots))
        def _():
            z_copy(i, 0).wait_recv()
            spread(i)

        @pl.when((i > 1) & (i < slots + 2))
        def _():
            compute(i - 2)

        @pl.when((i > 0) & (i <= slots))
        def _():
            relay(i - 1)

        for part in range(cores):

            @pl.when((i >= ready) & (i < slots + ready) & (lax.rem(i + cores - 1, cores) == part))
            def _():
                n = (i - ready) // cores
                if part == 0:
                    first_guess(n)

                first, middle, last = ITERS * part // cores, EARLY, ITERS * (part + 1) // cores

                @pl.loop(first, max(first, min(middle, last)))
                def _(iteration):
                    both = stack[...]
                    low = both.astype(jnp.bfloat16)
                    stack[...] = 2.0 * both - dot(low, low[electrons:, :])

                @pl.loop(min(last, max(middle, first)), last)
                def _(iteration):
                    both = stack[...]
                    stack[...] = 2.0 * both - dot3(both, both[electrons:, :])

                if part == cores - 1:
                    inverse[n * cores + core] = stack[0:electrons, :].astype(jnp.bfloat16)
                    for step in range(1, cores):
                        i_copy(n * cores + core, step).start()

        @pl.when(i > ready + cores)
        def _():
            finish(i - ready - cores - 1)


    column = lax.broadcasted_iota(jnp.int32, bias_ref.shape, 1)
    for terms, rows_of, result in ((traces, bias_rows, bias_ref), (squares, exch_rows, exch_ref)):
        for j in range(slots):
            block = terms[slot_of[j]]
            for g in range(vectors):
                rows_of[g, j : j + 1, :] = block[g : g + 1, :]
        total = jnp.zeros(result.shape, jnp.float32)
        for g in range(vectors):
            total = jnp.where(column == g, jnp.sum(rows_of[g], axis=1, keepdims=True), total)
        result[...] = total

    for i in range(local, slots):
        z_copy(i, i // local).wait_send()

    @pl.loop(0, slots)
    def _(i):
        for step in range(1, slabs):
            x_copy(i, step).wait_send()
        for hop in range(slabs):
            for step in range(1, cores):
                c_copy(i, hop, step).wait_send()

    for x, c in pairs:
        for step in range(1, slabs):
            x(step).wait_send()
        for hop in range(slabs):
            for step in range(1, cores):
                c(hop, step).wait_send()
    for n in range(share):
        for step in range(1, cores):
            i_copy(n * cores + core, step).wait_send()


def xor(a, b, size):
    result, bit = 0, 1
    while bit < size:
        left, right = lax.rem(lax.div(a, bit), 2), lax.rem(lax.div(b, bit), 2)
        result += bit * lax.rem(left + right, 2)
        bit *= 2
    return result


def origin_kernel(
    sizes, branch_in, walker_ref, trial_ref, chol_ref, field_ref, bias_ref, exch_ref, living_ref,
    branch_ref, source, fields, chosen, outgoing, prop, trial, trial_t, chol, stack, green, lanes, sums, arrived,
    own_sem, f_send, f_recv, t_send, t_recv, tx_send, tp_sem, cx_send, cd_send, c_send, c_recv, cp_sem, w_send, w_recv, o_send, o_recv,
):
    walks, slabs, cores, slots, local, items = sizes
    walk, slab, core = lax.axis_index("walk"), lax.axis_index("slab"), lax.axis_index("row")
    rows, electrons = trial_ref.shape
    shards = slabs * cores
    vectors = chol_ref.shape[0] // electrons
    mine = slab * cores + core
    other_slab, other_core = 1 - slab, 1 - core
    across, beside, diagonal_q = other_slab * cores + core, slab * cores + other_core, other_slab * cores + other_core
    below, above = walk > 0, walk < walks - 1
    steps = ((1, 1), (1, 0), (0, 1))

    loads = [(branch_in, branch_ref), (walker_ref, source), (field_ref, fields.at[walk]), (trial_ref, trial.at[mine]), (chol_ref, chol.at[mine])]
    own = [pltpu.make_async_copy(src, dst, own_sem.at[k]) for k, (src, dst) in enumerate(loads)]
    for copy in own:
        copy.start()
    barrier = pltpu.get_barrier_semaphore()

    def greet(target):
        pl.semaphore_signal(barrier, inc=1, device_id=target, device_id_type=MESH)

    def place_of(dx, dc):
        return {"slab": lax.rem(slab + dx, slabs), "row": lax.rem(core + dc, cores)}

    for dx, dc in steps:
        greet(place_of(dx, dc))

    @pl.when(below)
    def _():
        greet({"walk": walk - 1})

    @pl.when(above)
    def _():
        greet({"walk": walk + 1})

    for copy in own:
        copy.wait()
    pl.semaphore_wait(barrier, len(steps) + jnp.where(below, 1, 0) + jnp.where(above, 1, 0))

    def remote(src, dst, send, recv, target):
        return pltpu.make_async_remote_copy(
            src_ref=src, dst_ref=dst, send_sem=send, recv_sem=recv, device_id=target, device_id_type=MESH
        )

    def field_copy(o, way):
        return remote(fields.at[o], fields.at[o], f_send.at[way, o], f_recv.at[o], {"walk": walk + 1 - 2 * way})

    half = lax.rem(walk, 2)

    def trial_view(q, part):
        size = rows // 2
        return trial.at[q, pl.ds(pl.multiple_of(part * size, size), size)]

    def chol_rows(o, p):
        size = chol_ref.shape[0] // (walks * PIECES)
        return pl.ds(pl.multiple_of((o * PIECES + p) * size, size), size)

    def trial_next(part):
        view = trial_view(across, part)
        return remote(view, view, t_send.at[0], t_recv.at[0, part], {"walk": walk + 1 - 2 * half})

    def trial_relay(part):
        view = trial_view(across, part)
        return remote(view, view, t_send.at[1 + part], t_recv.at[1, part], {"row": other_core})

    def trial_beside(part):
        view = trial_view(diagonal_q, part)
        return remote(view, view, t_send.at[1 + part], t_recv.at[1, part], {"row": other_core})

    def chol_copy(o, p, way):
        view = chol.at[across, chol_rows(o, p)]
        if way == 2:
            return remote(view, view, c_send.at[2, o, p], c_recv.at[1, o, p], {"row": other_core})
        return remote(view, view, c_send.at[way, o, p], c_recv.at[0, o, p], {"walk": walk + 1 - 2 * way})

    def chol_beside(o, p):
        view = chol.at[diagonal_q, chol_rows(o, p)]
        return remote(view, view, c_send.at[2, o, p], c_recv.at[1, o, p], {"row": other_core})

    def trial_across():
        view = trial_view(mine, half)
        return remote(view, view, tx_send.at[0], t_recv.at[0, half], {"slab": other_slab})

    def chol_across(p):
        return remote(chol.at[mine, chol_rows(walk, p)], chol.at[mine, chol_rows(walk, p)], cx_send.at[p], c_recv.at[0, walk, p], {"slab": other_slab})

    trial_whole = remote(trial.at[mine], trial.at[mine], tp_sem.at[0], tp_sem.at[1], {"row": other_core})
    chol_whole = remote(chol.at[mine], chol.at[mine], cp_sem.at[0], cp_sem.at[1], {"row": other_core})

    def both_ways(action):
        @pl.when(above)
        def _():
            action(0)

        @pl.when(below)
        def _():
            action(1)

    def hop(k, arrive, forward):
        @pl.when(walk >= k)
        def _():
            arrive(walk - k)
            if k < walks - 1:
                pl.when(above)(lambda: forward(walk - k, 0))

        @pl.when(walk + k < walks)
        def _():
            arrive(walk + k)
            if k < walks - 1:
                pl.when(below)(lambda: forward(walk + k, 1))

    def field_hop(k):
        hop(k, lambda o: field_copy(o, 0).wait_recv(), lambda o, way: field_copy(o, way).start())

    def chol_hop(k, p):
        def arrive(o):
            chol_copy(o, p, 0).wait_recv()
            chol_copy(o, p, 2).start()

        def forward(o, way):
            if k < walks - 2 or p < PIECES - DIRECT:
                chol_copy(o, p, way).start()

        hop(k, arrive, forward)

    def chol_direct(p, action):
        if walks > 2:
            far = walks - 1 - walk
            view = chol.at[mine, chol_rows(far, p)]
            copy = remote(view, view, cd_send.at[p], c_recv.at[0, far, p], {"slab": other_slab})
            pl.when(jnp.logical_not(above & below))(lambda: action(copy))

    def chol_start(p):
        chol_copy(walk, p, 0).wait_recv()
        both_ways(lambda way: chol_copy(walk, p, way).start())
        chol_copy(walk, p, 2).start()

    def sender(w, k):
        return lax.div(branch_ref[w * slots + k], slots)

    def step_of(number):
        order = lax.div(number, shards) * cores + lax.rem(number, cores)
        return walks - 1 - order, lax.div(lax.rem(number, shards), cores)

    def item_target(number):
        return xor(walk, step_of(number)[0], walks)

    def locate(number):
        target, place = item_target(number), step_of(number)[1]
        pick, spot, count = jnp.int32(0), jnp.int32(0), jnp.int32(0)
        for k in range(slots):
            hit = sender(target, k) == walk
            here = hit & (count == place)
            pick = jnp.where(here, lax.rem(branch_ref[target * slots + k], slots), pick)
            spot = jnp.where(here, k, spot)
            count = count + jnp.where(hit, 1, 0)
        return target, pick, spot

    slot_line = lax.broadcasted_iota(jnp.int32, (slots, rows), 0)
    my_rows = pl.ds(pl.multiple_of(mine * rows, rows), rows)

    def w_copy(r, dx, row):
        place = {"slab": lax.rem(slab + dx, slabs), "row": row}
        return remote(outgoing.at[r, dx * cores + row], prop.at[r, my_rows], w_send.at[r, dx * cores + row], w_recv.at[r, mine], place)

    def send_group(r, row):
        found = []
        for dx in range(slabs):
            target, pick, spot = locate(r * shards + lax.rem(slab + dx, slabs) * cores + row)
            found.append(pick)
            chosen[dx : dx + 1, :] = jnp.sum(jnp.where(slot_line == spot, fields[target], 0.0), axis=0, keepdims=True)
        scales = jnp.transpose(chosen[...])
        for dx in reversed(range(slabs)):
            block = (source[found[dx]].astype(jnp.float32) * scales[:, dx : dx + 1]).astype(jnp.bfloat16)
            outgoing[r, dx * cores + row] = block
            if dx:
                w_copy(r, dx, row).start()
            else:
                pl.when(core != row)(w_copy(r, dx, row).start)

                @pl.when(core == row)
                def _():
                    prop[r, my_rows] = outgoing[r, row]

    both_ways(lambda way: field_copy(walk, way).start())
    chol_across(0).start()
    trial_across().start()
    for p in range(1, PIECES):
        chol_across(p).start()
    trial_whole.start()
    chol_whole.start()

    last = walks - 1
    field_hop(1)
    chol_start(0)
    for k in range(2, last):
        field_hop(k)
    trial_next(half).wait_recv()
    trial_next(half).start()
    trial_relay(half).start()
    send_group(0, 1)
    chol_start(1)
    if last > 1:
        field_hop(last)
    send_group(0, 0)
    send_group(1, 0)
    send_group(1, 1)
    for p in range(PIECES - DIRECT, PIECES):
        chol_direct(p, lambda copy: copy.start())
    if last > 2:
        chol_hop(1, 0)
    chol_start(2)
    trial_next(1 - half).wait_recv()
    trial_relay(1 - half).start()
    chol_start(3)
    for k in range(1, last - 1):
        for p in range(1 if k == 1 else 0, PIECES):
            chol_hop(k, p)
    for part in range(2):
        trial_beside(part).wait_recv()
    trial_whole.wait_recv()
    for q in range(shards):
        trial_t[:, q * rows : (q + 1) * rows] = jnp.transpose(trial[q].astype(jnp.float32)).astype(jnp.bfloat16)

    line = lax.broadcasted_iota(jnp.int32, (electrons, electrons), 0)
    on_diagonal = line == lax.broadcasted_iota(jnp.int32, (electrons, electrons), 1)

    def invert(r, hooks):
        for q in (beside, across, diagonal_q):
            part = pl.ds(pl.multiple_of(q * rows, rows), rows)
            remote(prop.at[r, part], prop.at[r, part], w_send.at[r, 0], w_recv.at[r, q], {"row": other_core}).wait_recv()
        hooks[0]()
        matrix = dot(trial_t[...], prop[r])
        sizes_of = jnp.abs(matrix)
        column_max = jnp.max(jnp.sum(sizes_of, axis=0, keepdims=True), axis=1, keepdims=True)
        row_max = jnp.max(jnp.sum(sizes_of, axis=1, keepdims=True), axis=0, keepdims=True)
        start = jnp.transpose(matrix) / (column_max * row_max)
        stack[0:electrons, :] = start
        stack[electrons:, :] = dot3(matrix, start)

        hooks[1]()

        @pl.loop(0, PASSES)
        def _(iteration):
            both = stack[...]
            low = both.astype(jnp.bfloat16)
            stack[...] = 2.0 * both - dot(low, low[electrons:, :])

        hooks[2]()

        for first, end, hook in ((PASSES, LATER, 3), (LATER, ITERS, 4)):

            @pl.loop(first, end)
            def _(iteration):
                both = stack[...]
                stack[...] = 2.0 * both - dot3(both, both[electrons:, :])

            hooks[hook]()

        green[r] = dot(prop[r], stack[0:electrons, :].astype(jnp.bfloat16)).astype(jnp.bfloat16)

    blocks = (mine, beside, across, diagonal_q)

    def contract(r, n):
        for g in range(vectors):
            block = dot(chol[blocks[n], g * electrons : (g + 1) * electrons, :], green[r])
            number = n * vectors + g
            lanes[r, 0, number : number + 1, :] = jnp.sum(jnp.where(on_diagonal, block, 0.0), axis=0, keepdims=True)
            lanes[r, 1, number : number + 1, :] = jnp.sum(block * jnp.transpose(block), axis=0, keepdims=True)

    def o_copy(r, dx, dc):
        number = r * shards + mine
        target = item_target(number)
        device = {"walk": target, **place_of(dx, dc)}
        return target, remote(sums.at[r], arrived.at[number], o_send.at[r, dx * cores + dc], o_recv.at[number], device)

    def publish(r):
        for kind in range(2):
            total = jnp.sum(lanes[r, kind], axis=1, keepdims=True)
            sums[r, kind] = jnp.broadcast_to(total, sums.shape[2:])
        for dx, dc in steps:
            o_copy(r, dx, dc)[1].start()
        target, copy = o_copy(r, 0, 0)
        pl.when(target != walk)(copy.start)

        @pl.when(target == walk)
        def _():
            arrived[r * shards + mine] = sums[r]

    def hooks_of(k, pieces):
        def relay(group):
            def run():
                if k > 0:
                    for p in group:
                        chol_hop(k, p)

            return run

        return [relay(group) for group in pieces]

    invert(0, hooks_of(last - 1 if last > 2 else 0, HOOKS[0]))
    contract(0, 0)
    chol_whole.wait_recv()
    contract(0, 1)
    for r in range(1, items):
        invert(r, hooks_of(last, HOOKS[1]) if r == 1 else hooks_of(0, HOOKS[1]))
    contract(0, 2)

    @pl.loop(0, walks)
    def _(o):
        @pl.loop(0, PIECES)
        def _(p):
            chol_beside(o, p).wait_recv()

    contract(0, 3)
    publish(0)
    for r in range(1, items):
        for n in range(shards):
            contract(r, n)
        publish(r)

    def number_of(j):
        origin, rank = sender(walk, j), jnp.int32(0)
        for k in range(j):
            rank = rank + jnp.where(sender(walk, k) == origin, 1, 0)
        step = jnp.int32(0)
        for s in range(walks):
            step = jnp.where(xor(walk, s, walks) == origin, s, step)
        order = walks - 1 - step
        number = lax.div(order, cores) * shards + lax.min(rank, local - 1) * cores + lax.rem(order, cores)
        return jnp.clip(number, 0, slots - 1)

    numbers = [number_of(j) for j in range(slots)]

    for number in range(slots):
        target = item_target(number)
        from_me = (target == walk) & (mine == number % shards)

        @pl.when(jnp.logical_not(from_me))
        def _():
            remote(sums.at[0], arrived.at[number], o_send.at[0, 0], o_recv.at[number], {"row": other_core}).wait_recv()

    column = lax.broadcasted_iota(jnp.int32, bias_ref.shape, 1)
    for kind, result in enumerate((bias_ref, exch_ref)):
        total = jnp.zeros(result.shape, jnp.float32)
        for j in range(slots):
            q = lax.rem(numbers[j], shards)
            dx, dc = lax.rem(lax.div(q, cores) + slab, slabs), lax.rem(lax.rem(q, cores) + core, cores)
            first = (dx * cores + dc) * vectors
            total = jnp.where(column == j, arrived[numbers[j], kind, pl.ds(first, vectors), 0:slots], total)
        result[...] = total
    living_ref[...] = jnp.where(column < branch_ref[walks * slots], 1.0, 0.0)

    trial_across().wait_send()
    trial_next(half).wait_send()
    for part in range(2):
        trial_relay(part).wait_send()
    trial_whole.wait_send()
    for p in range(PIECES - DIRECT, PIECES):
        chol_direct(p, lambda copy: copy.wait_send())
    chol_whole.wait_send()
    for p in range(PIECES):
        chol_across(p).wait_send()

    @pl.loop(0, walks)
    def _(o):
        def sent(way):
            field_copy(o, way).wait_send()

        pl.when(above & (o <= walk))(lambda: sent(0))
        pl.when(below & (o >= walk))(lambda: sent(1))

        @pl.loop(0, PIECES)
        def _(p):
            chol_copy(o, p, 2).wait_send()
            chained = (p < PIECES - DIRECT) | (walks < 3)
            upward, downward = (o > 0) | (walk < walks - 2), (o < walks - 1) | (walk > 1)
            pl.when(above & (o <= walk) & (chained | upward))(lambda: chol_copy(o, p, 0).wait_send())
            pl.when(below & (o >= walk) & (chained | downward))(lambda: chol_copy(o, p, 1).wait_send())

    for r in range(items):
        for dx, dc in steps:
            o_copy(r, dx, dc)[1].wait_send()
        target, copy = o_copy(r, 0, 0)
        pl.when(target != walk)(copy.wait_send)
        for row in range(cores):
            for dx in range(1, slabs):
                w_copy(r, dx, row).wait_send()
            pl.when(core != row)(w_copy(r, 0, row).wait_send)


def gathered(walkers, trial_orbitals, cholesky, branches, field):
    walks, slabs, cores = lax.axis_size("walk"), lax.axis_size("slab"), lax.axis_size("row")
    walk = lax.axis_index("walk")
    per_device, rows, electrons = walkers.shape
    vectors = cholesky.shape[0]
    capacity = (per_device + walks - 1) // walks
    local = capacity if walks * capacity == per_device else per_device
    if local == per_device:
        sender = branches.reshape(walks, per_device) // per_device
        local_index = branches.reshape(walks, per_device) % per_device
        places = jnp.arange(per_device, dtype=jnp.int32)
        same_sender = sender[:, :, None] == sender[:, None, :]
        rank = jnp.sum(same_sender & (places[None, :] < places[:, None])[None], axis=2)
        ranks = jnp.arange(capacity, dtype=jnp.int32)[None, :, None]
        wanted = (sender[:, None, :] == walk) & (rank[:, None, :] == ranks)
        chosen = jnp.sum(jnp.where(wanted, local_index[:, None, :], 0), axis=2)
        outgoing = jnp.take(walkers, chosen.reshape(-1), axis=0, mode="clip")
        outgoing = outgoing.reshape(walks, capacity, rows, electrons)
        arrived = lax.all_to_all(outgoing, "walk", split_axis=0, concat_axis=0, tiled=True)
        arrived = arrived.reshape(walks * capacity, rows, electrons)
        my_sender = lax.dynamic_index_in_dim(sender, walk, 0, keepdims=False)
        my_rank = lax.dynamic_index_in_dim(rank, walk, 0, keepdims=False)
        walkers = jnp.take(arrived, my_sender * capacity + my_rank, axis=0, mode="clip")
    shards = slabs * cores
    share = per_device // cores
    dma = pltpu.SemaphoreType.DMA
    vmem = pl.BlockSpec(memory_space=pltpu.VMEM)
    bias, exchange = pl.pallas_call(
        functools.partial(kernel, (walks, slabs, cores, per_device, local)),
        out_shape=[jax.ShapeDtypeStruct((per_device, vectors), jnp.float32)] * 2,
        in_specs=[pl.BlockSpec(memory_space=pl.ANY)] * 5,
        out_specs=[vmem] * 2,
        scratch_shapes=[
            pltpu.SMEM(branches.shape, jnp.int32),
            pltpu.VMEM((shards, electrons, rows), jnp.bfloat16),
            pltpu.VMEM((per_device, rows, electrons), jnp.bfloat16),
            pltpu.VMEM((per_device, rows, electrons), jnp.bfloat16),
            pltpu.VMEM((per_device, rows), jnp.float32),
            pltpu.VMEM((per_device, rows), jnp.float32),
            pltpu.VMEM((per_device, vectors, electrons), jnp.float32),
            pltpu.VMEM((per_device, vectors, electrons), jnp.float32),
            pltpu.VMEM((vectors, per_device, electrons), jnp.float32),
            pltpu.VMEM((vectors, per_device, electrons), jnp.float32),
            pltpu.VMEM((per_device, shards, rows, electrons), jnp.bfloat16),
            pltpu.VMEM((shards, rows, electrons), jnp.bfloat16),
            pltpu.VMEM((shards, per_device, rows), jnp.float32),
            pltpu.VMEM((vectors * electrons, shards * rows), jnp.bfloat16),
            pltpu.VMEM((shards * rows, electrons), jnp.bfloat16),
            pltpu.VMEM((per_device, vectors * electrons, electrons), jnp.bfloat16),
            pltpu.VMEM((share, electrons, electrons), jnp.float32),
            pltpu.VMEM((2 * electrons, electrons), jnp.float32),
            pltpu.VMEM((per_device, electrons, electrons), jnp.bfloat16),
            dma((per_device,)), dma((per_device,)),
            dma((slabs, per_device)), dma((slabs, per_device)),
            dma((slabs, cores, per_device)), dma((slabs, cores, per_device)),
            dma((share, cores)), dma((share, cores)),
            dma((slabs,)), dma((slabs,)), dma((slabs, cores)), dma((slabs, cores)),
            dma((slabs,)), dma((slabs,)), dma((slabs, cores)), dma((slabs, cores)),
            dma((5,)),
        ],
        compiler_params=pltpu.CompilerParams(
            collective_id=0, has_side_effects=True, vmem_limit_bytes=63 * 1024 * 1024
        ),
    )(branches, walkers, trial_orbitals, cholesky.reshape(vectors * electrons, shards * rows), field)
    return bias, exchange


def at_origin(walkers, trial_orbitals, cholesky, branches, counts, field):
    walks, slabs, cores = lax.axis_size("walk"), lax.axis_size("slab"), lax.axis_size("row")
    slots, rows, electrons = walkers.shape
    vectors = cholesky.shape[0]
    shards, local = slabs * cores, slots // walks
    items, lines, columns = slots // shards, vectors * electrons, shards * rows
    dma = pltpu.SemaphoreType.DMA
    vmem = pl.BlockSpec(memory_space=pltpu.VMEM)
    numbers = jnp.concatenate([branches, counts])
    bias, exchange, living = pl.pallas_call(
        functools.partial(origin_kernel, (walks, slabs, cores, slots, local, items)),
        out_shape=[jax.ShapeDtypeStruct((vectors, slots), jnp.float32)] * 3,
        in_specs=[pl.BlockSpec(memory_space=pltpu.HBM)] * 5,
        out_specs=[vmem] * 3,
        scratch_shapes=[
            pltpu.SMEM(numbers.shape, jnp.int32),
            pltpu.VMEM((slots, rows, electrons), jnp.bfloat16),
            pltpu.VMEM((walks, slots, rows), jnp.float32),
            pltpu.VMEM((slots, rows), jnp.float32),
            pltpu.VMEM((items, shards, rows, electrons), jnp.bfloat16),
            pltpu.VMEM((items, columns, electrons), jnp.bfloat16),
            pltpu.VMEM((shards, rows, electrons), jnp.bfloat16),
            pltpu.VMEM((electrons, columns), jnp.bfloat16),
            pltpu.VMEM((shards, lines, columns), jnp.bfloat16),
            pltpu.VMEM((2 * electrons, electrons), jnp.float32),
            pltpu.VMEM((items, columns, electrons), jnp.bfloat16),
            pltpu.VMEM((items, 2, shards * vectors, electrons), jnp.float32),
            pltpu.VMEM((items, 2, shards * vectors, 128), jnp.float32),
            pltpu.VMEM((slots, 2, shards * vectors, 128), jnp.float32),
            dma((5,)),
            dma((2, walks)), dma((walks,)),
            dma((3,)), dma((2, 2)), dma((2,)), dma((2,)),
            dma((PIECES,)), dma((PIECES,)), dma((3, walks, PIECES)), dma((2, walks, PIECES)), dma((2,)),
            dma((items, shards)), dma((items, shards)),
            dma((items, shards)), dma((slots,)),
        ],
        compiler_params=pltpu.CompilerParams(
            collective_id=0, has_side_effects=True, vmem_limit_bytes=55216 * 1024
        ),
    )(numbers, walkers, trial_orbitals, cholesky.reshape(lines, columns), field)
    return (bias * living).T, (-0.5 * exchange * living).T


def on_device(walkers, trial_orbitals, cholesky, branches, counts, field):
    walks, slabs, cores = lax.axis_size("walk"), lax.axis_size("slab"), lax.axis_size("row")
    slots, rows, electrons = walkers.shape
    lines = cholesky.shape[0] * electrons
    even = walks & (walks - 1) == 0 and slots % walks == 0 and slots % (slabs * cores) == 0
    whole = lines % (walks * PIECES * 16) == 0 and rows % 32 == 0 and walks > 2
    if slabs == cores == 2 and slots == 2 * walks and PIECES == 4 and even and whole:
        return at_origin(walkers, trial_orbitals, cholesky, branches, counts, field)
    bias, exchange = gathered(walkers, trial_orbitals, cholesky, branches, field)
    living = (jnp.arange(slots, dtype=jnp.int32) < counts[0]).astype(jnp.float32)[:, None]
    return bias * living, -0.5 * exchange * living


def solution(mesh):
    return jax.shard_map(
        on_device,
        mesh=mesh,
        in_specs=(
            P(("parts", "walk"), ("slab", "row"), None),
            P(("parts", "slab", "row"), None),
            P(("parts", "slab", "row"), None, None),
            P("parts"),
            P(("parts", "walk")),
            P(("parts", "walk"), ("slab", "row")),
        ),
        out_specs=(P(("parts", "walk"), ("slab", "row")), P(("parts", "walk"), ("slab", "row"))),
        check_vma=False,
    )
```

```python
import functools

import jax
import jax.numpy as jnp
from jax import lax
from jax.experimental import pallas as pl
from jax.experimental.pallas import tpu as pltpu
from jax.sharding import PartitionSpec as P

ITERS = 10
EARLY = 4
PASSES = 7
PIECES = 4
DIRECT = 3
LATER = 8
HOOKS = (((), (), (0,), (1,), (2, 3)), ((), (), (), (), (0, 1, 2, 3)))
MESH = pl.DeviceIdType.MESH


def split(x):
    high = x.astype(jnp.bfloat16)
    low = (x - high.astype(jnp.float32)).astype(jnp.bfloat16)
    return high, low


def dot(a, b):
    return jnp.dot(a, b, preferred_element_type=jnp.float32)


def dot3(a, b):
    ah, al = split(a)
    bh, bl = split(b)
    return dot(ah, bh) + (dot(ah, bl) + dot(al, bh))


def partner(position, step, size):
    if size & (size - 1):
        return (position + step) % size
    result, bit = 0, 1
    while bit < size:
        digit = (position // bit) % 2
        result += bit * (1 - digit if step & bit else digit)
        bit *= 2
    return result


def kernel(
    sizes, branch_in, walker_ref, trial_ref, chol_ref, field_ref, bias_ref, exch_ref,
    branch_ref, trial_t, source, outgoing, field_in, field_out, traces, squares, bias_rows, exch_rows, raw, trial, field, chol, prop, half, inter, stack, inverse,
    z_send, z_recv, x_send, x_recv, c_send, c_recv, i_send, i_recv,
    tx_send, tx_recv, tc_send, tc_recv, fx_send, fx_recv, fc_send, fc_recv, own_sem,
):
    walks, slabs, cores, slots, local = sizes
    walk, slab, core = lax.axis_index("walk"), lax.axis_index("slab"), lax.axis_index("row")
    rows, electrons = trial_ref.shape
    vectors = chol_ref.shape[0] // electrons
    mine = slab * cores + core

    def slab_peer(step):
        return lax.rem(slab + step, slabs)

    def core_peer(step):
        return lax.rem(core + step, cores)

    def slab_source(step):
        return lax.rem(slab + slabs - step, slabs)

    def core_source(step):
        return lax.rem(core + cores - step, cores)

    loads = [(branch_in, branch_ref), (walker_ref, source), (field_ref, field_in), (trial_ref, trial.at[mine]), (chol_ref, chol)]
    own = [pltpu.make_async_copy(src, dst, own_sem.at[k]) for k, (src, dst) in enumerate(loads)]
    for copy in own:
        copy.start()
    barrier = pltpu.get_barrier_semaphore()
    greeted = 0
    if local < slots:
        for step in range(1, walks):
            pl.semaphore_signal(barrier, inc=1, device_id={"walk": partner(walk, step, walks)}, device_id_type=MESH)
            greeted += 1
    for step in range(1, slabs):
        pl.semaphore_signal(barrier, inc=1, device_id={"slab": slab_peer(step)}, device_id_type=MESH)
        greeted += 1
    for step in range(1, cores):
        pl.semaphore_signal(barrier, inc=1, device_id={"row": core_peer(step)}, device_id_type=MESH)
        greeted += 1

    def sender(w, k):
        return lax.div(branch_ref[w * slots + k], slots)

    def kth(w, origin, values):
        picks, count = [jnp.int32(0)] * local, jnp.int32(0)
        for k in range(slots):
            hit = sender(w, k) == origin
            picks = [jnp.where(hit & (count == place), values(k), pick) for place, pick in enumerate(picks)]
            count = count + jnp.where(hit, 1, 0)
        return picks

    for copy in own[:3]:
        copy.wait()
    slot_of = list(range(slots))
    if local < slots:
        origins = []
        for step in range(walks):
            target = partner(walk, step, walks)
            picks = kth(target, walk, lambda k: lax.rem(branch_ref[target * slots + k], slots))
            for place, pick in enumerate(picks):
                if step == 0:
                    raw[place, mine] = source[pick]
                else:
                    outgoing[step * local + place] = source[pick]
            origin = target if walks & (walks - 1) == 0 else (walk + walks - step) % walks
            origins.append(origin)
            for place, pick in enumerate(kth(walk, origin, lambda k: k)):
                i = step * local + place
                field_out[i : i + 1, :] = field_in[pl.ds(pick, 1), :]
        for j in range(slots):
            origin, rank, step_of = sender(walk, j), jnp.int32(0), jnp.int32(0)
            for k in range(j):
                rank = rank + jnp.where(sender(walk, k) == origin, 1, 0)
            for step in range(walks):
                step_of = jnp.where(origins[step] == origin, step, step_of)
            slot_of[j] = jnp.minimum(step_of * local + rank, slots - 1)
    else:
        for i in range(slots):
            raw[i, mine] = source[i]
        field_out[...] = field_in[...]
    field[mine] = field_out[...]
    for copy in own[3:]:
        copy.wait()
    pl.semaphore_wait(barrier, greeted)

    def remote(src, dst, send, recv, target):
        return pltpu.make_async_remote_copy(
            src_ref=src, dst_ref=dst, send_sem=send, recv_sem=recv, device_id=target, device_id_type=MESH
        )

    def z_copy(i, step):
        return remote(outgoing.at[i], raw.at[i, mine], z_send.at[i], z_recv.at[i], {"walk": partner(walk, step, walks)})

    def x_copy(i, step):
        return remote(raw.at[i, mine], raw.at[i, mine], x_send.at[step, i], x_recv.at[step, i], {"slab": slab_peer(step)})

    def c_copy(i, hop, step):
        q = slab_source(hop) * cores + core
        return remote(raw.at[i, q], raw.at[i, q], c_send.at[hop, step, i], c_recv.at[hop, step, i], {"row": core_peer(step)})

    def small(src, buf, xs, xr, cs, cr):
        def x(step):
            return remote(src, buf.at[mine], xs.at[step], xr.at[step], {"slab": slab_peer(step)})

        def c(hop, step):
            q = slab_source(hop) * cores + core
            block = src if hop == 0 else buf.at[q]
            return remote(block, buf.at[q], cs.at[hop, step], cr.at[hop, step], {"row": core_peer(step)})

        return x, c

    for i in range(local, slots):
        z_copy(i, i // local).start()
    pairs = [
        small(trial_ref, trial, tx_send, tx_recv, tc_send, tc_recv),
        small(field_out, field, fx_send, fx_recv, fc_send, fc_recv),
    ]
    for x, c in pairs:
        for step in range(1, slabs):
            x(step).start()
        for step in range(1, cores):
            c(0, step).start()
    def spread(i):
        for step in range(1, slabs):
            x_copy(i, step).start()
        for step in range(1, cores):
            c_copy(i, 0, step).start()

    def relay(i):
        for hop in range(1, slabs):
            x_copy(i, hop).wait_recv()
            for step in range(1, cores):
                c_copy(i, hop, step).start()

    def compute(i):
        for hop in range(slabs):
            for step in range(1, cores):
                c_copy(i, hop, step).wait_recv()
        for q in range(slabs * cores):
            column = jnp.transpose(field[q])
            lane = lax.broadcasted_iota(jnp.int32, column.shape, 1)
            scale = jnp.sum(jnp.where(lane == i, column, 0.0), axis=1, keepdims=True)
            prop[q * rows : (q + 1) * rows, :] = (raw[i, q].astype(jnp.float32) * scale).astype(jnp.bfloat16)
        @pl.when(lax.rem(i, cores) == core)
        def _():
            total = dot(trial_t[0], prop[0:rows, :])
            for q in range(1, slabs * cores):
                total += dot(trial_t[q], prop[q * rows : (q + 1) * rows, :])
            inter[i // cores] = total

        half[i] = dot(chol[...], prop[...]).astype(jnp.bfloat16)

    for i in range(local):
        spread(i)
    for x, c in pairs:
        for hop in range(1, slabs):
            x(hop).wait_recv()
            for step in range(1, cores):
                c(hop, step).start()
    for x, c in pairs:
        for hop in range(slabs):
            for step in range(1, cores):
                c(hop, step).wait_recv()

    for q in range(slabs * cores):
        trial_t[q] = jnp.transpose(trial[q].astype(jnp.float32)).astype(jnp.bfloat16)
    share = slots // cores
    line = lax.broadcasted_iota(jnp.int32, (electrons, electrons), 0)
    diagonal = line == lax.broadcasted_iota(jnp.int32, (electrons, electrons), 1)

    def i_copy(i, step):
        place = inverse.at[i]
        return remote(place, place, i_send.at[i // cores, step], i_recv.at[i // cores, step], {"row": core_peer(step)})

    def first_guess(n):
        matrix = inter[n]
        sizes_of = jnp.abs(matrix)
        column_max = jnp.max(jnp.sum(sizes_of, axis=0, keepdims=True), axis=1, keepdims=True)
        row_max = jnp.max(jnp.sum(sizes_of, axis=1, keepdims=True), axis=0, keepdims=True)
        start = jnp.transpose(matrix) / (column_max * row_max)
        stack[0:electrons, :] = start
        stack[electrons:, :] = dot3(matrix, start)

    def finish(i):
        @pl.when(lax.rem(i, cores) != core)
        def _():
            i_copy(i, lax.rem(core + cores - lax.rem(i, cores), cores)).wait_recv()

        contracted = dot(half[i], inverse[i])
        for g in range(vectors):
            block = contracted[g * electrons : (g + 1) * electrons, :]
            traces[i, g : g + 1, :] = jnp.sum(jnp.where(diagonal, block, 0.0), axis=0, keepdims=True)
            squares[i, g : g + 1, :] = jnp.sum(block * jnp.transpose(block), axis=0, keepdims=True)

    ready = cores + 1

    @pl.loop(0, slots + ready + cores + 1)
    def _(i):
        @pl.when((i >= local) & (i < slots))
        def _():
            z_copy(i, 0).wait_recv()
            spread(i)

        @pl.when((i > 1) & (i < slots + 2))
        def _():
            compute(i - 2)

        @pl.when((i > 0) & (i <= slots))
        def _():
            relay(i - 1)

        for part in range(cores):

            @pl.when((i >= ready) & (i < slots + ready) & (lax.rem(i + cores - 1, cores) == part))
            def _():
                n = (i - ready) // cores
                if part == 0:
                    first_guess(n)

                first, middle, last = ITERS * part // cores, EARLY, ITERS * (part + 1) // cores

                @pl.loop(first, max(first, min(middle, last)))
                def _(iteration):
                    both = stack[...]
                    low = both.astype(jnp.bfloat16)
                    stack[...] = 2.0 * both - dot(low, low[electrons:, :])

                @pl.loop(min(last, max(middle, first)), last)
                def _(iteration):
                    both = stack[...]
                    stack[...] = 2.0 * both - dot3(both, both[electrons:, :])

                if part == cores - 1:
                    inverse[n * cores + core] = stack[0:electrons, :].astype(jnp.bfloat16)
                    for step in range(1, cores):
                        i_copy(n * cores + core, step).start()

        @pl.when(i > ready + cores)
        def _():
            finish(i - ready - cores - 1)


    column = lax.broadcasted_iota(jnp.int32, bias_ref.shape, 1)
    for terms, rows_of, result in ((traces, bias_rows, bias_ref), (squares, exch_rows, exch_ref)):
        for j in range(slots):
            block = terms[slot_of[j]]
            for g in range(vectors):
                rows_of[g, j : j + 1, :] = block[g : g + 1, :]
        total = jnp.zeros(result.shape, jnp.float32)
        for g in range(vectors):
            total = jnp.where(column == g, jnp.sum(rows_of[g], axis=1, keepdims=True), total)
        result[...] = total

    for i in range(local, slots):
        z_copy(i, i // local).wait_send()

    @pl.loop(0, slots)
    def _(i):
        for step in range(1, slabs):
            x_copy(i, step).wait_send()
        for hop in range(slabs):
            for step in range(1, cores):
                c_copy(i, hop, step).wait_send()

    for x, c in pairs:
        for step in range(1, slabs):
            x(step).wait_send()
        for hop in range(slabs):
            for step in range(1, cores):
                c(hop, step).wait_send()
    for n in range(share):
        for step in range(1, cores):
            i_copy(n * cores + core, step).wait_send()


def xor(a, b, size):
    result, bit = 0, 1
    while bit < size:
        left, right = lax.rem(lax.div(a, bit), 2), lax.rem(lax.div(b, bit), 2)
        result += bit * lax.rem(left + right, 2)
        bit *= 2
    return result


def origin_kernel(
    sizes, branch_in, walker_ref, trial_ref, chol_ref, field_ref, bias_ref, exch_ref, living_ref,
    branch_ref, source, fields, chosen, outgoing, prop, trial, trial_t, chol, stack, green, lanes, sums, arrived,
    own_sem, f_send, f_recv, t_send, t_recv, tx_send, tp_sem, cx_send, cd_send, c_send, c_recv, cp_sem, w_send, w_recv, o_send, o_recv,
):
    walks, slabs, cores, slots, local, items = sizes
    walk, slab, core = lax.axis_index("walk"), lax.axis_index("slab"), lax.axis_index("row")
    rows, electrons = trial_ref.shape
    shards = slabs * cores
    vectors = chol_ref.shape[0] // electrons
    mine = slab * cores + core
    other_slab, other_core = 1 - slab, 1 - core
    across, beside, diagonal_q = other_slab * cores + core, slab * cores + other_core, other_slab * cores + other_core
    below, above = walk > 0, walk < walks - 1
    steps = ((1, 1), (1, 0), (0, 1))

    loads = [(branch_in, branch_ref), (walker_ref, source), (field_ref, fields.at[walk]), (trial_ref, trial.at[mine]), (chol_ref, chol.at[mine])]
    own = [pltpu.make_async_copy(src, dst, own_sem.at[k]) for k, (src, dst) in enumerate(loads)]
    for copy in own:
        copy.start()
    barrier = pltpu.get_barrier_semaphore()

    def greet(target):
        pl.semaphore_signal(barrier, inc=1, device_id=target, device_id_type=MESH)

    def place_of(dx, dc):
        return {"slab": lax.rem(slab + dx, slabs), "row": lax.rem(core + dc, cores)}

    for dx, dc in steps:
        greet(place_of(dx, dc))

    @pl.when(below)
    def _():
        greet({"walk": walk - 1})

    @pl.when(above)
    def _():
        greet({"walk": walk + 1})

    for copy in own:
        copy.wait()
    pl.semaphore_wait(barrier, len(steps) + jnp.where(below, 1, 0) + jnp.where(above, 1, 0))

    def remote(src, dst, send, recv, target):
        return pltpu.make_async_remote_copy(
            src_ref=src, dst_ref=dst, send_sem=send, recv_sem=recv, device_id=target, device_id_type=MESH
        )

    def field_copy(o, way):
        return remote(fields.at[o], fields.at[o], f_send.at[way, o], f_recv.at[o], {"walk": walk + 1 - 2 * way})

    half = lax.rem(walk, 2)

    def trial_view(q, part):
        size = rows // 2
        return trial.at[q, pl.ds(pl.multiple_of(part * size, size), size)]

    def chol_rows(o, p):
        size = chol_ref.shape[0] // (walks * PIECES)
        return pl.ds(pl.multiple_of((o * PIECES + p) * size, size), size)

    def trial_next(part):
        view = trial_view(across, part)
        return remote(view, view, t_send.at[0], t_recv.at[0, part], {"walk": walk + 1 - 2 * half})

    def trial_relay(part):
        view = trial_view(across, part)
        return remote(view, view, t_send.at[1 + part], t_recv.at[1, part], {"row": other_core})

    def trial_beside(part):
        view = trial_view(diagonal_q, part)
        return remote(view, view, t_send.at[1 + part], t_recv.at[1, part], {"row": other_core})

    def chol_copy(o, p, way):
        view = chol.at[across, chol_rows(o, p)]
        if way == 2:
            return remote(view, view, c_send.at[2, o, p], c_recv.at[1, o, p], {"row": other_core})
        return remote(view, view, c_send.at[way, o, p], c_recv.at[0, o, p], {"walk": walk + 1 - 2 * way})

    def chol_beside(o, p):
        view = chol.at[diagonal_q, chol_rows(o, p)]
        return remote(view, view, c_send.at[2, o, p], c_recv.at[1, o, p], {"row": other_core})

    def trial_across():
        view = trial_view(mine, half)
        return remote(view, view, tx_send.at[0], t_recv.at[0, half], {"slab": other_slab})

    def chol_across(p):
        return remote(chol.at[mine, chol_rows(walk, p)], chol.at[mine, chol_rows(walk, p)], cx_send.at[p], c_recv.at[0, walk, p], {"slab": other_slab})

    trial_whole = remote(trial.at[mine], trial.at[mine], tp_sem.at[0], tp_sem.at[1], {"row": other_core})
    chol_whole = remote(chol.at[mine], chol.at[mine], cp_sem.at[0], cp_sem.at[1], {"row": other_core})

    def both_ways(action):
        @pl.when(above)
        def _():
            action(0)

        @pl.when(below)
        def _():
            action(1)

    def hop(k, arrive, forward):
        @pl.when(walk >= k)
        def _():
            arrive(walk - k)
            if k < walks - 1:
                pl.when(above)(lambda: forward(walk - k, 0))

        @pl.when(walk + k < walks)
        def _():
            arrive(walk + k)
            if k < walks - 1:
                pl.when(below)(lambda: forward(walk + k, 1))

    def field_hop(k):
        hop(k, lambda o: field_copy(o, 0).wait_recv(), lambda o, way: field_copy(o, way).start())

    def chol_hop(k, p):
        def arrive(o):
            chol_copy(o, p, 0).wait_recv()
            chol_copy(o, p, 2).start()

        def forward(o, way):
            if k < walks - 2 or p < PIECES - DIRECT:
                chol_copy(o, p, way).start()

        hop(k, arrive, forward)

    def chol_direct(p, action):
        if walks > 2:
            far = walks - 1 - walk
            view = chol.at[mine, chol_rows(far, p)]
            copy = remote(view, view, cd_send.at[p], c_recv.at[0, far, p], {"slab": other_slab})
            pl.when(jnp.logical_not(above & below))(lambda: action(copy))

    def chol_start(p):
        chol_copy(walk, p, 0).wait_recv()
        both_ways(lambda way: chol_copy(walk, p, way).start())
        chol_copy(walk, p, 2).start()

    def sender(w, k):
        return lax.div(branch_ref[w * slots + k], slots)

    def step_of(number):
        order = lax.div(number, shards) * cores + lax.rem(number, cores)
        return walks - 1 - order, lax.div(lax.rem(number, shards), cores)

    def item_target(number):
        return xor(walk, step_of(number)[0], walks)

    def locate(number):
        target, place = item_target(number), step_of(number)[1]
        pick, spot, count = jnp.int32(0), jnp.int32(0), jnp.int32(0)
        for k in range(slots):
            hit = sender(target, k) == walk
            here = hit & (count == place)
            pick = jnp.where(here, lax.rem(branch_ref[target * slots + k], slots), pick)
            spot = jnp.where(here, k, spot)
            count = count + jnp.where(hit, 1, 0)
        return target, pick, spot

    slot_line = lax.broadcasted_iota(jnp.int32, (slots, rows), 0)
    my_rows = pl.ds(pl.multiple_of(mine * rows, rows), rows)

    def w_copy(r, dx, row):
        place = {"slab": lax.rem(slab + dx, slabs), "row": row}
        return remote(outgoing.at[r, dx * cores + row], prop.at[r, my_rows], w_send.at[r, dx * cores + row], w_recv.at[r, mine], place)

    def send_group(r, row):
        found = []
        for dx in range(slabs):
            target, pick, spot = locate(r * shards + lax.rem(slab + dx, slabs) * cores + row)
            found.append(pick)
            chosen[dx : dx + 1, :] = jnp.sum(jnp.where(slot_line == spot, fields[target], 0.0), axis=0, keepdims=True)
        scales = jnp.transpose(chosen[...])
        for dx in reversed(range(slabs)):
            block = (source[found[dx]].astype(jnp.float32) * scales[:, dx : dx + 1]).astype(jnp.bfloat16)
            outgoing[r, dx * cores + row] = block
            if dx:
                w_copy(r, dx, row).start()
            else:
                pl.when(core != row)(w_copy(r, dx, row).start)

                @pl.when(core == row)
                def _():
                    prop[r, my_rows] = outgoing[r, row]

    both_ways(lambda way: field_copy(walk, way).start())
    chol_across(0).start()
    trial_across().start()
    for p in range(1, PIECES):
        chol_across(p).start()
    trial_whole.start()
    chol_whole.start()

    last = walks - 1
    field_hop(1)
    chol_start(0)
    for k in range(2, last):
        field_hop(k)
    trial_next(half).wait_recv()
    trial_next(half).start()
    trial_relay(half).start()
    send_group(0, 1)
    chol_start(1)
    if last > 1:
        field_hop(last)
    send_group(0, 0)
    send_group(1, 0)
    send_group(1, 1)
    for p in range(PIECES - DIRECT, PIECES):
        chol_direct(p, lambda copy: copy.start())
    if last > 2:
        chol_hop(1, 0)
    chol_start(2)
    trial_next(1 - half).wait_recv()
    trial_relay(1 - half).start()
    chol_start(3)
    for k in range(1, last - 1):
        for p in range(1 if k == 1 else 0, PIECES):
            chol_hop(k, p)
    for part in range(2):
        trial_beside(part).wait_recv()
    trial_whole.wait_recv()
    for q in range(shards):
        trial_t[:, q * rows : (q + 1) * rows] = jnp.transpose(trial[q].astype(jnp.float32)).astype(jnp.bfloat16)

    line = lax.broadcasted_iota(jnp.int32, (electrons, electrons), 0)
    on_diagonal = line == lax.broadcasted_iota(jnp.int32, (electrons, electrons), 1)

    def invert(r, hooks):
        for q in (beside, across, diagonal_q):
            part = pl.ds(pl.multiple_of(q * rows, rows), rows)
            remote(prop.at[r, part], prop.at[r, part], w_send.at[r, 0], w_recv.at[r, q], {"row": other_core}).wait_recv()
        hooks[0]()
        matrix = dot(trial_t[...], prop[r])
        sizes_of = jnp.abs(matrix)
        column_max = jnp.max(jnp.sum(sizes_of, axis=0, keepdims=True), axis=1, keepdims=True)
        row_max = jnp.max(jnp.sum(sizes_of, axis=1, keepdims=True), axis=0, keepdims=True)
        start = jnp.transpose(matrix) / (column_max * row_max)
        stack[0:electrons, :] = start
        stack[electrons:, :] = dot3(matrix, start)

        hooks[1]()

        @pl.loop(0, PASSES)
        def _(iteration):
            both = stack[...]
            low = both.astype(jnp.bfloat16)
            stack[...] = 2.0 * both - dot(low, low[electrons:, :])

        hooks[2]()

        for first, end, hook in ((PASSES, LATER, 3), (LATER, ITERS, 4)):

            @pl.loop(first, end)
            def _(iteration):
                both = stack[...]
                stack[...] = 2.0 * both - dot3(both, both[electrons:, :])

            hooks[hook]()

        green[r] = dot(prop[r], stack[0:electrons, :].astype(jnp.bfloat16)).astype(jnp.bfloat16)

    blocks = (mine, beside, across, diagonal_q)

    def contract(r, n):
        for g in range(vectors):
            block = dot(chol[blocks[n], g * electrons : (g + 1) * electrons, :], green[r])
            number = n * vectors + g
            lanes[r, 0, number : number + 1, :] = jnp.sum(jnp.where(on_diagonal, block, 0.0), axis=0, keepdims=True)
            lanes[r, 1, number : number + 1, :] = jnp.sum(block * jnp.transpose(block), axis=0, keepdims=True)

    def o_copy(r, dx, dc):
        number = r * shards + mine
        target = item_target(number)
        device = {"walk": target, **place_of(dx, dc)}
        return target, remote(sums.at[r], arrived.at[number], o_send.at[r, dx * cores + dc], o_recv.at[number], device)

    def publish(r):
        for kind in range(2):
            total = jnp.sum(lanes[r, kind], axis=1, keepdims=True)
            sums[r, kind] = jnp.broadcast_to(total, sums.shape[2:])
        for dx, dc in steps:
            o_copy(r, dx, dc)[1].start()
        target, copy = o_copy(r, 0, 0)
        pl.when(target != walk)(copy.start)

        @pl.when(target == walk)
        def _():
            arrived[r * shards + mine] = sums[r]

    def hooks_of(k, pieces):
        def relay(group):
            def run():
                if k > 0:
                    for p in group:
                        chol_hop(k, p)

            return run

        return [relay(group) for group in pieces]

    invert(0, hooks_of(last - 1 if last > 2 else 0, HOOKS[0]))
    contract(0, 0)
    chol_whole.wait_recv()
    contract(0, 1)
    for r in range(1, items):
        invert(r, hooks_of(last, HOOKS[1]) if r == 1 else hooks_of(0, HOOKS[1]))
    contract(0, 2)
    for r in range(1, items):
        contract(r, 0)

    @pl.loop(0, walks)
    def _(o):
        @pl.loop(0, PIECES)
        def _(p):
            chol_beside(o, p).wait_recv()

    contract(0, 3)
    publish(0)
    for r in range(1, items):
        for n in range(1, shards):
            contract(r, n)
        publish(r)

    def number_of(j):
        origin, rank = sender(walk, j), jnp.int32(0)
        for k in range(j):
            rank = rank + jnp.where(sender(walk, k) == origin, 1, 0)
        step = jnp.int32(0)
        for s in range(walks):
            step = jnp.where(xor(walk, s, walks) == origin, s, step)
        order = walks - 1 - step
        number = lax.div(order, cores) * shards + lax.min(rank, local - 1) * cores + lax.rem(order, cores)
        return jnp.clip(number, 0, slots - 1)

    numbers = [number_of(j) for j in range(slots)]

    for number in range(slots):
        target = item_target(number)
        from_me = (target == walk) & (mine == number % shards)

        @pl.when(jnp.logical_not(from_me))
        def _():
            remote(sums.at[0], arrived.at[number], o_send.at[0, 0], o_recv.at[number], {"row": other_core}).wait_recv()

    column = lax.broadcasted_iota(jnp.int32, bias_ref.shape, 1)
    for kind, result in enumerate((bias_ref, exch_ref)):
        total = jnp.zeros(result.shape, jnp.float32)
        for j in range(slots):
            q = lax.rem(numbers[j], shards)
            dx, dc = lax.rem(lax.div(q, cores) + slab, slabs), lax.rem(lax.rem(q, cores) + core, cores)
            first = (dx * cores + dc) * vectors
            total = jnp.where(column == j, arrived[numbers[j], kind, pl.ds(first, vectors), 0:slots], total)
        result[...] = total
    living_ref[...] = jnp.where(column < branch_ref[walks * slots], 1.0, 0.0)

    trial_across().wait_send()
    trial_next(half).wait_send()
    for part in range(2):
        trial_relay(part).wait_send()
    trial_whole.wait_send()
    for p in range(PIECES - DIRECT, PIECES):
        chol_direct(p, lambda copy: copy.wait_send())
    chol_whole.wait_send()
    for p in range(PIECES):
        chol_across(p).wait_send()

    @pl.loop(0, walks)
    def _(o):
        def sent(way):
            field_copy(o, way).wait_send()

        pl.when(above & (o <= walk))(lambda: sent(0))
        pl.when(below & (o >= walk))(lambda: sent(1))

        @pl.loop(0, PIECES)
        def _(p):
            chol_copy(o, p, 2).wait_send()
            chained = (p < PIECES - DIRECT) | (walks < 3)
            upward, downward = (o > 0) | (walk < walks - 2), (o < walks - 1) | (walk > 1)
            pl.when(above & (o <= walk) & (chained | upward))(lambda: chol_copy(o, p, 0).wait_send())
            pl.when(below & (o >= walk) & (chained | downward))(lambda: chol_copy(o, p, 1).wait_send())

    for r in range(items):
        for dx, dc in steps:
            o_copy(r, dx, dc)[1].wait_send()
        target, copy = o_copy(r, 0, 0)
        pl.when(target != walk)(copy.wait_send)
        for row in range(cores):
            for dx in range(1, slabs):
                w_copy(r, dx, row).wait_send()
            pl.when(core != row)(w_copy(r, 0, row).wait_send)


def gathered(walkers, trial_orbitals, cholesky, branches, field):
    walks, slabs, cores = lax.axis_size("walk"), lax.axis_size("slab"), lax.axis_size("row")
    walk = lax.axis_index("walk")
    per_device, rows, electrons = walkers.shape
    vectors = cholesky.shape[0]
    capacity = (per_device + walks - 1) // walks
    local = capacity if walks * capacity == per_device else per_device
    if local == per_device:
        sender = branches.reshape(walks, per_device) // per_device
        local_index = branches.reshape(walks, per_device) % per_device
        places = jnp.arange(per_device, dtype=jnp.int32)
        same_sender = sender[:, :, None] == sender[:, None, :]
        rank = jnp.sum(same_sender & (places[None, :] < places[:, None])[None], axis=2)
        ranks = jnp.arange(capacity, dtype=jnp.int32)[None, :, None]
        wanted = (sender[:, None, :] == walk) & (rank[:, None, :] == ranks)
        chosen = jnp.sum(jnp.where(wanted, local_index[:, None, :], 0), axis=2)
        outgoing = jnp.take(walkers, chosen.reshape(-1), axis=0, mode="clip")
        outgoing = outgoing.reshape(walks, capacity, rows, electrons)
        arrived = lax.all_to_all(outgoing, "walk", split_axis=0, concat_axis=0, tiled=True)
        arrived = arrived.reshape(walks * capacity, rows, electrons)
        my_sender = lax.dynamic_index_in_dim(sender, walk, 0, keepdims=False)
        my_rank = lax.dynamic_index_in_dim(rank, walk, 0, keepdims=False)
        walkers = jnp.take(arrived, my_sender * capacity + my_rank, axis=0, mode="clip")
    shards = slabs * cores
    share = per_device // cores
    dma = pltpu.SemaphoreType.DMA
    vmem = pl.BlockSpec(memory_space=pltpu.VMEM)
    bias, exchange = pl.pallas_call(
        functools.partial(kernel, (walks, slabs, cores, per_device, local)),
        out_shape=[jax.ShapeDtypeStruct((per_device, vectors), jnp.float32)] * 2,
        in_specs=[pl.BlockSpec(memory_space=pl.ANY)] * 5,
        out_specs=[vmem] * 2,
        scratch_shapes=[
            pltpu.SMEM(branches.shape, jnp.int32),
            pltpu.VMEM((shards, electrons, rows), jnp.bfloat16),
            pltpu.VMEM((per_device, rows, electrons), jnp.bfloat16),
            pltpu.VMEM((per_device, rows, electrons), jnp.bfloat16),
            pltpu.VMEM((per_device, rows), jnp.float32),
            pltpu.VMEM((per_device, rows), jnp.float32),
            pltpu.VMEM((per_device, vectors, electrons), jnp.float32),
            pltpu.VMEM((per_device, vectors, electrons), jnp.float32),
            pltpu.VMEM((vectors, per_device, electrons), jnp.float32),
            pltpu.VMEM((vectors, per_device, electrons), jnp.float32),
            pltpu.VMEM((per_device, shards, rows, electrons), jnp.bfloat16),
            pltpu.VMEM((shards, rows, electrons), jnp.bfloat16),
            pltpu.VMEM((shards, per_device, rows), jnp.float32),
            pltpu.VMEM((vectors * electrons, shards * rows), jnp.bfloat16),
            pltpu.VMEM((shards * rows, electrons), jnp.bfloat16),
            pltpu.VMEM((per_device, vectors * electrons, electrons), jnp.bfloat16),
            pltpu.VMEM((share, electrons, electrons), jnp.float32),
            pltpu.VMEM((2 * electrons, electrons), jnp.float32),
            pltpu.VMEM((per_device, electrons, electrons), jnp.bfloat16),
            dma((per_device,)), dma((per_device,)),
            dma((slabs, per_device)), dma((slabs, per_device)),
            dma((slabs, cores, per_device)), dma((slabs, cores, per_device)),
            dma((share, cores)), dma((share, cores)),
            dma((slabs,)), dma((slabs,)), dma((slabs, cores)), dma((slabs, cores)),
            dma((slabs,)), dma((slabs,)), dma((slabs, cores)), dma((slabs, cores)),
            dma((5,)),
        ],
        compiler_params=pltpu.CompilerParams(
            collective_id=0, has_side_effects=True, vmem_limit_bytes=63 * 1024 * 1024
        ),
    )(branches, walkers, trial_orbitals, cholesky.reshape(vectors * electrons, shards * rows), field)
    return bias, exchange


def at_origin(walkers, trial_orbitals, cholesky, branches, counts, field):
    walks, slabs, cores = lax.axis_size("walk"), lax.axis_size("slab"), lax.axis_size("row")
    slots, rows, electrons = walkers.shape
    vectors = cholesky.shape[0]
    shards, local = slabs * cores, slots // walks
    items, lines, columns = slots // shards, vectors * electrons, shards * rows
    dma = pltpu.SemaphoreType.DMA
    vmem = pl.BlockSpec(memory_space=pltpu.VMEM)
    numbers = jnp.concatenate([branches, counts])
    bias, exchange, living = pl.pallas_call(
        functools.partial(origin_kernel, (walks, slabs, cores, slots, local, items)),
        out_shape=[jax.ShapeDtypeStruct((vectors, slots), jnp.float32)] * 3,
        in_specs=[pl.BlockSpec(memory_space=pltpu.HBM)] * 5,
        out_specs=[vmem] * 3,
        scratch_shapes=[
            pltpu.SMEM(numbers.shape, jnp.int32),
            pltpu.VMEM((slots, rows, electrons), jnp.bfloat16),
            pltpu.VMEM((walks, slots, rows), jnp.float32),
            pltpu.VMEM((slots, rows), jnp.float32),
            pltpu.VMEM((items, shards, rows, electrons), jnp.bfloat16),
            pltpu.VMEM((items, columns, electrons), jnp.bfloat16),
            pltpu.VMEM((shards, rows, electrons), jnp.bfloat16),
            pltpu.VMEM((electrons, columns), jnp.bfloat16),
            pltpu.VMEM((shards, lines, columns), jnp.bfloat16),
            pltpu.VMEM((2 * electrons, electrons), jnp.float32),
            pltpu.VMEM((items, columns, electrons), jnp.bfloat16),
            pltpu.VMEM((items, 2, shards * vectors, electrons), jnp.float32),
            pltpu.VMEM((items, 2, shards * vectors, 128), jnp.float32),
            pltpu.VMEM((slots, 2, shards * vectors, 128), jnp.float32),
            dma((5,)),
            dma((2, walks)), dma((walks,)),
            dma((3,)), dma((2, 2)), dma((2,)), dma((2,)),
            dma((PIECES,)), dma((PIECES,)), dma((3, walks, PIECES)), dma((2, walks, PIECES)), dma((2,)),
            dma((items, shards)), dma((items, shards)),
            dma((items, shards)), dma((slots,)),
        ],
        compiler_params=pltpu.CompilerParams(
            collective_id=0, has_side_effects=True, vmem_limit_bytes=55216 * 1024
        ),
    )(numbers, walkers, trial_orbitals, cholesky.reshape(lines, columns), field)
    return (bias * living).T, (-0.5 * exchange * living).T


def on_device(walkers, trial_orbitals, cholesky, branches, counts, field):
    walks, slabs, cores = lax.axis_size("walk"), lax.axis_size("slab"), lax.axis_size("row")
    slots, rows, electrons = walkers.shape
    lines = cholesky.shape[0] * electrons
    even = walks & (walks - 1) == 0 and slots % walks == 0 and slots % (slabs * cores) == 0
    whole = lines % (walks * PIECES * 16) == 0 and rows % 32 == 0 and walks > 2
    if slabs == cores == 2 and slots == 2 * walks and PIECES == 4 and even and whole:
        return at_origin(walkers, trial_orbitals, cholesky, branches, counts, field)
    bias, exchange = gathered(walkers, trial_orbitals, cholesky, branches, field)
    living = (jnp.arange(slots, dtype=jnp.int32) < counts[0]).astype(jnp.float32)[:, None]
    return bias * living, -0.5 * exchange * living


def solution(mesh):
    return jax.shard_map(
        on_device,
        mesh=mesh,
        in_specs=(
            P(("parts", "walk"), ("slab", "row"), None),
            P(("parts", "slab", "row"), None),
            P(("parts", "slab", "row"), None, None),
            P("parts"),
            P(("parts", "walk")),
            P(("parts", "walk"), ("slab", "row")),
        ),
        out_specs=(P(("parts", "walk"), ("slab", "row")), P(("parts", "walk"), ("slab", "row"))),
        check_vma=False,
    )
```

```python
import functools

import jax
import jax.numpy as jnp
from jax import lax
from jax.experimental import pallas as pl
from jax.experimental.pallas import tpu as pltpu
from jax.sharding import PartitionSpec as P

ITERS = 10
EARLY = 4
PASSES = 7
PIECES = 4
DIRECT = 3
LATER = 8
HOOKS = (((), (), (0,), (1,), (2, 3)), ((), (), (), (), (0, 1, 2, 3)))
MESH = pl.DeviceIdType.MESH


def split(x):
    high = x.astype(jnp.bfloat16)
    low = (x - high.astype(jnp.float32)).astype(jnp.bfloat16)
    return high, low


def dot(a, b):
    return jnp.dot(a, b, preferred_element_type=jnp.float32)


def dot3(a, b):
    ah, al = split(a)
    bh, bl = split(b)
    return dot(ah, bh) + (dot(ah, bl) + dot(al, bh))


def partner(position, step, size):
    if size & (size - 1):
        return (position + step) % size
    result, bit = 0, 1
    while bit < size:
        digit = (position // bit) % 2
        result += bit * (1 - digit if step & bit else digit)
        bit *= 2
    return result


def kernel(
    sizes, branch_in, walker_ref, trial_ref, chol_ref, field_ref, bias_ref, exch_ref,
    branch_ref, trial_t, source, outgoing, field_in, field_out, traces, squares, bias_rows, exch_rows, raw, trial, field, chol, prop, half, inter, stack, inverse,
    z_send, z_recv, x_send, x_recv, c_send, c_recv, i_send, i_recv,
    tx_send, tx_recv, tc_send, tc_recv, fx_send, fx_recv, fc_send, fc_recv, own_sem,
):
    walks, slabs, cores, slots, local = sizes
    walk, slab, core = lax.axis_index("walk"), lax.axis_index("slab"), lax.axis_index("row")
    rows, electrons = trial_ref.shape
    vectors = chol_ref.shape[0] // electrons
    mine = slab * cores + core

    def slab_peer(step):
        return lax.rem(slab + step, slabs)

    def core_peer(step):
        return lax.rem(core + step, cores)

    def slab_source(step):
        return lax.rem(slab + slabs - step, slabs)

    def core_source(step):
        return lax.rem(core + cores - step, cores)

    loads = [(branch_in, branch_ref), (walker_ref, source), (field_ref, field_in), (trial_ref, trial.at[mine]), (chol_ref, chol)]
    own = [pltpu.make_async_copy(src, dst, own_sem.at[k]) for k, (src, dst) in enumerate(loads)]
    for copy in own:
        copy.start()
    barrier = pltpu.get_barrier_semaphore()
    greeted = 0
    if local < slots:
        for step in range(1, walks):
            pl.semaphore_signal(barrier, inc=1, device_id={"walk": partner(walk, step, walks)}, device_id_type=MESH)
            greeted += 1
    for step in range(1, slabs):
        pl.semaphore_signal(barrier, inc=1, device_id={"slab": slab_peer(step)}, device_id_type=MESH)
        greeted += 1
    for step in range(1, cores):
        pl.semaphore_signal(barrier, inc=1, device_id={"row": core_peer(step)}, device_id_type=MESH)
        greeted += 1

    def sender(w, k):
        return lax.div(branch_ref[w * slots + k], slots)

    def kth(w, origin, values):
        picks, count = [jnp.int32(0)] * local, jnp.int32(0)
        for k in range(slots):
            hit = sender(w, k) == origin
            picks = [jnp.where(hit & (count == place), values(k), pick) for place, pick in enumerate(picks)]
            count = count + jnp.where(hit, 1, 0)
        return picks

    for copy in own[:3]:
        copy.wait()
    slot_of = list(range(slots))
    if local < slots:
        origins = []
        for step in range(walks):
            target = partner(walk, step, walks)
            picks = kth(target, walk, lambda k: lax.rem(branch_ref[target * slots + k], slots))
            for place, pick in enumerate(picks):
                if step == 0:
                    raw[place, mine] = source[pick]
                else:
                    outgoing[step * local + place] = source[pick]
            origin = target if walks & (walks - 1) == 0 else (walk + walks - step) % walks
            origins.append(origin)
            for place, pick in enumerate(kth(walk, origin, lambda k: k)):
                i = step * local + place
                field_out[i : i + 1, :] = field_in[pl.ds(pick, 1), :]
        for j in range(slots):
            origin, rank, step_of = sender(walk, j), jnp.int32(0), jnp.int32(0)
            for k in range(j):
                rank = rank + jnp.where(sender(walk, k) == origin, 1, 0)
            for step in range(walks):
                step_of = jnp.where(origins[step] == origin, step, step_of)
            slot_of[j] = jnp.minimum(step_of * local + rank, slots - 1)
    else:
        for i in range(slots):
            raw[i, mine] = source[i]
        field_out[...] = field_in[...]
    field[mine] = field_out[...]
    for copy in own[3:]:
        copy.wait()
    pl.semaphore_wait(barrier, greeted)

    def remote(src, dst, send, recv, target):
        return pltpu.make_async_remote_copy(
            src_ref=src, dst_ref=dst, send_sem=send, recv_sem=recv, device_id=target, device_id_type=MESH
        )

    def z_copy(i, step):
        return remote(outgoing.at[i], raw.at[i, mine], z_send.at[i], z_recv.at[i], {"walk": partner(walk, step, walks)})

    def x_copy(i, step):
        return remote(raw.at[i, mine], raw.at[i, mine], x_send.at[step, i], x_recv.at[step, i], {"slab": slab_peer(step)})

    def c_copy(i, hop, step):
        q = slab_source(hop) * cores + core
        return remote(raw.at[i, q], raw.at[i, q], c_send.at[hop, step, i], c_recv.at[hop, step, i], {"row": core_peer(step)})

    def small(src, buf, xs, xr, cs, cr):
        def x(step):
            return remote(src, buf.at[mine], xs.at[step], xr.at[step], {"slab": slab_peer(step)})

        def c(hop, step):
            q = slab_source(hop) * cores + core
            block = src if hop == 0 else buf.at[q]
            return remote(block, buf.at[q], cs.at[hop, step], cr.at[hop, step], {"row": core_peer(step)})

        return x, c

    for i in range(local, slots):
        z_copy(i, i // local).start()
    pairs = [
        small(trial_ref, trial, tx_send, tx_recv, tc_send, tc_recv),
        small(field_out, field, fx_send, fx_recv, fc_send, fc_recv),
    ]
    for x, c in pairs:
        for step in range(1, slabs):
            x(step).start()
        for step in range(1, cores):
            c(0, step).start()
    def spread(i):
        for step in range(1, slabs):
            x_copy(i, step).start()
        for step in range(1, cores):
            c_copy(i, 0, step).start()

    def relay(i):
        for hop in range(1, slabs):
            x_copy(i, hop).wait_recv()
            for step in range(1, cores):
                c_copy(i, hop, step).start()

    def compute(i):
        for hop in range(slabs):
            for step in range(1, cores):
                c_copy(i, hop, step).wait_recv()
        for q in range(slabs * cores):
            column = jnp.transpose(field[q])
            lane = lax.broadcasted_iota(jnp.int32, column.shape, 1)
            scale = jnp.sum(jnp.where(lane == i, column, 0.0), axis=1, keepdims=True)
            prop[q * rows : (q + 1) * rows, :] = (raw[i, q].astype(jnp.float32) * scale).astype(jnp.bfloat16)
        @pl.when(lax.rem(i, cores) == core)
        def _():
            total = dot(trial_t[0], prop[0:rows, :])
            for q in range(1, slabs * cores):
                total += dot(trial_t[q], prop[q * rows : (q + 1) * rows, :])
            inter[i // cores] = total

        half[i] = dot(chol[...], prop[...]).astype(jnp.bfloat16)

    for i in range(local):
        spread(i)
    for x, c in pairs:
        for hop in range(1, slabs):
            x(hop).wait_recv()
            for step in range(1, cores):
                c(hop, step).start()
    for x, c in pairs:
        for hop in range(slabs):
            for step in range(1, cores):
                c(hop, step).wait_recv()

    for q in range(slabs * cores):
        trial_t[q] = jnp.transpose(trial[q].astype(jnp.float32)).astype(jnp.bfloat16)
    share = slots // cores
    line = lax.broadcasted_iota(jnp.int32, (electrons, electrons), 0)
    diagonal = line == lax.broadcasted_iota(jnp.int32, (electrons, electrons), 1)

    def i_copy(i, step):
        place = inverse.at[i]
        return remote(place, place, i_send.at[i // cores, step], i_recv.at[i // cores, step], {"row": core_peer(step)})

    def first_guess(n):
        matrix = inter[n]
        sizes_of = jnp.abs(matrix)
        column_max = jnp.max(jnp.sum(sizes_of, axis=0, keepdims=True), axis=1, keepdims=True)
        row_max = jnp.max(jnp.sum(sizes_of, axis=1, keepdims=True), axis=0, keepdims=True)
        start = jnp.transpose(matrix) / (column_max * row_max)
        stack[0:electrons, :] = start
        stack[electrons:, :] = dot3(matrix, start)

    def finish(i):
        @pl.when(lax.rem(i, cores) != core)
        def _():
            i_copy(i, lax.rem(core + cores - lax.rem(i, cores), cores)).wait_recv()

        contracted = dot(half[i], inverse[i])
        for g in range(vectors):
            block = contracted[g * electrons : (g + 1) * electrons, :]
            traces[i, g : g + 1, :] = jnp.sum(jnp.where(diagonal, block, 0.0), axis=0, keepdims=True)
            squares[i, g : g + 1, :] = jnp.sum(block * jnp.transpose(block), axis=0, keepdims=True)

    ready = cores + 1

    @pl.loop(0, slots + ready + cores + 1)
    def _(i):
        @pl.when((i >= local) & (i < slots))
        def _():
            z_copy(i, 0).wait_recv()
            spread(i)

        @pl.when((i > 1) & (i < slots + 2))
        def _():
            compute(i - 2)

        @pl.when((i > 0) & (i <= slots))
        def _():
            relay(i - 1)

        for part in range(cores):

            @pl.when((i >= ready) & (i < slots + ready) & (lax.rem(i + cores - 1, cores) == part))
            def _():
                n = (i - ready) // cores
                if part == 0:
                    first_guess(n)

                first, middle, last = ITERS * part // cores, EARLY, ITERS * (part + 1) // cores

                @pl.loop(first, max(first, min(middle, last)))
                def _(iteration):
                    both = stack[...]
                    low = both.astype(jnp.bfloat16)
                    stack[...] = 2.0 * both - dot(low, low[electrons:, :])

                @pl.loop(min(last, max(middle, first)), last)
                def _(iteration):
                    both = stack[...]
                    stack[...] = 2.0 * both - dot3(both, both[electrons:, :])

                if part == cores - 1:
                    inverse[n * cores + core] = stack[0:electrons, :].astype(jnp.bfloat16)
                    for step in range(1, cores):
                        i_copy(n * cores + core, step).start()

        @pl.when(i > ready + cores)
        def _():
            finish(i - ready - cores - 1)


    column = lax.broadcasted_iota(jnp.int32, bias_ref.shape, 1)
    for terms, rows_of, result in ((traces, bias_rows, bias_ref), (squares, exch_rows, exch_ref)):
        for j in range(slots):
            block = terms[slot_of[j]]
            for g in range(vectors):
                rows_of[g, j : j + 1, :] = block[g : g + 1, :]
        total = jnp.zeros(result.shape, jnp.float32)
        for g in range(vectors):
            total = jnp.where(column == g, jnp.sum(rows_of[g], axis=1, keepdims=True), total)
        result[...] = total

    for i in range(local, slots):
        z_copy(i, i // local).wait_send()

    @pl.loop(0, slots)
    def _(i):
        for step in range(1, slabs):
            x_copy(i, step).wait_send()
        for hop in range(slabs):
            for step in range(1, cores):
                c_copy(i, hop, step).wait_send()

    for x, c in pairs:
        for step in range(1, slabs):
            x(step).wait_send()
        for hop in range(slabs):
            for step in range(1, cores):
                c(hop, step).wait_send()
    for n in range(share):
        for step in range(1, cores):
            i_copy(n * cores + core, step).wait_send()


def xor(a, b, size):
    result, bit = 0, 1
    while bit < size:
        left, right = lax.rem(lax.div(a, bit), 2), lax.rem(lax.div(b, bit), 2)
        result += bit * lax.rem(left + right, 2)
        bit *= 2
    return result


def origin_kernel(
    sizes, branch_in, walker_ref, trial_ref, chol_ref, field_ref, bias_ref, exch_ref, living_ref,
    branch_ref, source, fields, chosen, outgoing, prop, trial, trial_t, chol, stack, green, lanes, sums, arrived,
    own_sem, f_send, f_recv, t_send, t_recv, tx_send, tp_sem, cx_send, cd_send, c_send, c_recv, cp_sem, w_send, w_recv, o_send, o_recv,
):
    walks, slabs, cores, slots, local, items = sizes
    walk, slab, core = lax.axis_index("walk"), lax.axis_index("slab"), lax.axis_index("row")
    rows, electrons = trial_ref.shape
    shards = slabs * cores
    vectors = chol_ref.shape[0] // electrons
    mine = slab * cores + core
    other_slab, other_core = 1 - slab, 1 - core
    across, beside, diagonal_q = other_slab * cores + core, slab * cores + other_core, other_slab * cores + other_core
    below, above = walk > 0, walk < walks - 1
    steps = ((1, 1), (1, 0), (0, 1))

    loads = [(branch_in, branch_ref), (walker_ref, source), (field_ref, fields.at[walk]), (trial_ref, trial.at[mine]), (chol_ref, chol.at[mine])]
    own = [pltpu.make_async_copy(src, dst, own_sem.at[k]) for k, (src, dst) in enumerate(loads)]
    barrier = pltpu.get_barrier_semaphore()

    def greet(target):
        pl.semaphore_signal(barrier, inc=1, device_id=target, device_id_type=MESH)

    def place_of(dx, dc):
        return {"slab": lax.rem(slab + dx, slabs), "row": lax.rem(core + dc, cores)}

    for dx, dc in steps:
        greet(place_of(dx, dc))

    @pl.when(below)
    def _():
        greet({"walk": walk - 1})

    @pl.when(above)
    def _():
        greet({"walk": walk + 1})

    for copy in own:
        copy.start()
    for copy in own:
        copy.wait()
    pl.semaphore_wait(barrier, len(steps) + jnp.where(below, 1, 0) + jnp.where(above, 1, 0))

    def remote(src, dst, send, recv, target):
        return pltpu.make_async_remote_copy(
            src_ref=src, dst_ref=dst, send_sem=send, recv_sem=recv, device_id=target, device_id_type=MESH
        )

    def field_copy(o, way):
        return remote(fields.at[o], fields.at[o], f_send.at[way, o], f_recv.at[o], {"walk": walk + 1 - 2 * way})

    half = lax.rem(walk, 2)

    def trial_view(q, part):
        size = rows // 2
        return trial.at[q, pl.ds(pl.multiple_of(part * size, size), size)]

    def chol_rows(o, p):
        size = chol_ref.shape[0] // (walks * PIECES)
        return pl.ds(pl.multiple_of((o * PIECES + p) * size, size), size)

    def trial_next(part):
        view = trial_view(across, part)
        return remote(view, view, t_send.at[0], t_recv.at[0, part], {"walk": walk + 1 - 2 * half})

    def trial_relay(part):
        view = trial_view(across, part)
        return remote(view, view, t_send.at[1 + part], t_recv.at[1, part], {"row": other_core})

    def trial_beside(part):
        view = trial_view(diagonal_q, part)
        return remote(view, view, t_send.at[1 + part], t_recv.at[1, part], {"row": other_core})

    def chol_copy(o, p, way):
        view = chol.at[across, chol_rows(o, p)]
        if way == 2:
            return remote(view, view, c_send.at[2, o, p], c_recv.at[1, o, p], {"row": other_core})
        return remote(view, view, c_send.at[way, o, p], c_recv.at[0, o, p], {"walk": walk + 1 - 2 * way})

    def chol_beside(o, p):
        view = chol.at[diagonal_q, chol_rows(o, p)]
        return remote(view, view, c_send.at[2, o, p], c_recv.at[1, o, p], {"row": other_core})

    def trial_across():
        view = trial_view(mine, half)
        return remote(view, view, tx_send.at[0], t_recv.at[0, half], {"slab": other_slab})

    def chol_across(p):
        return remote(chol.at[mine, chol_rows(walk, p)], chol.at[mine, chol_rows(walk, p)], cx_send.at[p], c_recv.at[0, walk, p], {"slab": other_slab})

    trial_whole = remote(trial.at[mine], trial.at[mine], tp_sem.at[0], tp_sem.at[1], {"row": other_core})
    chol_whole = remote(chol.at[mine], chol.at[mine], cp_sem.at[0], cp_sem.at[1], {"row": other_core})

    def both_ways(action):
        @pl.when(above)
        def _():
            action(0)

        @pl.when(below)
        def _():
            action(1)

    def hop(k, arrive, forward):
        @pl.when(walk >= k)
        def _():
            arrive(walk - k)
            if k < walks - 1:
                pl.when(above)(lambda: forward(walk - k, 0))

        @pl.when(walk + k < walks)
        def _():
            arrive(walk + k)
            if k < walks - 1:
                pl.when(below)(lambda: forward(walk + k, 1))

    def field_hop(k):
        hop(k, lambda o: field_copy(o, 0).wait_recv(), lambda o, way: field_copy(o, way).start())

    def chol_hop(k, p):
        def arrive(o):
            chol_copy(o, p, 0).wait_recv()
            chol_copy(o, p, 2).start()

        def forward(o, way):
            if k < walks - 2 or p < PIECES - DIRECT:
                chol_copy(o, p, way).start()

        hop(k, arrive, forward)

    def chol_direct(p, action):
        if walks > 2:
            far = walks - 1 - walk
            view = chol.at[mine, chol_rows(far, p)]
            copy = remote(view, view, cd_send.at[p], c_recv.at[0, far, p], {"slab": other_slab})
            pl.when(jnp.logical_not(above & below))(lambda: action(copy))

    def chol_start(p):
        chol_copy(walk, p, 0).wait_recv()
        both_ways(lambda way: chol_copy(walk, p, way).start())
        chol_copy(walk, p, 2).start()

    def sender(w, k):
        return lax.div(branch_ref[w * slots + k], slots)

    def step_of(number):
        order = lax.div(number, shards) * cores + lax.rem(number, cores)
        return walks - 1 - order, lax.div(lax.rem(number, shards), cores)

    def item_target(number):
        return xor(walk, step_of(number)[0], walks)

    def locate(number):
        target, place = item_target(number), step_of(number)[1]
        pick, spot, count = jnp.int32(0), jnp.int32(0), jnp.int32(0)
        for k in range(slots):
            hit = sender(target, k) == walk
            here = hit & (count == place)
            pick = jnp.where(here, lax.rem(branch_ref[target * slots + k], slots), pick)
            spot = jnp.where(here, k, spot)
            count = count + jnp.where(hit, 1, 0)
        return target, pick, spot

    slot_line = lax.broadcasted_iota(jnp.int32, (slots, rows), 0)
    my_rows = pl.ds(pl.multiple_of(mine * rows, rows), rows)

    def w_copy(r, dx, row):
        place = {"slab": lax.rem(slab + dx, slabs), "row": row}
        return remote(outgoing.at[r, dx * cores + row], prop.at[r, my_rows], w_send.at[r, dx * cores + row], w_recv.at[r, mine], place)

    def send_group(r, row):
        found = []
        for dx in range(slabs):
            target, pick, spot = locate(r * shards + lax.rem(slab + dx, slabs) * cores + row)
            found.append(pick)
            chosen[dx : dx + 1, :] = jnp.sum(jnp.where(slot_line == spot, fields[target], 0.0), axis=0, keepdims=True)
        scales = jnp.transpose(chosen[...])
        for dx in reversed(range(slabs)):
            block = (source[found[dx]].astype(jnp.float32) * scales[:, dx : dx + 1]).astype(jnp.bfloat16)
            outgoing[r, dx * cores + row] = block
            if dx:
                w_copy(r, dx, row).start()
            else:
                pl.when(core != row)(w_copy(r, dx, row).start)

                @pl.when(core == row)
                def _():
                    prop[r, my_rows] = outgoing[r, row]

    both_ways(lambda way: field_copy(walk, way).start())
    chol_across(0).start()
    trial_across().start()
    for p in range(1, PIECES):
        chol_across(p).start()
    trial_whole.start()
    chol_whole.start()

    last = walks - 1
    field_hop(1)
    chol_start(0)
    for k in range(2, last):
        field_hop(k)
    trial_next(half).wait_recv()
    trial_next(half).start()
    trial_relay(half).start()
    send_group(0, 1)
    chol_start(1)
    if last > 1:
        field_hop(last)
    send_group(0, 0)
    send_group(1, 0)
    send_group(1, 1)
    for p in range(PIECES - DIRECT, PIECES):
        chol_direct(p, lambda copy: copy.start())
    if last > 2:
        chol_hop(1, 0)
    chol_start(2)
    trial_next(1 - half).wait_recv()
    trial_relay(1 - half).start()
    chol_start(3)
    for k in range(1, last - 1):
        for p in range(1 if k == 1 else 0, PIECES):
            chol_hop(k, p)
    for part in range(2):
        trial_beside(part).wait_recv()
    trial_whole.wait_recv()
    for q in range(shards):
        trial_t[:, q * rows : (q + 1) * rows] = jnp.transpose(trial[q].astype(jnp.float32)).astype(jnp.bfloat16)

    line = lax.broadcasted_iota(jnp.int32, (electrons, electrons), 0)
    on_diagonal = line == lax.broadcasted_iota(jnp.int32, (electrons, electrons), 1)

    def invert(r, hooks):
        for q in (beside, across, diagonal_q):
            part = pl.ds(pl.multiple_of(q * rows, rows), rows)
            remote(prop.at[r, part], prop.at[r, part], w_send.at[r, 0], w_recv.at[r, q], {"row": other_core}).wait_recv()
        hooks[0]()
        matrix = dot(trial_t[...], prop[r])
        sizes_of = jnp.abs(matrix)
        column_max = jnp.max(jnp.sum(sizes_of, axis=0, keepdims=True), axis=1, keepdims=True)
        row_max = jnp.max(jnp.sum(sizes_of, axis=1, keepdims=True), axis=0, keepdims=True)
        start = jnp.transpose(matrix) / (column_max * row_max)
        stack[0:electrons, :] = start
        stack[electrons:, :] = dot3(matrix, start)

        hooks[1]()

        @pl.loop(0, PASSES)
        def _(iteration):
            both = stack[...]
            low = both.astype(jnp.bfloat16)
            stack[...] = 2.0 * both - dot(low, low[electrons:, :])

        hooks[2]()

        for first, end, hook in ((PASSES, LATER, 3), (LATER, ITERS, 4)):

            @pl.loop(first, end)
            def _(iteration):
                both = stack[...]
                stack[...] = 2.0 * both - dot3(both, both[electrons:, :])

            hooks[hook]()

        green[r] = dot(prop[r], stack[0:electrons, :].astype(jnp.bfloat16)).astype(jnp.bfloat16)

    blocks = (mine, beside, across, diagonal_q)

    def contract(r, n):
        for g in range(vectors):
            block = dot(chol[blocks[n], g * electrons : (g + 1) * electrons, :], green[r])
            number = n * vectors + g
            lanes[r, 0, number : number + 1, :] = jnp.sum(jnp.where(on_diagonal, block, 0.0), axis=0, keepdims=True)
            lanes[r, 1, number : number + 1, :] = jnp.sum(block * jnp.transpose(block), axis=0, keepdims=True)

    def o_copy(r, dx, dc):
        number = r * shards + mine
        target = item_target(number)
        device = {"walk": target, **place_of(dx, dc)}
        return target, remote(sums.at[r], arrived.at[number], o_send.at[r, dx * cores + dc], o_recv.at[number], device)

    def publish(r):
        for kind in range(2):
            total = jnp.sum(lanes[r, kind], axis=1, keepdims=True)
            sums[r, kind] = jnp.broadcast_to(total, sums.shape[2:])
        for dx, dc in steps:
            o_copy(r, dx, dc)[1].start()
        target, copy = o_copy(r, 0, 0)
        pl.when(target != walk)(copy.start)

        @pl.when(target == walk)
        def _():
            arrived[r * shards + mine] = sums[r]

    def hooks_of(k, pieces):
        def relay(group):
            def run():
                if k > 0:
                    for p in group:
                        chol_hop(k, p)

            return run

        return [relay(group) for group in pieces]

    invert(0, hooks_of(last - 1 if last > 2 else 0, HOOKS[0]))
    contract(0, 0)
    chol_whole.wait_recv()
    contract(0, 1)
    for r in range(1, items):
        invert(r, hooks_of(last, HOOKS[1]) if r == 1 else hooks_of(0, HOOKS[1]))
    contract(0, 2)

    @pl.loop(0, walks)
    def _(o):
        @pl.loop(0, PIECES)
        def _(p):
            chol_beside(o, p).wait_recv()

    contract(0, 3)
    publish(0)
    for r in range(1, items):
        for n in range(shards):
            contract(r, n)
        publish(r)

    def number_of(j):
        origin, rank = sender(walk, j), jnp.int32(0)
        for k in range(j):
            rank = rank + jnp.where(sender(walk, k) == origin, 1, 0)
        step = jnp.int32(0)
        for s in range(walks):
            step = jnp.where(xor(walk, s, walks) == origin, s, step)
        order = walks - 1 - step
        number = lax.div(order, cores) * shards + lax.min(rank, local - 1) * cores + lax.rem(order, cores)
        return jnp.clip(number, 0, slots - 1)

    numbers = [number_of(j) for j in range(slots)]

    for number in range(slots):
        target = item_target(number)
        from_me = (target == walk) & (mine == number % shards)

        @pl.when(jnp.logical_not(from_me))
        def _():
            remote(sums.at[0], arrived.at[number], o_send.at[0, 0], o_recv.at[number], {"row": other_core}).wait_recv()

    column = lax.broadcasted_iota(jnp.int32, bias_ref.shape, 1)
    for kind, result in enumerate((bias_ref, exch_ref)):
        total = jnp.zeros(result.shape, jnp.float32)
        for j in range(slots):
            q = lax.rem(numbers[j], shards)
            dx, dc = lax.rem(lax.div(q, cores) + slab, slabs), lax.rem(lax.rem(q, cores) + core, cores)
            first = (dx * cores + dc) * vectors
            total = jnp.where(column == j, arrived[numbers[j], kind, pl.ds(first, vectors), 0:slots], total)
        result[...] = total
    living_ref[...] = jnp.where(column < branch_ref[walks * slots], 1.0, 0.0)

    trial_across().wait_send()
    trial_next(half).wait_send()
    for part in range(2):
        trial_relay(part).wait_send()
    trial_whole.wait_send()
    for p in range(PIECES - DIRECT, PIECES):
        chol_direct(p, lambda copy: copy.wait_send())
    chol_whole.wait_send()
    for p in range(PIECES):
        chol_across(p).wait_send()

    @pl.loop(0, walks)
    def _(o):
        def sent(way):
            field_copy(o, way).wait_send()

        pl.when(above & (o <= walk))(lambda: sent(0))
        pl.when(below & (o >= walk))(lambda: sent(1))

        @pl.loop(0, PIECES)
        def _(p):
            chol_copy(o, p, 2).wait_send()
            chained = (p < PIECES - DIRECT) | (walks < 3)
            upward, downward = (o > 0) | (walk < walks - 2), (o < walks - 1) | (walk > 1)
            pl.when(above & (o <= walk) & (chained | upward))(lambda: chol_copy(o, p, 0).wait_send())
            pl.when(below & (o >= walk) & (chained | downward))(lambda: chol_copy(o, p, 1).wait_send())

    for r in range(items):
        for dx, dc in steps:
            o_copy(r, dx, dc)[1].wait_send()
        target, copy = o_copy(r, 0, 0)
        pl.when(target != walk)(copy.wait_send)
        for row in range(cores):
            for dx in range(1, slabs):
                w_copy(r, dx, row).wait_send()
            pl.when(core != row)(w_copy(r, 0, row).wait_send)


def gathered(walkers, trial_orbitals, cholesky, branches, field):
    walks, slabs, cores = lax.axis_size("walk"), lax.axis_size("slab"), lax.axis_size("row")
    walk = lax.axis_index("walk")
    per_device, rows, electrons = walkers.shape
    vectors = cholesky.shape[0]
    capacity = (per_device + walks - 1) // walks
    local = capacity if walks * capacity == per_device else per_device
    if local == per_device:
        sender = branches.reshape(walks, per_device) // per_device
        local_index = branches.reshape(walks, per_device) % per_device
        places = jnp.arange(per_device, dtype=jnp.int32)
        same_sender = sender[:, :, None] == sender[:, None, :]
        rank = jnp.sum(same_sender & (places[None, :] < places[:, None])[None], axis=2)
        ranks = jnp.arange(capacity, dtype=jnp.int32)[None, :, None]
        wanted = (sender[:, None, :] == walk) & (rank[:, None, :] == ranks)
        chosen = jnp.sum(jnp.where(wanted, local_index[:, None, :], 0), axis=2)
        outgoing = jnp.take(walkers, chosen.reshape(-1), axis=0, mode="clip")
        outgoing = outgoing.reshape(walks, capacity, rows, electrons)
        arrived = lax.all_to_all(outgoing, "walk", split_axis=0, concat_axis=0, tiled=True)
        arrived = arrived.reshape(walks * capacity, rows, electrons)
        my_sender = lax.dynamic_index_in_dim(sender, walk, 0, keepdims=False)
        my_rank = lax.dynamic_index_in_dim(rank, walk, 0, keepdims=False)
        walkers = jnp.take(arrived, my_sender * capacity + my_rank, axis=0, mode="clip")
    shards = slabs * cores
    share = per_device // cores
    dma = pltpu.SemaphoreType.DMA
    vmem = pl.BlockSpec(memory_space=pltpu.VMEM)
    bias, exchange = pl.pallas_call(
        functools.partial(kernel, (walks, slabs, cores, per_device, local)),
        out_shape=[jax.ShapeDtypeStruct((per_device, vectors), jnp.float32)] * 2,
        in_specs=[pl.BlockSpec(memory_space=pl.ANY)] * 5,
        out_specs=[vmem] * 2,
        scratch_shapes=[
            pltpu.SMEM(branches.shape, jnp.int32),
            pltpu.VMEM((shards, electrons, rows), jnp.bfloat16),
            pltpu.VMEM((per_device, rows, electrons), jnp.bfloat16),
            pltpu.VMEM((per_device, rows, electrons), jnp.bfloat16),
            pltpu.VMEM((per_device, rows), jnp.float32),
            pltpu.VMEM((per_device, rows), jnp.float32),
            pltpu.VMEM((per_device, vectors, electrons), jnp.float32),
            pltpu.VMEM((per_device, vectors, electrons), jnp.float32),
            pltpu.VMEM((vectors, per_device, electrons), jnp.float32),
            pltpu.VMEM((vectors, per_device, electrons), jnp.float32),
            pltpu.VMEM((per_device, shards, rows, electrons), jnp.bfloat16),
            pltpu.VMEM((shards, rows, electrons), jnp.bfloat16),
            pltpu.VMEM((shards, per_device, rows), jnp.float32),
            pltpu.VMEM((vectors * electrons, shards * rows), jnp.bfloat16),
            pltpu.VMEM((shards * rows, electrons), jnp.bfloat16),
            pltpu.VMEM((per_device, vectors * electrons, electrons), jnp.bfloat16),
            pltpu.VMEM((share, electrons, electrons), jnp.float32),
            pltpu.VMEM((2 * electrons, electrons), jnp.float32),
            pltpu.VMEM((per_device, electrons, electrons), jnp.bfloat16),
            dma((per_device,)), dma((per_device,)),
            dma((slabs, per_device)), dma((slabs, per_device)),
            dma((slabs, cores, per_device)), dma((slabs, cores, per_device)),
            dma((share, cores)), dma((share, cores)),
            dma((slabs,)), dma((slabs,)), dma((slabs, cores)), dma((slabs, cores)),
            dma((slabs,)), dma((slabs,)), dma((slabs, cores)), dma((slabs, cores)),
            dma((5,)),
        ],
        compiler_params=pltpu.CompilerParams(
            collective_id=0, has_side_effects=True, vmem_limit_bytes=63 * 1024 * 1024
        ),
    )(branches, walkers, trial_orbitals, cholesky.reshape(vectors * electrons, shards * rows), field)
    return bias, exchange


def at_origin(walkers, trial_orbitals, cholesky, branches, counts, field):
    walks, slabs, cores = lax.axis_size("walk"), lax.axis_size("slab"), lax.axis_size("row")
    slots, rows, electrons = walkers.shape
    vectors = cholesky.shape[0]
    shards, local = slabs * cores, slots // walks
    items, lines, columns = slots // shards, vectors * electrons, shards * rows
    dma = pltpu.SemaphoreType.DMA
    vmem = pl.BlockSpec(memory_space=pltpu.VMEM)
    numbers = jnp.concatenate([branches, counts])
    bias, exchange, living = pl.pallas_call(
        functools.partial(origin_kernel, (walks, slabs, cores, slots, local, items)),
        out_shape=[jax.ShapeDtypeStruct((vectors, slots), jnp.float32)] * 3,
        in_specs=[pl.BlockSpec(memory_space=pltpu.HBM)] * 5,
        out_specs=[vmem] * 3,
        scratch_shapes=[
            pltpu.SMEM(numbers.shape, jnp.int32),
            pltpu.VMEM((slots, rows, electrons), jnp.bfloat16),
            pltpu.VMEM((walks, slots, rows), jnp.float32),
            pltpu.VMEM((slots, rows), jnp.float32),
            pltpu.VMEM((items, shards, rows, electrons), jnp.bfloat16),
            pltpu.VMEM((items, columns, electrons), jnp.bfloat16),
            pltpu.VMEM((shards, rows, electrons), jnp.bfloat16),
            pltpu.VMEM((electrons, columns), jnp.bfloat16),
            pltpu.VMEM((shards, lines, columns), jnp.bfloat16),
            pltpu.VMEM((2 * electrons, electrons), jnp.float32),
            pltpu.VMEM((items, columns, electrons), jnp.bfloat16),
            pltpu.VMEM((items, 2, shards * vectors, electrons), jnp.float32),
            pltpu.VMEM((items, 2, shards * vectors, 128), jnp.float32),
            pltpu.VMEM((slots, 2, shards * vectors, 128), jnp.float32),
            dma((5,)),
            dma((2, walks)), dma((walks,)),
            dma((3,)), dma((2, 2)), dma((2,)), dma((2,)),
            dma((PIECES,)), dma((PIECES,)), dma((3, walks, PIECES)), dma((2, walks, PIECES)), dma((2,)),
            dma((items, shards)), dma((items, shards)),
            dma((items, shards)), dma((slots,)),
        ],
        compiler_params=pltpu.CompilerParams(
            collective_id=0, has_side_effects=True, vmem_limit_bytes=55216 * 1024
        ),
    )(numbers, walkers, trial_orbitals, cholesky.reshape(lines, columns), field)
    return (bias * living).T, (-0.5 * exchange * living).T


def on_device(walkers, trial_orbitals, cholesky, branches, counts, field):
    walks, slabs, cores = lax.axis_size("walk"), lax.axis_size("slab"), lax.axis_size("row")
    slots, rows, electrons = walkers.shape
    lines = cholesky.shape[0] * electrons
    even = walks & (walks - 1) == 0 and slots % walks == 0 and slots % (slabs * cores) == 0
    whole = lines % (walks * PIECES * 16) == 0 and rows % 32 == 0 and walks > 2
    if slabs == cores == 2 and slots == 2 * walks and PIECES == 4 and even and whole:
        return at_origin(walkers, trial_orbitals, cholesky, branches, counts, field)
    bias, exchange = gathered(walkers, trial_orbitals, cholesky, branches, field)
    living = (jnp.arange(slots, dtype=jnp.int32) < counts[0]).astype(jnp.float32)[:, None]
    return bias * living, -0.5 * exchange * living


def solution(mesh):
    return jax.shard_map(
        on_device,
        mesh=mesh,
        in_specs=(
            P(("parts", "walk"), ("slab", "row"), None),
            P(("parts", "slab", "row"), None),
            P(("parts", "slab", "row"), None, None),
            P("parts"),
            P(("parts", "walk")),
            P(("parts", "walk"), ("slab", "row")),
        ),
        out_specs=(P(("parts", "walk"), ("slab", "row")), P(("parts", "walk"), ("slab", "row"))),
        check_vma=False,
    )
```

```python
import functools

import jax
import jax.numpy as jnp
from jax import lax
from jax.experimental import pallas as pl
from jax.experimental.pallas import tpu as pltpu
from jax.sharding import PartitionSpec as P

ITERS = 10
EARLY = 4
PASSES = 7
PIECES = 4
DIRECT = 3
LATER = 8
HOOKS = (((), (), (0,), (1,), (2, 3)), ((), (), (), (), (0, 1, 2, 3)))
MESH = pl.DeviceIdType.MESH


def split(x):
    high = x.astype(jnp.bfloat16)
    low = (x - high.astype(jnp.float32)).astype(jnp.bfloat16)
    return high, low


def dot(a, b):
    return jnp.dot(a, b, preferred_element_type=jnp.float32)


def dot3(a, b):
    ah, al = split(a)
    bh, bl = split(b)
    return dot(ah, bh) + (dot(ah, bl) + dot(al, bh))


def partner(position, step, size):
    if size & (size - 1):
        return (position + step) % size
    result, bit = 0, 1
    while bit < size:
        digit = (position // bit) % 2
        result += bit * (1 - digit if step & bit else digit)
        bit *= 2
    return result


def kernel(
    sizes, branch_in, walker_ref, trial_ref, chol_ref, field_ref, bias_ref, exch_ref,
    branch_ref, trial_t, source, outgoing, field_in, field_out, traces, squares, bias_rows, exch_rows, raw, trial, field, chol, prop, half, inter, stack, inverse,
    z_send, z_recv, x_send, x_recv, c_send, c_recv, i_send, i_recv,
    tx_send, tx_recv, tc_send, tc_recv, fx_send, fx_recv, fc_send, fc_recv, own_sem,
):
    walks, slabs, cores, slots, local = sizes
    walk, slab, core = lax.axis_index("walk"), lax.axis_index("slab"), lax.axis_index("row")
    rows, electrons = trial_ref.shape
    vectors = chol_ref.shape[0] // electrons
    mine = slab * cores + core

    def slab_peer(step):
        return lax.rem(slab + step, slabs)

    def core_peer(step):
        return lax.rem(core + step, cores)

    def slab_source(step):
        return lax.rem(slab + slabs - step, slabs)

    def core_source(step):
        return lax.rem(core + cores - step, cores)

    loads = [(branch_in, branch_ref), (walker_ref, source), (field_ref, field_in), (trial_ref, trial.at[mine]), (chol_ref, chol)]
    own = [pltpu.make_async_copy(src, dst, own_sem.at[k]) for k, (src, dst) in enumerate(loads)]
    for copy in own:
        copy.start()
    barrier = pltpu.get_barrier_semaphore()
    greeted = 0
    if local < slots:
        for step in range(1, walks):
            pl.semaphore_signal(barrier, inc=1, device_id={"walk": partner(walk, step, walks)}, device_id_type=MESH)
            greeted += 1
    for step in range(1, slabs):
        pl.semaphore_signal(barrier, inc=1, device_id={"slab": slab_peer(step)}, device_id_type=MESH)
        greeted += 1
    for step in range(1, cores):
        pl.semaphore_signal(barrier, inc=1, device_id={"row": core_peer(step)}, device_id_type=MESH)
        greeted += 1

    def sender(w, k):
        return lax.div(branch_ref[w * slots + k], slots)

    def kth(w, origin, values):
        picks, count = [jnp.int32(0)] * local, jnp.int32(0)
        for k in range(slots):
            hit = sender(w, k) == origin
            picks = [jnp.where(hit & (count == place), values(k), pick) for place, pick in enumerate(picks)]
            count = count + jnp.where(hit, 1, 0)
        return picks

    for copy in own[:3]:
        copy.wait()
    slot_of = list(range(slots))
    if local < slots:
        origins = []
        for step in range(walks):
            target = partner(walk, step, walks)
            picks = kth(target, walk, lambda k: lax.rem(branch_ref[target * slots + k], slots))
            for place, pick in enumerate(picks):
                if step == 0:
                    raw[place, mine] = source[pick]
                else:
                    outgoing[step * local + place] = source[pick]
            origin = target if walks & (walks - 1) == 0 else (walk + walks - step) % walks
            origins.append(origin)
            for place, pick in enumerate(kth(walk, origin, lambda k: k)):
                i = step * local + place
                field_out[i : i + 1, :] = field_in[pl.ds(pick, 1), :]
        for j in range(slots):
            origin, rank, step_of = sender(walk, j), jnp.int32(0), jnp.int32(0)
            for k in range(j):
                rank = rank + jnp.where(sender(walk, k) == origin, 1, 0)
            for step in range(walks):
                step_of = jnp.where(origins[step] == origin, step, step_of)
            slot_of[j] = jnp.minimum(step_of * local + rank, slots - 1)
    else:
        for i in range(slots):
            raw[i, mine] = source[i]
        field_out[...] = field_in[...]
    field[mine] = field_out[...]
    for copy in own[3:]:
        copy.wait()
    pl.semaphore_wait(barrier, greeted)

    def remote(src, dst, send, recv, target):
        return pltpu.make_async_remote_copy(
            src_ref=src, dst_ref=dst, send_sem=send, recv_sem=recv, device_id=target, device_id_type=MESH
        )

    def z_copy(i, step):
        return remote(outgoing.at[i], raw.at[i, mine], z_send.at[i], z_recv.at[i], {"walk": partner(walk, step, walks)})

    def x_copy(i, step):
        return remote(raw.at[i, mine], raw.at[i, mine], x_send.at[step, i], x_recv.at[step, i], {"slab": slab_peer(step)})

    def c_copy(i, hop, step):
        q = slab_source(hop) * cores + core
        return remote(raw.at[i, q], raw.at[i, q], c_send.at[hop, step, i], c_recv.at[hop, step, i], {"row": core_peer(step)})

    def small(src, buf, xs, xr, cs, cr):
        def x(step):
            return remote(src, buf.at[mine], xs.at[step], xr.at[step], {"slab": slab_peer(step)})

        def c(hop, step):
            q = slab_source(hop) * cores + core
            block = src if hop == 0 else buf.at[q]
            return remote(block, buf.at[q], cs.at[hop, step], cr.at[hop, step], {"row": core_peer(step)})

        return x, c

    for i in range(local, slots):
        z_copy(i, i // local).start()
    pairs = [
        small(trial_ref, trial, tx_send, tx_recv, tc_send, tc_recv),
        small(field_out, field, fx_send, fx_recv, fc_send, fc_recv),
    ]
    for x, c in pairs:
        for step in range(1, slabs):
            x(step).start()
        for step in range(1, cores):
            c(0, step).start()
    def spread(i):
        for step in range(1, slabs):
            x_copy(i, step).start()
        for step in range(1, cores):
            c_copy(i, 0, step).start()

    def relay(i):
        for hop in range(1, slabs):
            x_copy(i, hop).wait_recv()
            for step in range(1, cores):
                c_copy(i, hop, step).start()

    def compute(i):
        for hop in range(slabs):
            for step in range(1, cores):
                c_copy(i, hop, step).wait_recv()
        for q in range(slabs * cores):
            column = jnp.transpose(field[q])
            lane = lax.broadcasted_iota(jnp.int32, column.shape, 1)
            scale = jnp.sum(jnp.where(lane == i, column, 0.0), axis=1, keepdims=True)
            prop[q * rows : (q + 1) * rows, :] = (raw[i, q].astype(jnp.float32) * scale).astype(jnp.bfloat16)
        @pl.when(lax.rem(i, cores) == core)
        def _():
            total = dot(trial_t[0], prop[0:rows, :])
            for q in range(1, slabs * cores):
                total += dot(trial_t[q], prop[q * rows : (q + 1) * rows, :])
            inter[i // cores] = total

        half[i] = dot(chol[...], prop[...]).astype(jnp.bfloat16)

    for i in range(local):
        spread(i)
    for x, c in pairs:
        for hop in range(1, slabs):
            x(hop).wait_recv()
            for step in range(1, cores):
                c(hop, step).start()
    for x, c in pairs:
        for hop in range(slabs):
            for step in range(1, cores):
                c(hop, step).wait_recv()

    for q in range(slabs * cores):
        trial_t[q] = jnp.transpose(trial[q].astype(jnp.float32)).astype(jnp.bfloat16)
    share = slots // cores
    line = lax.broadcasted_iota(jnp.int32, (electrons, electrons), 0)
    diagonal = line == lax.broadcasted_iota(jnp.int32, (electrons, electrons), 1)

    def i_copy(i, step):
        place = inverse.at[i]
        return remote(place, place, i_send.at[i // cores, step], i_recv.at[i // cores, step], {"row": core_peer(step)})

    def first_guess(n):
        matrix = inter[n]
        sizes_of = jnp.abs(matrix)
        column_max = jnp.max(jnp.sum(sizes_of, axis=0, keepdims=True), axis=1, keepdims=True)
        row_max = jnp.max(jnp.sum(sizes_of, axis=1, keepdims=True), axis=0, keepdims=True)
        start = jnp.transpose(matrix) / (column_max * row_max)
        stack[0:electrons, :] = start
        stack[electrons:, :] = dot3(matrix, start)

    def finish(i):
        @pl.when(lax.rem(i, cores) != core)
        def _():
            i_copy(i, lax.rem(core + cores - lax.rem(i, cores), cores)).wait_recv()

        contracted = dot(half[i], inverse[i])
        for g in range(vectors):
            block = contracted[g * electrons : (g + 1) * electrons, :]
            traces[i, g : g + 1, :] = jnp.sum(jnp.where(diagonal, block, 0.0), axis=0, keepdims=True)
            squares[i, g : g + 1, :] = jnp.sum(block * jnp.transpose(block), axis=0, keepdims=True)

    ready = cores + 1

    @pl.loop(0, slots + ready + cores + 1)
    def _(i):
        @pl.when((i >= local) & (i < slots))
        def _():
            z_copy(i, 0).wait_recv()
            spread(i)

        @pl.when((i > 1) & (i < slots + 2))
        def _():
            compute(i - 2)

        @pl.when((i > 0) & (i <= slots))
        def _():
            relay(i - 1)

        for part in range(cores):

            @pl.when((i >= ready) & (i < slots + ready) & (lax.rem(i + cores - 1, cores) == part))
            def _():
                n = (i - ready) // cores
                if part == 0:
                    first_guess(n)

                first, middle, last = ITERS * part // cores, EARLY, ITERS * (part + 1) // cores

                @pl.loop(first, max(first, min(middle, last)))
                def _(iteration):
                    both = stack[...]
                    low = both.astype(jnp.bfloat16)
                    stack[...] = 2.0 * both - dot(low, low[electrons:, :])

                @pl.loop(min(last, max(middle, first)), last)
                def _(iteration):
                    both = stack[...]
                    stack[...] = 2.0 * both - dot3(both, both[electrons:, :])

                if part == cores - 1:
                    inverse[n * cores + core] = stack[0:electrons, :].astype(jnp.bfloat16)
                    for step in range(1, cores):
                        i_copy(n * cores + core, step).start()

        @pl.when(i > ready + cores)
        def _():
            finish(i - ready - cores - 1)


    column = lax.broadcasted_iota(jnp.int32, bias_ref.shape, 1)
    for terms, rows_of, result in ((traces, bias_rows, bias_ref), (squares, exch_rows, exch_ref)):
        for j in range(slots):
            block = terms[slot_of[j]]
            for g in range(vectors):
                rows_of[g, j : j + 1, :] = block[g : g + 1, :]
        total = jnp.zeros(result.shape, jnp.float32)
        for g in range(vectors):
            total = jnp.where(column == g, jnp.sum(rows_of[g], axis=1, keepdims=True), total)
        result[...] = total

    for i in range(local, slots):
        z_copy(i, i // local).wait_send()

    @pl.loop(0, slots)
    def _(i):
        for step in range(1, slabs):
            x_copy(i, step).wait_send()
        for hop in range(slabs):
            for step in range(1, cores):
                c_copy(i, hop, step).wait_send()

    for x, c in pairs:
        for step in range(1, slabs):
            x(step).wait_send()
        for hop in range(slabs):
            for step in range(1, cores):
                c(hop, step).wait_send()
    for n in range(share):
        for step in range(1, cores):
            i_copy(n * cores + core, step).wait_send()


def xor(a, b, size):
    result, bit = 0, 1
    while bit < size:
        left, right = lax.rem(lax.div(a, bit), 2), lax.rem(lax.div(b, bit), 2)
        result += bit * lax.rem(left + right, 2)
        bit *= 2
    return result


def origin_kernel(
    sizes, branch_in, walker_ref, trial_ref, chol_ref, field_ref, bias_ref, exch_ref, living_ref,
    branch_ref, source, fields, chosen, outgoing, prop, trial, trial_t, chol, stack, green, lanes, sums, arrived,
    own_sem, f_send, f_recv, t_send, t_recv, tx_send, tp_sem, cx_send, cd_send, c_send, c_recv, cp_sem, w_send, w_recv, o_send, o_recv,
):
    walks, slabs, cores, slots, local, items = sizes
    walk, slab, core = lax.axis_index("walk"), lax.axis_index("slab"), lax.axis_index("row")
    rows, electrons = trial_ref.shape
    shards = slabs * cores
    vectors = chol_ref.shape[0] // electrons
    mine = slab * cores + core
    other_slab, other_core = 1 - slab, 1 - core
    across, beside, diagonal_q = other_slab * cores + core, slab * cores + other_core, other_slab * cores + other_core
    below, above = walk > 0, walk < walks - 1
    steps = ((1, 1), (1, 0), (0, 1))

    loads = [(branch_in, branch_ref), (walker_ref, source), (field_ref, fields.at[walk]), (trial_ref, trial.at[mine]), (chol_ref, chol.at[mine])]
    own = [pltpu.make_async_copy(src, dst, own_sem.at[k]) for k, (src, dst) in enumerate(loads)]
    for copy in own:
        copy.start()
    barrier = pltpu.get_barrier_semaphore()

    def greet(target):
        pl.semaphore_signal(barrier, inc=1, device_id=target, device_id_type=MESH)

    def place_of(dx, dc):
        return {"slab": lax.rem(slab + dx, slabs), "row": lax.rem(core + dc, cores)}

    for dx, dc in steps:
        greet(place_of(dx, dc))

    @pl.when(below)
    def _():
        greet({"walk": walk - 1})

    @pl.when(above)
    def _():
        greet({"walk": walk + 1})

    for copy in own:
        copy.wait()
    pl.semaphore_wait(barrier, len(steps) + jnp.where(below, 1, 0) + jnp.where(above, 1, 0))

    def remote(src, dst, send, recv, target):
        return pltpu.make_async_remote_copy(
            src_ref=src, dst_ref=dst, send_sem=send, recv_sem=recv, device_id=target, device_id_type=MESH
        )

    def field_copy(o, way):
        return remote(fields.at[o], fields.at[o], f_send.at[way, o], f_recv.at[o], {"walk": walk + 1 - 2 * way})

    half = lax.rem(walk, 2)

    def trial_view(q, part):
        size = rows // 2
        return trial.at[q, pl.ds(pl.multiple_of(part * size, size), size)]

    def chol_rows(o, p):
        size = chol_ref.shape[0] // (walks * PIECES)
        return pl.ds(pl.multiple_of((o * PIECES + p) * size, size), size)

    def trial_next(part):
        view = trial_view(across, part)
        return remote(view, view, t_send.at[0], t_recv.at[0, part], {"walk": walk + 1 - 2 * half})

    def trial_relay(part):
        view = trial_view(across, part)
        return remote(view, view, t_send.at[1 + part], t_recv.at[1, part], {"row": other_core})

    def trial_beside(part):
        view = trial_view(diagonal_q, part)
        return remote(view, view, t_send.at[1 + part], t_recv.at[1, part], {"row": other_core})

    def chol_copy(o, p, way):
        view = chol.at[across, chol_rows(o, p)]
        if way == 2:
            return remote(view, view, c_send.at[2, o, p], c_recv.at[1, o, p], {"row": other_core})
        return remote(view, view, c_send.at[way, o, p], c_recv.at[0, o, p], {"walk": walk + 1 - 2 * way})

    def chol_beside(o, p):
        view = chol.at[diagonal_q, chol_rows(o, p)]
        return remote(view, view, c_send.at[2, o, p], c_recv.at[1, o, p], {"row": other_core})

    def trial_across():
        view = trial_view(mine, half)
        return remote(view, view, tx_send.at[0], t_recv.at[0, half], {"slab": other_slab})

    def chol_across(p):
        return remote(chol.at[mine, chol_rows(walk, p)], chol.at[mine, chol_rows(walk, p)], cx_send.at[p], c_recv.at[0, walk, p], {"slab": other_slab})

    trial_whole = remote(trial.at[mine], trial.at[mine], tp_sem.at[0], tp_sem.at[1], {"row": other_core})
    chol_whole = remote(chol.at[mine], chol.at[mine], cp_sem.at[0], cp_sem.at[1], {"row": other_core})

    def both_ways(action):
        @pl.when(above)
        def _():
            action(0)

        @pl.when(below)
        def _():
            action(1)

    def hop(k, arrive, forward):
        @pl.when(walk >= k)
        def _():
            arrive(walk - k)
            if k < walks - 1:
                pl.when(above)(lambda: forward(walk - k, 0))

        @pl.when(walk + k < walks)
        def _():
            arrive(walk + k)
            if k < walks - 1:
                pl.when(below)(lambda: forward(walk + k, 1))

    def field_hop(k):
        hop(k, lambda o: field_copy(o, 0).wait_recv(), lambda o, way: field_copy(o, way).start())

    def chol_hop(k, p):
        def arrive(o):
            chol_copy(o, p, 0).wait_recv()
            chol_copy(o, p, 2).start()

        def forward(o, way):
            if k < walks - 2 or p < PIECES - DIRECT:
                chol_copy(o, p, way).start()

        hop(k, arrive, forward)

    def chol_direct(p, action):
        if walks > 2:
            far = walks - 1 - walk
            view = chol.at[mine, chol_rows(far, p)]
            copy = remote(view, view, cd_send.at[p], c_recv.at[0, far, p], {"slab": other_slab})
            pl.when(jnp.logical_not(above & below))(lambda: action(copy))

    def chol_start(p):
        chol_copy(walk, p, 0).wait_recv()
        both_ways(lambda way: chol_copy(walk, p, way).start())
        chol_copy(walk, p, 2).start()

    def sender(w, k):
        return lax.div(branch_ref[w * slots + k], slots)

    def step_of(number):
        order = lax.div(number, shards) * cores + lax.rem(number, cores)
        return walks - 1 - order, lax.div(lax.rem(number, shards), cores)

    def item_target(number):
        return xor(walk, step_of(number)[0], walks)

    def locate(number):
        target, place = item_target(number), step_of(number)[1]
        pick, spot, count = jnp.int32(0), jnp.int32(0), jnp.int32(0)
        for k in range(slots):
            hit = sender(target, k) == walk
            here = hit & (count == place)
            pick = jnp.where(here, lax.rem(branch_ref[target * slots + k], slots), pick)
            spot = jnp.where(here, k, spot)
            count = count + jnp.where(hit, 1, 0)
        return target, pick, spot

    slot_line = lax.broadcasted_iota(jnp.int32, (slots, rows), 0)
    my_rows = pl.ds(pl.multiple_of(mine * rows, rows), rows)

    def w_copy(r, dx, row):
        place = {"slab": lax.rem(slab + dx, slabs), "row": row}
        return remote(outgoing.at[r, dx * cores + row], prop.at[r, my_rows], w_send.at[r, dx * cores + row], w_recv.at[r, mine], place)

    def send_group(r, row):
        found = []
        for dx in range(slabs):
            target, pick, spot = locate(r * shards + lax.rem(slab + dx, slabs) * cores + row)
            found.append(pick)
            chosen[dx : dx + 1, :] = jnp.sum(jnp.where(slot_line == spot, fields[target], 0.0), axis=0, keepdims=True)
        scales = jnp.transpose(chosen[...])
        for dx in reversed(range(slabs)):
            block = (source[found[dx]].astype(jnp.float32) * scales[:, dx : dx + 1]).astype(jnp.bfloat16)
            outgoing[r, dx * cores + row] = block
            if dx:
                w_copy(r, dx, row).start()
            else:
                pl.when(core != row)(w_copy(r, dx, row).start)

                @pl.when(core == row)
                def _():
                    prop[r, my_rows] = outgoing[r, row]

    both_ways(lambda way: field_copy(walk, way).start())
    chol_across(0).start()
    trial_across().start()
    for p in range(1, PIECES):
        chol_across(p).start()
    trial_whole.start()
    chol_whole.start()

    last = walks - 1
    field_hop(1)
    chol_start(0)
    for k in range(2, last):
        field_hop(k)
    trial_next(half).wait_recv()
    trial_next(half).start()
    trial_relay(half).start()
    send_group(0, 1)
    chol_start(1)
    if last > 2:
        chol_hop(1, 0)
    if last > 1:
        field_hop(last)
    send_group(0, 0)
    send_group(1, 0)
    send_group(1, 1)
    for p in range(PIECES - DIRECT, PIECES):
        chol_direct(p, lambda copy: copy.start())
    chol_start(2)
    trial_next(1 - half).wait_recv()
    trial_relay(1 - half).start()
    chol_start(3)
    for k in range(1, last - 1):
        for p in range(1 if k == 1 else 0, PIECES):
            chol_hop(k, p)
    for part in range(2):
        trial_beside(part).wait_recv()
    trial_whole.wait_recv()
    for q in range(shards):
        trial_t[:, q * rows : (q + 1) * rows] = jnp.transpose(trial[q].astype(jnp.float32)).astype(jnp.bfloat16)

    line = lax.broadcasted_iota(jnp.int32, (electrons, electrons), 0)
    on_diagonal = line == lax.broadcasted_iota(jnp.int32, (electrons, electrons), 1)

    def invert(r, hooks):
        for q in (beside, across, diagonal_q):
            part = pl.ds(pl.multiple_of(q * rows, rows), rows)
            remote(prop.at[r, part], prop.at[r, part], w_send.at[r, 0], w_recv.at[r, q], {"row": other_core}).wait_recv()
        hooks[0]()
        matrix = dot(trial_t[...], prop[r])
        sizes_of = jnp.abs(matrix)
        column_max = jnp.max(jnp.sum(sizes_of, axis=0, keepdims=True), axis=1, keepdims=True)
        row_max = jnp.max(jnp.sum(sizes_of, axis=1, keepdims=True), axis=0, keepdims=True)
        start = jnp.transpose(matrix) / (column_max * row_max)
        stack[0:electrons, :] = start
        stack[electrons:, :] = dot3(matrix, start)

        hooks[1]()

        @pl.loop(0, PASSES)
        def _(iteration):
            both = stack[...]
            low = both.astype(jnp.bfloat16)
            stack[...] = 2.0 * both - dot(low, low[electrons:, :])

        hooks[2]()

        for first, end, hook in ((PASSES, LATER, 3), (LATER, ITERS, 4)):

            @pl.loop(first, end)
            def _(iteration):
                both = stack[...]
                stack[...] = 2.0 * both - dot3(both, both[electrons:, :])

            hooks[hook]()

        green[r] = dot(prop[r], stack[0:electrons, :].astype(jnp.bfloat16)).astype(jnp.bfloat16)

    blocks = (mine, beside, across, diagonal_q)

    def contract(r, n):
        for g in range(vectors):
            block = dot(chol[blocks[n], g * electrons : (g + 1) * electrons, :], green[r])
            number = n * vectors + g
            lanes[r, 0, number : number + 1, :] = jnp.sum(jnp.where(on_diagonal, block, 0.0), axis=0, keepdims=True)
            lanes[r, 1, number : number + 1, :] = jnp.sum(block * jnp.transpose(block), axis=0, keepdims=True)

    def o_copy(r, dx, dc):
        number = r * shards + mine
        target = item_target(number)
        device = {"walk": target, **place_of(dx, dc)}
        return target, remote(sums.at[r], arrived.at[number], o_send.at[r, dx * cores + dc], o_recv.at[number], device)

    def publish(r):
        for kind in range(2):
            total = jnp.sum(lanes[r, kind], axis=1, keepdims=True)
            sums[r, kind] = jnp.broadcast_to(total, sums.shape[2:])
        for dx, dc in steps:
            o_copy(r, dx, dc)[1].start()
        target, copy = o_copy(r, 0, 0)
        pl.when(target != walk)(copy.start)

        @pl.when(target == walk)
        def _():
            arrived[r * shards + mine] = sums[r]

    def hooks_of(k, pieces):
        def relay(group):
            def run():
                if k > 0:
                    for p in group:
                        chol_hop(k, p)

            return run

        return [relay(group) for group in pieces]

    invert(0, hooks_of(last - 1 if last > 2 else 0, HOOKS[0]))
    contract(0, 0)
    chol_whole.wait_recv()
    contract(0, 1)
    for r in range(1, items):
        invert(r, hooks_of(last, HOOKS[1]) if r == 1 else hooks_of(0, HOOKS[1]))
    contract(0, 2)

    @pl.loop(0, walks)
    def _(o):
        @pl.loop(0, PIECES)
        def _(p):
            chol_beside(o, p).wait_recv()

    contract(0, 3)
    publish(0)
    for r in range(1, items):
        for n in range(shards):
            contract(r, n)
        publish(r)

    def number_of(j):
        origin, rank = sender(walk, j), jnp.int32(0)
        for k in range(j):
            rank = rank + jnp.where(sender(walk, k) == origin, 1, 0)
        step = jnp.int32(0)
        for s in range(walks):
            step = jnp.where(xor(walk, s, walks) == origin, s, step)
        order = walks - 1 - step
        number = lax.div(order, cores) * shards + lax.min(rank, local - 1) * cores + lax.rem(order, cores)
        return jnp.clip(number, 0, slots - 1)

    numbers = [number_of(j) for j in range(slots)]

    for number in range(slots):
        target = item_target(number)
        from_me = (target == walk) & (mine == number % shards)

        @pl.when(jnp.logical_not(from_me))
        def _():
            remote(sums.at[0], arrived.at[number], o_send.at[0, 0], o_recv.at[number], {"row": other_core}).wait_recv()

    column = lax.broadcasted_iota(jnp.int32, bias_ref.shape, 1)
    for kind, result in enumerate((bias_ref, exch_ref)):
        total = jnp.zeros(result.shape, jnp.float32)
        for j in range(slots):
            q = lax.rem(numbers[j], shards)
            dx, dc = lax.rem(lax.div(q, cores) + slab, slabs), lax.rem(lax.rem(q, cores) + core, cores)
            first = (dx * cores + dc) * vectors
            total = jnp.where(column == j, arrived[numbers[j], kind, pl.ds(first, vectors), 0:slots], total)
        result[...] = total
    living_ref[...] = jnp.where(column < branch_ref[walks * slots], 1.0, 0.0)

    trial_across().wait_send()
    trial_next(half).wait_send()
    for part in range(2):
        trial_relay(part).wait_send()
    trial_whole.wait_send()
    for p in range(PIECES - DIRECT, PIECES):
        chol_direct(p, lambda copy: copy.wait_send())
    chol_whole.wait_send()
    for p in range(PIECES):
        chol_across(p).wait_send()

    @pl.loop(0, walks)
    def _(o):
        def sent(way):
            field_copy(o, way).wait_send()

        pl.when(above & (o <= walk))(lambda: sent(0))
        pl.when(below & (o >= walk))(lambda: sent(1))

        @pl.loop(0, PIECES)
        def _(p):
            chol_copy(o, p, 2).wait_send()
            chained = (p < PIECES - DIRECT) | (walks < 3)
            upward, downward = (o > 0) | (walk < walks - 2), (o < walks - 1) | (walk > 1)
            pl.when(above & (o <= walk) & (chained | upward))(lambda: chol_copy(o, p, 0).wait_send())
            pl.when(below & (o >= walk) & (chained | downward))(lambda: chol_copy(o, p, 1).wait_send())

    for r in range(items):
        for dx, dc in steps:
            o_copy(r, dx, dc)[1].wait_send()
        target, copy = o_copy(r, 0, 0)
        pl.when(target != walk)(copy.wait_send)
        for row in range(cores):
            for dx in range(1, slabs):
                w_copy(r, dx, row).wait_send()
            pl.when(core != row)(w_copy(r, 0, row).wait_send)


def gathered(walkers, trial_orbitals, cholesky, branches, field):
    walks, slabs, cores = lax.axis_size("walk"), lax.axis_size("slab"), lax.axis_size("row")
    walk = lax.axis_index("walk")
    per_device, rows, electrons = walkers.shape
    vectors = cholesky.shape[0]
    capacity = (per_device + walks - 1) // walks
    local = capacity if walks * capacity == per_device else per_device
    if local == per_device:
        sender = branches.reshape(walks, per_device) // per_device
        local_index = branches.reshape(walks, per_device) % per_device
        places = jnp.arange(per_device, dtype=jnp.int32)
        same_sender = sender[:, :, None] == sender[:, None, :]
        rank = jnp.sum(same_sender & (places[None, :] < places[:, None])[None], axis=2)
        ranks = jnp.arange(capacity, dtype=jnp.int32)[None, :, None]
        wanted = (sender[:, None, :] == walk) & (rank[:, None, :] == ranks)
        chosen = jnp.sum(jnp.where(wanted, local_index[:, None, :], 0), axis=2)
        outgoing = jnp.take(walkers, chosen.reshape(-1), axis=0, mode="clip")
        outgoing = outgoing.reshape(walks, capacity, rows, electrons)
        arrived = lax.all_to_all(outgoing, "walk", split_axis=0, concat_axis=0, tiled=True)
        arrived = arrived.reshape(walks * capacity, rows, electrons)
        my_sender = lax.dynamic_index_in_dim(sender, walk, 0, keepdims=False)
        my_rank = lax.dynamic_index_in_dim(rank, walk, 0, keepdims=False)
        walkers = jnp.take(arrived, my_sender * capacity + my_rank, axis=0, mode="clip")
    shards = slabs * cores
    share = per_device // cores
    dma = pltpu.SemaphoreType.DMA
    vmem = pl.BlockSpec(memory_space=pltpu.VMEM)
    bias, exchange = pl.pallas_call(
        functools.partial(kernel, (walks, slabs, cores, per_device, local)),
        out_shape=[jax.ShapeDtypeStruct((per_device, vectors), jnp.float32)] * 2,
        in_specs=[pl.BlockSpec(memory_space=pl.ANY)] * 5,
        out_specs=[vmem] * 2,
        scratch_shapes=[
            pltpu.SMEM(branches.shape, jnp.int32),
            pltpu.VMEM((shards, electrons, rows), jnp.bfloat16),
            pltpu.VMEM((per_device, rows, electrons), jnp.bfloat16),
            pltpu.VMEM((per_device, rows, electrons), jnp.bfloat16),
            pltpu.VMEM((per_device, rows), jnp.float32),
            pltpu.VMEM((per_device, rows), jnp.float32),
            pltpu.VMEM((per_device, vectors, electrons), jnp.float32),
            pltpu.VMEM((per_device, vectors, electrons), jnp.float32),
            pltpu.VMEM((vectors, per_device, electrons), jnp.float32),
            pltpu.VMEM((vectors, per_device, electrons), jnp.float32),
            pltpu.VMEM((per_device, shards, rows, electrons), jnp.bfloat16),
            pltpu.VMEM((shards, rows, electrons), jnp.bfloat16),
            pltpu.VMEM((shards, per_device, rows), jnp.float32),
            pltpu.VMEM((vectors * electrons, shards * rows), jnp.bfloat16),
            pltpu.VMEM((shards * rows, electrons), jnp.bfloat16),
            pltpu.VMEM((per_device, vectors * electrons, electrons), jnp.bfloat16),
            pltpu.VMEM((share, electrons, electrons), jnp.float32),
            pltpu.VMEM((2 * electrons, electrons), jnp.float32),
            pltpu.VMEM((per_device, electrons, electrons), jnp.bfloat16),
            dma((per_device,)), dma((per_device,)),
            dma((slabs, per_device)), dma((slabs, per_device)),
            dma((slabs, cores, per_device)), dma((slabs, cores, per_device)),
            dma((share, cores)), dma((share, cores)),
            dma((slabs,)), dma((slabs,)), dma((slabs, cores)), dma((slabs, cores)),
            dma((slabs,)), dma((slabs,)), dma((slabs, cores)), dma((slabs, cores)),
            dma((5,)),
        ],
        compiler_params=pltpu.CompilerParams(
            collective_id=0, has_side_effects=True, vmem_limit_bytes=63 * 1024 * 1024
        ),
    )(branches, walkers, trial_orbitals, cholesky.reshape(vectors * electrons, shards * rows), field)
    return bias, exchange


def at_origin(walkers, trial_orbitals, cholesky, branches, counts, field):
    walks, slabs, cores = lax.axis_size("walk"), lax.axis_size("slab"), lax.axis_size("row")
    slots, rows, electrons = walkers.shape
    vectors = cholesky.shape[0]
    shards, local = slabs * cores, slots // walks
    items, lines, columns = slots // shards, vectors * electrons, shards * rows
    dma = pltpu.SemaphoreType.DMA
    vmem = pl.BlockSpec(memory_space=pltpu.VMEM)
    numbers = jnp.concatenate([branches, counts])
    bias, exchange, living = pl.pallas_call(
        functools.partial(origin_kernel, (walks, slabs, cores, slots, local, items)),
        out_shape=[jax.ShapeDtypeStruct((vectors, slots), jnp.float32)] * 3,
        in_specs=[pl.BlockSpec(memory_space=pltpu.HBM)] * 5,
        out_specs=[vmem] * 3,
        scratch_shapes=[
            pltpu.SMEM(numbers.shape, jnp.int32),
            pltpu.VMEM((slots, rows, electrons), jnp.bfloat16),
            pltpu.VMEM((walks, slots, rows), jnp.float32),
            pltpu.VMEM((slots, rows), jnp.float32),
            pltpu.VMEM((items, shards, rows, electrons), jnp.bfloat16),
            pltpu.VMEM((items, columns, electrons), jnp.bfloat16),
            pltpu.VMEM((shards, rows, electrons), jnp.bfloat16),
            pltpu.VMEM((electrons, columns), jnp.bfloat16),
            pltpu.VMEM((shards, lines, columns), jnp.bfloat16),
            pltpu.VMEM((2 * electrons, electrons), jnp.float32),
            pltpu.VMEM((items, columns, electrons), jnp.bfloat16),
            pltpu.VMEM((items, 2, shards * vectors, electrons), jnp.float32),
            pltpu.VMEM((items, 2, shards * vectors, 128), jnp.float32),
            pltpu.VMEM((slots, 2, shards * vectors, 128), jnp.float32),
            dma((5,)),
            dma((2, walks)), dma((walks,)),
            dma((3,)), dma((2, 2)), dma((2,)), dma((2,)),
            dma((PIECES,)), dma((PIECES,)), dma((3, walks, PIECES)), dma((2, walks, PIECES)), dma((2,)),
            dma((items, shards)), dma((items, shards)),
            dma((items, shards)), dma((slots,)),
        ],
        compiler_params=pltpu.CompilerParams(
            collective_id=0, has_side_effects=True, vmem_limit_bytes=55216 * 1024
        ),
    )(numbers, walkers, trial_orbitals, cholesky.reshape(lines, columns), field)
    return (bias * living).T, (-0.5 * exchange * living).T


def on_device(walkers, trial_orbitals, cholesky, branches, counts, field):
    walks, slabs, cores = lax.axis_size("walk"), lax.axis_size("slab"), lax.axis_size("row")
    slots, rows, electrons = walkers.shape
    lines = cholesky.shape[0] * electrons
    even = walks & (walks - 1) == 0 and slots % walks == 0 and slots % (slabs * cores) == 0
    whole = lines % (walks * PIECES * 16) == 0 and rows % 32 == 0 and walks > 2
    if slabs == cores == 2 and slots == 2 * walks and PIECES == 4 and even and whole:
        return at_origin(walkers, trial_orbitals, cholesky, branches, counts, field)
    bias, exchange = gathered(walkers, trial_orbitals, cholesky, branches, field)
    living = (jnp.arange(slots, dtype=jnp.int32) < counts[0]).astype(jnp.float32)[:, None]
    return bias * living, -0.5 * exchange * living


def solution(mesh):
    return jax.shard_map(
        on_device,
        mesh=mesh,
        in_specs=(
            P(("parts", "walk"), ("slab", "row"), None),
            P(("parts", "slab", "row"), None),
            P(("parts", "slab", "row"), None, None),
            P("parts"),
            P(("parts", "walk")),
            P(("parts", "walk"), ("slab", "row")),
        ),
        out_specs=(P(("parts", "walk"), ("slab", "row")), P(("parts", "walk"), ("slab", "row"))),
        check_vma=False,
    )
```
